256 devices in a mesh: gx: 4 (over y_hi, core), gy: 8 (over y_lo, x), gz: 8 (over z).
Axes of the slice: x: 4, y: 4 (y_hi: 2, y_lo: 2; y = y_hi * 2 + y_lo), z: 8, core: 2. Of those that a mesh axis runs over, the one named last changes fastest.
Arguments:
- positions: float32 [3, 4, 8, 8, 512], P(None, 'gx', 'gy', 'gz'), may hold values from 0 to 16, as said below
- charges: float32 [4, 8, 8, 512], P('gx', 'gy', 'gz'), may hold values from -4 to 4
- atom_types: int32 [4, 8, 8, 512], P('gx', 'gy', 'gz'), may hold values from 0 to 7
- type_table: float32 [3, 8], replicated, may hold values from 0.5 to 2
- live_count: int32 [4, 8, 8], P('gx', 'gy', 'gz'), may hold values from 358 to 512, as said below
- exp_map: float32 [64, 128, 128], P('gx', 'gy', 'gz'), may hold values from -6 to 6
Outputs:
- displacement: float32 [3, 4, 8, 8, 512], P(None, 'gx', 'gy', 'gz')
- last_force: float32 [3, 4, 8, 8, 512], P(None, 'gx', 'gy', 'gz')
- evolved: float32 [64, 128, 128], P('gx', 'gy', 'gz')
The draws below stay inside these ranges and needn't reach their ends.
Inputs may be any that keep to these rules, and one draw needn't show every extreme that they name: `positions`: each coordinate lies within its cell's brick: 0 to 16, 16, 16 along x, y, z. The live atoms of a cell are its first live_count slots; some cell has all 512 slots live.
All inputs are finite; a program needn't handle non-finite values.
Results may differ from the reference program's by a relative error of at most 0.0003.
Values sent between devices are 32-bit elements; how exact they have to be, the bound alone decides.
No kernel may reach another device: no remote copies, remote signals or barrier semaphores. Data moves between devices by JAX's collectives and lax.ppermute only.
A program may use at most 128 MiB of HBM per device.

```python
import math
import jax
import jax.numpy as jnp
from jax import lax

BRICK_X = 16
BRICK_Y = 16
BRICK_Z = 16
ATOMS = 512
NTYPES = 8
SPLAT_MARGIN = 3
BLUR_REACH = 2
STEPS = 2
CELLS_X = 4
CELLS_Y = 8
CELLS_Z = 8
MAP_X = 64
MAP_Y = 128
MAP_Z = 128


def draw_positions(key, part):
    unit = jax.random.uniform(key, (3, CELLS_X, CELLS_Y, CELLS_Z, ATOMS), jnp.float32)
    extent = jnp.array([BRICK_X, BRICK_Y, BRICK_Z], jnp.float32).reshape(3, 1, 1, 1, 1)
    return (unit * extent).astype(jnp.float32)


def draw_live_count(key, part):
    key_one, key_two = jax.random.split(jax.random.fold_in(key, 17), 2)
    shape = (CELLS_X, CELLS_Y, CELLS_Z)
    counts = jax.random.randint(key_one, shape, 7 * ATOMS // 10, ATOMS + 1).reshape(-1)
    chosen = jax.random.randint(key_two, (), 0, CELLS_X * CELLS_Y * CELLS_Z)
    marker = jnp.arange(counts.shape[0], dtype=jnp.int32) == chosen
    return jnp.where(marker, ATOMS, counts).reshape(shape).astype(jnp.int32)


def place_ends(values, rng, smallest, top_value):
    shape = values.shape
    spot = [jax.random.randint(jax.random.fold_in(rng, axis), (), 0, shape[axis]) for axis in range(len(shape))]
    values = values.at[tuple(spot)].set(smallest)
    longest = shape.index(max(shape))
    spot[longest] = (spot[longest] + 1) % shape[longest]
    return values.at[tuple(spot)].set(top_value)


def steps_of(stream_key, dims, pieces, smallest, largest):
    def one(dim, blocks):
        draws = jax.random.uniform(jax.random.fold_in(jax.random.fold_in(stream_key, 6), dim), (blocks,), jnp.float32, smallest / len(pieces), largest / len(pieces))
        return jnp.repeat(jnp.exp(draws), dims[dim] // blocks).reshape((-1,) + (1,) * (len(dims) - dim - 1))

    level = one(*pieces[0])
    for cut in pieces[1:]:
        level = level * one(*cut)
    return level


def centred(rng, shape, deviation, most, pieces=(), kind=jnp.bfloat16):
    gain = steps_of(rng, shape, pieces, -0.22, 0.18) if pieces else 1.0
    values = jax.random.normal(rng, shape, jnp.float32) * deviation * gain
    return jnp.minimum(jnp.maximum(values, -most), most).astype(kind)


def setup_inputs(seed: int = 0) -> dict:
    seeds = jax.random.split(jax.random.key(seed), 7)
    return {
        "positions": draw_positions(jax.random.fold_in(seeds[6], 71), 0),
        "charges": centred(seeds[1], (CELLS_X, CELLS_Y, CELLS_Z, ATOMS), 1.0, 4.0, ((0, 4), (1, 8), (2, 8)), jnp.float32),
        "atom_types": place_ends(jax.random.randint(seeds[2], (CELLS_X, CELLS_Y, CELLS_Z, ATOMS), 0, NTYPES), jax.random.fold_in(seeds[2], 1), 0, NTYPES - 1).astype(jnp.int32),
        "type_table": jnp.clip(jnp.exp(jax.random.uniform(seeds[3], (3, NTYPES), jnp.float32, math.log(0.5), math.log(2.0))), 0.5, 2.0),
        "live_count": draw_live_count(jax.random.fold_in(seeds[6], 71), 0),
        "exp_map": centred(seeds[5], (MAP_X, MAP_Y, MAP_Z), 1.0, 6.0, ((0, 4), (1, 8), (2, 8)), jnp.float32),
    }


CUTOFF = 10.0
EPSILON = 1e-06
STEP_SIZE = 1.0
FIT_GAIN = 0.2

def pack_atoms(positions, charges, atom_types, type_table, live_count):
    type_total = type_table.shape[1]
    onehot = (atom_types[..., None] == jnp.arange(type_total, dtype=jnp.int32)).astype(jnp.float32)
    props = lax.optimization_barrier(jnp.sum(onehot[None] * type_table[:, None, None, None, None, :], axis=-1))
    slots = lax.broadcasted_iota(jnp.int32, charges.shape, 3)
    living = (slots < live_count[..., None]).astype(jnp.float32)
    return jnp.concatenate([positions, charges[None], props, living[None]], axis=0)

def block_list(nearby, brick_dims):
    channels = nearby.shape[0]
    slot_count = nearby.shape[-1]
    blocks = jnp.transpose(nearby.reshape(channels, 27, slot_count), (1, 0, 2))
    number = jnp.arange(27, dtype=jnp.int32)
    sides = jnp.stack([number // 9 - 1, number // 3 % 3 - 1, number % 3 - 1], axis=1).astype(jnp.float32)
    offsets = sides * jnp.array(brick_dims, jnp.float32)[None, :]
    centre = (number == 13).astype(jnp.float32)
    return (blocks, offsets, centre)

def geometry(own_atoms, block, offset):
    separation = own_atoms[0:3, :, None] - (block[0:3, None, :] + offset[:, None, None])
    squared = lax.optimization_barrier(jnp.sum(separation * separation, axis=0))
    smooth_cut = jnp.maximum(1.0 - squared / (CUTOFF * CUTOFF), 0.0)
    return (separation, squared, smooth_cut)

def born_radius(own_atoms, nearby, brick_dims):
    blocks, offsets, centre = block_list(nearby, brick_dims)
    slot_count = own_atoms.shape[1]
    identity_mask = jnp.eye(slot_count, dtype=jnp.float32)

    def visit(summed, element):
        block, offset, middle = element
        separation, squared, smooth_cut = geometry(own_atoms, block, offset)
        keep_mask = 1.0 - middle * identity_mask
        weight_term = jnp.exp(-squared / 8.0) * smooth_cut * smooth_cut * keep_mask * (block[5] * block[7])[None, :]
        return (summed + lax.optimization_barrier(jnp.sum(weight_term, axis=1)), None)
    summed, unused = lax.scan(visit, jnp.zeros((slot_count,), jnp.float32), (blocks, offsets, centre))
    return own_atoms[4] + summed

def gb_forces(own_atoms, own_radius, nearby, near_radius, brick_dims):
    blocks, offsets, centre = block_list(nearby, brick_dims)
    slot_count = own_atoms.shape[1]
    identity_mask = jnp.eye(slot_count, dtype=jnp.float32)
    radii = near_radius.reshape(27, slot_count)

    def visit(summed, element):
        block, radius_block, offset, middle = element
        separation, squared, smooth_cut = geometry(own_atoms, block, offset)
        product = own_radius[:, None] * radius_block[None, :]
        fading = jnp.exp(-squared / (4.0 * product))
        inverse = lax.rsqrt(squared + product * fading)
        charge_pair = (own_atoms[3] * own_atoms[7])[:, None] * (block[3] * block[7])[None, :] * (1.0 - middle * identity_mask)
        slope = -0.5 * charge_pair * (-2.0 * smooth_cut / (CUTOFF * CUTOFF) * inverse - 0.5 * smooth_cut * smooth_cut * inverse * inverse * inverse * (1.0 - 0.25 * fading))
        return (summed - 2.0 * lax.optimization_barrier(jnp.sum(slope[None] * separation, axis=2)), None)
    summed, unused = lax.scan(visit, jnp.zeros((3, slot_count), jnp.float32), (blocks, radii, offsets, centre))
    return summed

def profile(coord, start, stop, shift):
    points = jnp.arange(start, stop, dtype=jnp.float32)
    gap = points[None, :] - (coord[:, None] + shift)
    return (jnp.exp(-0.5 * gap * gap), gap)

def splat_extended(own_atoms, brick_dims):
    margin = SPLAT_MARGIN
    profile_x = profile(own_atoms[0], -margin, brick_dims[0] + margin, 0.0)[0]
    profile_y = profile(own_atoms[1], -margin, brick_dims[1] + margin, 0.0)[0]
    profile_z = profile(own_atoms[2], -margin, brick_dims[2] + margin, 0.0)[0]
    slot_count = own_atoms.shape[1]
    mass = own_atoms[6] * own_atoms[7]
    outer = (profile_y[:, :, None] * profile_z[:, None, :]).reshape(slot_count, -1)
    placed = jnp.dot((profile_x * mass[:, None]).T, outer, precision=lax.Precision.HIGHEST)
    return placed.reshape(profile_x.shape[1], profile_y.shape[1], profile_z.shape[1])

def kernel_weights(reach):
    values = [math.exp(-0.5 * (index - reach) ** 2) for index in range(2 * reach + 1)]
    whole = sum(values)
    return [value / whole for value in values]

def blur_axis(field, axis):
    weights = kernel_weights(BLUR_REACH)
    length = field.shape[axis]
    widths = [(0, 0), (0, 0), (0, 0)]
    widths[axis] = (BLUR_REACH, BLUR_REACH)
    padded = jnp.pad(field, widths)
    result = jnp.zeros_like(field)
    for index in range(len(weights)):
        result = result + weights[index] * lax.slice_in_dim(padded, index, index + length, axis=axis)
    return result

def blur_map(field):
    return blur_axis(blur_axis(blur_axis(field, 0), 1), 2)

def correlation_slope(evolved, exp_map, sums):
    squares, cross_sum, target = sums
    norm_value = jnp.sqrt((squares + EPSILON) * (target + EPSILON))
    score = cross_sum / norm_value
    return exp_map / norm_value - score * evolved / (squares + EPSILON)

def fit_force(grad_ext, own_atoms, brick_dims, scale):
    margin = SPLAT_MARGIN
    slot_count = own_atoms.shape[1]
    profile_x, gap_x = profile(own_atoms[0], -margin, brick_dims[0] + margin, 0.0)
    profile_y, gap_y = profile(own_atoms[1], -margin, brick_dims[1] + margin, 0.0)
    profile_z, gap_z = profile(own_atoms[2], -margin, brick_dims[2] + margin, 0.0)
    stacked = jnp.concatenate([profile_z, gap_z * profile_z], axis=0)
    inner = jnp.dot(grad_ext.reshape(-1, grad_ext.shape[2]), stacked.T, precision=lax.Precision.HIGHEST)
    inner = inner.reshape(grad_ext.shape[0], grad_ext.shape[1], 2 * slot_count)
    plain_z = inner[:, :, :slot_count]
    slope_z = inner[:, :, slot_count:]
    plain_y = jnp.einsum('ija,aj->ia', plain_z, profile_y, precision=lax.Precision.HIGHEST)
    turned_y = jnp.einsum('ija,aj->ia', plain_z, gap_y * profile_y, precision=lax.Precision.HIGHEST)
    turned_z = jnp.einsum('ija,aj->ia', slope_z, profile_y, precision=lax.Precision.HIGHEST)
    force = jnp.stack([lax.optimization_barrier(jnp.sum(gap_x * profile_x * plain_y.T, axis=1)), lax.optimization_barrier(jnp.sum(profile_x * turned_y.T, axis=1)), lax.optimization_barrier(jnp.sum(profile_x * turned_z.T, axis=1))])
    return scale * (own_atoms[6] * own_atoms[7])[None, :] * force

def per_cell(function, total):
    group = 16 if total % 16 == 0 else 1
    indices = jnp.arange(total, dtype=jnp.int32).reshape(-1, group)
    results = lax.map(jax.vmap(function), indices)
    return results.reshape((total,) + results.shape[2:])

def reference(positions, charges, atom_types, type_table, live_count, exp_map):
    brick_dims = (BRICK_X, BRICK_Y, BRICK_Z)
    packed = pack_atoms(positions, charges, atom_types, type_table, live_count)
    cell_total = CELLS_X * CELLS_Y * CELLS_Z
    cell_index = jnp.arange(cell_total, dtype=jnp.int32)
    scale = FIT_GAIN * float(MAP_X * MAP_Y * MAP_Z)
    anchor = jnp.zeros((), jnp.int32)
    current = positions
    force = jnp.zeros_like(positions)
    evolved = jnp.zeros_like(exp_map)

    def locate(index):
        cell_x = (index // (CELLS_Y * CELLS_Z)).astype(jnp.int32)
        cell_y = (index // CELLS_Z % CELLS_Y).astype(jnp.int32)
        cell_z = (index % CELLS_Z).astype(jnp.int32)
        return (cell_x, cell_y, cell_z)
    for step_index in range(STEPS):
        packed = jnp.concatenate([current, packed[3:]], axis=0)
        framed = jnp.pad(packed, ((0, 0), (1, 1), (1, 1), (1, 1), (0, 0)))

        def radius_cell(index):
            cell_x, cell_y, cell_z = locate(index)
            nearby = lax.dynamic_slice(framed, (anchor, cell_x, cell_y, cell_z, anchor), (8, 3, 3, 3, ATOMS))
            return born_radius(nearby[:, 1, 1, 1, :], nearby, brick_dims)
        radius = per_cell(radius_cell, cell_total).reshape(CELLS_X, CELLS_Y, CELLS_Z, ATOMS)
        radius_framed = jnp.pad(radius, ((1, 1), (1, 1), (1, 1), (0, 0)))

        def force_cell(index):
            cell_x, cell_y, cell_z = locate(index)
            nearby = lax.dynamic_slice(framed, (anchor, cell_x, cell_y, cell_z, anchor), (8, 3, 3, 3, ATOMS))
            near_radius = lax.dynamic_slice(radius_framed, (cell_x, cell_y, cell_z, anchor), (3, 3, 3, ATOMS))
            return gb_forces(nearby[:, 1, 1, 1, :], near_radius[1, 1, 1], nearby, near_radius, brick_dims)
        gb_part = per_cell(force_cell, cell_total)
        gb_part = jnp.transpose(gb_part, (1, 0, 2)).reshape(3, CELLS_X, CELLS_Y, CELLS_Z, ATOMS)

        def splat_cell(canvas, index):
            cell_x, cell_y, cell_z = locate(index)
            own_atoms = lax.dynamic_slice(packed, (anchor, cell_x, cell_y, cell_z, anchor), (8, 1, 1, 1, ATOMS))[:, 0, 0, 0, :]
            extended = splat_extended(own_atoms, brick_dims)
            start = (cell_x * BRICK_X, cell_y * BRICK_Y, cell_z * BRICK_Z)
            present = lax.dynamic_slice(canvas, start, extended.shape)
            return (lax.dynamic_update_slice(canvas, present + extended, start), None)
        canvas = jnp.zeros((MAP_X + 2 * SPLAT_MARGIN, MAP_Y + 2 * SPLAT_MARGIN, MAP_Z + 2 * SPLAT_MARGIN), jnp.float32)
        canvas, unused = lax.scan(splat_cell, canvas, cell_index)
        density = canvas[SPLAT_MARGIN:SPLAT_MARGIN + MAP_X, SPLAT_MARGIN:SPLAT_MARGIN + MAP_Y, SPLAT_MARGIN:SPLAT_MARGIN + MAP_Z]
        evolved = blur_map(density)
        sums = (jnp.sum(evolved * evolved), jnp.sum(evolved * exp_map), jnp.sum(exp_map * exp_map))
        sensitivity = correlation_slope(evolved, exp_map, sums)
        map_grad = blur_map(sensitivity)
        grad_framed = jnp.pad(map_grad, SPLAT_MARGIN)

        def fit_cell(index):
            cell_x, cell_y, cell_z = locate(index)
            own_atoms = lax.dynamic_slice(packed, (anchor, cell_x, cell_y, cell_z, anchor), (8, 1, 1, 1, ATOMS))[:, 0, 0, 0, :]
            grad_ext = lax.dynamic_slice(grad_framed, (cell_x * BRICK_X, cell_y * BRICK_Y, cell_z * BRICK_Z), (BRICK_X + 2 * SPLAT_MARGIN, BRICK_Y + 2 * SPLAT_MARGIN, BRICK_Z + 2 * SPLAT_MARGIN))
            return fit_force(grad_ext, own_atoms, brick_dims, scale)
        fit_part = per_cell(fit_cell, cell_total)
        fit_part = jnp.transpose(fit_part, (1, 0, 2)).reshape(3, CELLS_X, CELLS_Y, CELLS_Z, ATOMS)
        force = gb_part + fit_part
        current = current + STEP_SIZE * (packed[7][None] * force)
    return (current - positions, force, evolved)
```

```python
import functools
import math

import jax
import jax.numpy as jnp
from jax import lax
from jax.experimental import pallas as pl
from jax.experimental.pallas import tpu as pltpu
from jax.sharding import PartitionSpec as P

SPLAT_MARGIN = 3
BLUR_REACH = 2
STEPS = 2
CUTOFF = 10.0
EPSILON = 1e-06
STEP_SIZE = 1.0
FIT_GAIN = 0.2

AXES = ("gx", "gy", "gz")
SLOTS = 512
LANES = 128
TILES = SLOTS // LANES
ROWS = 64
BRICK = 16
PLANES = 26
PAD = 8
WIDE = 32
INTERPRET = False


def call(kernel, out_shape, cost, scratch=(), smem=0, n_in=0, vmem=48):
    specs = [pl.BlockSpec(memory_space=pltpu.SMEM)] * smem
    specs += [pl.BlockSpec(memory_space=pltpu.VMEM)] * (n_in - smem)
    many = isinstance(out_shape, (tuple, list))
    out_spec = pl.BlockSpec(memory_space=pltpu.VMEM)
    return pl.pallas_call(
        kernel,
        out_shape=out_shape,
        in_specs=specs,
        out_specs=[out_spec] * len(out_shape) if many else out_spec,
        scratch_shapes=list(scratch),
        cost_estimate=pl.CostEstimate(flops=cost, bytes_accessed=1 << 18, transcendentals=0),
        compiler_params=pltpu.CompilerParams(vmem_limit_bytes=vmem << 20),
        interpret=INTERPRET,
    )


def spread(row):
    return jnp.transpose(jnp.broadcast_to(row, (LANES, LANES)))


def gather_rows(acc):
    return jnp.sum(jnp.transpose(acc), axis=0, keepdims=True)


def cell_sides(number, fixed_y, fixed_z):
    side_x = lax.rem(number, 3) - 1
    side_y = number // 3 - 1 if fixed_y is None else fixed_y
    return side_x, side_y, fixed_z


def born_kernel(groups, *refs):
    own = refs[0]
    cells = refs[1 : 1 + 2 * len(groups)]
    out, col, acc = refs[1 + 2 * len(groups) :]
    for channel in range(3):
        for tile in range(TILES):
            row = own[4 * channel + tile : 4 * channel + tile + 1, :] * (1.0 / CUTOFF)
            col[channel, tile * LANES : (tile + 1) * LANES, :] = spread(row)
    acc[...] = jnp.zeros_like(acc)
    for index, (count, fixed_y, fixed_z) in enumerate(groups):
        pos, aux = cells[2 * index], cells[2 * index + 1]

        def visit(number, carry, pos=pos, aux=aux, fixed_y=fixed_y, fixed_z=fixed_z):
            sides = cell_sides(number, fixed_y, fixed_z)
            shift = [side * float(BRICK) if isinstance(side, int) else side.astype(jnp.float32) * float(BRICK) for side in sides]
            rows = []
            for tile in range(TILES):
                coords = [
                    (pos[number, 4 * d + tile : 4 * d + tile + 1, :] + shift[d]) * (1.0 / CUTOFF)
                    for d in range(3)
                ]
                rows.append(coords + [aux[number, 16 + tile : 17 + tile, :]])

            def block(ib, inner):
                at = pl.ds(pl.multiple_of(ib * ROWS, ROWS), ROWS)
                xi, yi, zi = col[0, at, :], col[1, at, :], col[2, at, :]
                total = acc[at, :]
                for xj, yj, zj, wj in rows:
                    dx, dy, dz = xi - xj, yi - yj, zi - zj
                    u = dx * dx + dy * dy + dz * dz
                    s = jnp.maximum(1.0 - u, 0.0)
                    e = jnp.exp(u * (-CUTOFF * CUTOFF / 8.0))
                    total = total + e * s * (s * wj)
                acc[at, :] = total
                return inner

            return lax.fori_loop(0, SLOTS // ROWS, block, carry)

        lax.fori_loop(0, count, visit, 0)
    for tile in range(TILES):
        out[tile : tile + 1, :] = gather_rows(acc[tile * LANES : (tile + 1) * LANES, :])


def gb_kernel(groups, *refs):
    own, own_radius = refs[:2]
    cells = refs[2 : 2 + 3 * len(groups)]
    out, col, acc = refs[2 + 3 * len(groups) :]
    for tile in range(TILES):
        at = slice(tile * LANES, (tile + 1) * LANES)
        for channel in range(3):
            row = own[4 * channel + tile : 4 * channel + tile + 1, :] * (1.0 / CUTOFF)
            col[channel, at, :] = spread(row)
        radius = spread(own_radius[tile : tile + 1, :] * (1.0 / CUTOFF))
        col[3, at, :] = radius
        col[4, at, :] = -0.5 / radius
    acc[...] = jnp.zeros_like(acc)
    for index, (count, fixed_y, fixed_z) in enumerate(groups):
        pos, aux, rad = cells[3 * index : 3 * index + 3]

        def visit(number, carry, pos=pos, aux=aux, rad=rad, fixed_y=fixed_y, fixed_z=fixed_z):
            sides = cell_sides(number, fixed_y, fixed_z)
            shift = [side * float(BRICK) if isinstance(side, int) else side.astype(jnp.float32) * float(BRICK) for side in sides]
            rows = []
            for tile in range(TILES):
                coords = [
                    (pos[number, 4 * d + tile : 4 * d + tile + 1, :] + shift[d]) * (1.0 / CUTOFF)
                    for d in range(3)
                ]
                radius = jnp.maximum(rad[number, tile : tile + 1, :], 0.5) * (1.0 / CUTOFF)
                rows.append(coords + [aux[number, 12 + tile : 13 + tile, :], radius, 0.5 / radius])

            def block(ib, inner):
                at = pl.ds(pl.multiple_of(ib * ROWS, ROWS), ROWS)
                xi, yi, zi = col[0, at, :], col[1, at, :], col[2, at, :]
                ri, ai = col[3, at, :], col[4, at, :]
                fx, fy, fz = acc[0, at, :], acc[1, at, :], acc[2, at, :]
                for xj, yj, zj, qj, rj, aj in rows:
                    dx, dy, dz = xi - xj, yi - yj, zi - zj
                    u = dx * dx + dy * dy + dz * dz
                    s = jnp.maximum(1.0 - u, 0.0)
                    e = jnp.exp(u * (ai * aj))
                    inv = lax.rsqrt(u + (ri * rj) * e)
                    t = s * inv
                    m = (qj * t) * (1.0 + (t * inv) * (0.25 - 0.0625 * e))
                    fx = fx + m * dx
                    fy = fy + m * dy
                    fz = fz + m * dz
                acc[0, at, :] = fx
                acc[1, at, :] = fy
                acc[2, at, :] = fz
                return inner

            return lax.fori_loop(0, SLOTS // ROWS, block, carry)

        lax.fori_loop(0, count, visit, 0)
    for channel in range(3):
        for tile in range(TILES):
            total = gather_rows(acc[channel, tile * LANES : (tile + 1) * LANES, :])
            out[4 * channel + tile : 4 * channel + tile + 1, :] = total


def kernel_weights(reach):
    values = [math.exp(-0.5 * (index - reach) ** 2) for index in range(2 * reach + 1)]
    whole = sum(values)
    return [value / whole for value in values]


TAPS = kernel_weights(BLUR_REACH)


def blurred(values):
    rows = values.shape[0]
    near = pltpu.roll(values, 1, 0) + pltpu.roll(values, rows - 1, 0)
    far = pltpu.roll(values, 2, 0) + pltpu.roll(values, rows - 2, 0)
    return TAPS[2] * values + TAPS[1] * near + TAPS[0] * far


def profiles(row, side, base, rows, low, high, slope):
    number = lax.broadcasted_iota(jnp.int32, (rows, LANES), 0) + base
    shift = side * BRICK
    inside = (number >= low) & (number < high)
    window = inside & (number >= shift - SPLAT_MARGIN) & (number < shift + BRICK + SPLAT_MARGIN)
    moved = row + (float(shift) if isinstance(shift, int) else shift.astype(jnp.float32))
    gap = number.astype(jnp.float32) - moved
    plain = jnp.where(window, jnp.exp(-0.5 * gap * gap), 0.0)
    margin = SPLAT_MARGIN + BLUR_REACH
    reached = inside & (number >= shift - margin) & (number < shift + BRICK + margin)
    first = jnp.where(reached, blurred(plain), 0.0)
    if not slope:
        return first
    return first, jnp.where(reached, blurred(gap * plain), 0.0)


def split(values):
    high = values.astype(jnp.bfloat16)
    return high, (values - high.astype(jnp.float32)).astype(jnp.bfloat16)


def evolve_kernel(bounds, pos, aux, exp_ext, out, sums, px, left_hi, left_lo, right):
    out[...] = jnp.zeros_like(out)

    def splat(number, wide_x, wide_y):
        side_x = lax.rem(number, 3) - 1
        side_y = lax.rem(number // 3, 3) - 1
        side_z = number // 9 - 1
        if wide_x:
            side_x, base_x, rows_x, planes, first = 0, -PAD, WIDE, PLANES, 0
        else:
            base_x, rows_x, planes = side_x * 8, BRICK, 10
            base_x = jnp.where(side_x < 0, -PAD, PAD)
            first = jnp.where(side_x < 0, 0, BRICK)
        if wide_y:
            side_y, base_y, rows_y, start = 0, -PAD, WIDE, 0
        else:
            base_y, rows_y = jnp.where(side_y < 0, -PAD, PAD), BRICK
            start = pl.multiple_of(jnp.where(side_y < 0, 0, BRICK), BRICK)
        for tile in range(TILES):
            lanes = slice(tile * LANES, (tile + 1) * LANES)
            z = profiles(pos[number, 8 + tile : 9 + tile, :], side_z, -PAD, WIDE, bounds[4], bounds[5], False)
            z_hi, z_lo = split(z)
            right[0:WIDE, lanes] = z_hi
            right[WIDE : 2 * WIDE, lanes] = z_lo
            x = profiles(pos[number, tile : tile + 1, :], side_x, base_x, rows_x, bounds[0], bounds[1], False)
            px[0:rows_x, :] = x * aux[number, 20 + tile : 21 + tile, :]
            y = profiles(pos[number, 4 + tile : 5 + tile, :], side_y, base_y, rows_y, bounds[2], bounds[3], False)
            for plane in range(planes):
                rows = slice(plane * rows_y, (plane + 1) * rows_y)
                hi, lo = split(px[plane + 3 : plane + 4, :] * y)
                left_hi[rows, lanes] = hi
                left_lo[rows, lanes] = lo
        weights = right[...]
        dims = (((1,), (1,)), ((), ()))
        total = planes * rows_y
        placed = lax.dot_general(left_hi[0:total, :], weights, dims, preferred_element_type=jnp.float32)
        placed = placed + lax.dot_general(left_lo[0:total, :], weights, dims, preferred_element_type=jnp.float32)
        placed = placed.reshape(planes, rows_y, 2 * WIDE)
        at = pl.ds(first, planes)
        out[at, pl.ds(start, rows_y), 0 : 2 * WIDE] = out[at, pl.ds(start, rows_y), 0 : 2 * WIDE] + placed

    def both(k, carry):
        splat(9 * k + 4, True, True)
        return carry

    def only_x(k, carry):
        splat(9 * (k // 2) + 1 + 6 * lax.rem(k, 2), True, False)
        return carry

    def only_y(k, carry):
        splat(9 * (k // 2) + 3 + 2 * lax.rem(k, 2), False, True)
        return carry

    def neither(k, carry):
        splat(9 * (k // 4) + 2 * lax.rem(k, 2) + 6 * lax.rem(k // 2, 2), False, False)
        return carry

    lax.fori_loop(0, 3, both, 0)
    lax.fori_loop(0, 6, only_x, 0)
    lax.fori_loop(0, 6, only_y, 0)
    lax.fori_loop(0, 12, neither, 0)
    lane = lax.broadcasted_iota(jnp.int32, (WIDE, LANES), 1)
    row = lax.broadcasted_iota(jnp.int32, (WIDE, LANES), 0)
    own = (lane >= PAD) & (lane < PAD + BRICK) & (row >= PAD) & (row < PAD + BRICK)
    squares = jnp.zeros((WIDE, LANES), jnp.float32)
    cross = squares
    target = squares
    for plane in range(PLANES):
        raw = out[plane]
        value = jnp.where(lane < WIDE, raw + pltpu.roll(raw, LANES - WIDE, 1), 0.0)
        out[plane] = value
        if 5 <= plane < 5 + BRICK:
            value = jnp.where(own, value, 0.0)
            given = jnp.where(own, exp_ext[plane], 0.0)
            squares = squares + value * value
            cross = cross + value * given
            target = target + given * given
    sums[...] = jnp.zeros_like(sums)
    sums[0:1, :] = jnp.sum(squares, axis=0, keepdims=True)
    sums[1:2, :] = jnp.sum(cross, axis=0, keepdims=True)
    sums[2:3, :] = jnp.sum(target, axis=0, keepdims=True)


def fit_kernel(scale, parts, bounds, *refs):
    own, aux, extra, evolved, exp_ext, sums = refs[:6]
    gb = refs[6 : 6 + parts]
    moved, force, left, right, inner, px, pxs = refs[6 + parts :]
    squares = jnp.sum(sums[0:1, :], axis=1, keepdims=True)
    cross = jnp.sum(sums[1:2, :], axis=1, keepdims=True)
    target = jnp.sum(sums[2:3, :], axis=1, keepdims=True)
    norm = jnp.sqrt((squares + EPSILON) * (target + EPSILON))
    given_part = 1.0 / norm
    model_part = (cross / norm) / (squares + EPSILON)
    for plane in range(PLANES):
        s = exp_ext[plane] * given_part - evolved[plane] * model_part
        hi = s.astype(jnp.bfloat16).astype(jnp.float32)
        lo = (s - hi).astype(jnp.bfloat16).astype(jnp.float32)
        packed = hi + pltpu.roll(lo, WIDE, 1) + pltpu.roll(hi, 2 * WIDE, 1)
        left[plane * WIDE : (plane + 1) * WIDE, :] = packed.astype(jnp.bfloat16)
    right[...] = jnp.zeros_like(right)
    for tile in range(TILES):
        z, zs = profiles(own[8 + tile : 9 + tile, :], 0, -PAD, WIDE, bounds[4], bounds[5], True)
        for part, values in enumerate((z, zs)):
            lanes = slice(part * LANES, (part + 1) * LANES)
            hi, lo = split(values)
            right[0:WIDE, lanes] = hi
            right[WIDE : 2 * WIDE, lanes] = hi
            right[2 * WIDE : 3 * WIDE, lanes] = lo
        inner[...] = jnp.dot(left[...], right[...], preferred_element_type=jnp.float32)
        x, xs = profiles(own[tile : tile + 1, :], 0, -PAD, WIDE, bounds[0], bounds[1], True)
        y, ys = profiles(own[4 + tile : 5 + tile, :], 0, -PAD, WIDE, bounds[2], bounds[3], True)
        px[...] = x
        pxs[...] = xs
        turned_x = jnp.zeros((WIDE, LANES), jnp.float32)
        plain = turned_x
        turned_z = turned_x
        for plane in range(PLANES):
            rows = slice(plane * WIDE, (plane + 1) * WIDE)
            at_x = px[plane + 3 : plane + 4, :]
            part = inner[rows, 0:LANES]
            turned_x = turned_x + pxs[plane + 3 : plane + 4, :] * part
            plain = plain + at_x * part
            turned_z = turned_z + at_x * inner[rows, LANES : 2 * LANES]
        weight = scale * aux[20 + tile : 21 + tile, :]
        charge = -2.0 / (CUTOFF * CUTOFF) * aux[12 + tile : 13 + tile, :]
        sides = (turned_x * y, plain * ys, turned_z * y)
        for channel in range(3):
            at = slice(4 * channel + tile, 4 * channel + tile + 1)
            pair = gb[0][at, :]
            for other in gb[1:]:
                pair = pair + other[at, :]
            total = charge * pair + weight * jnp.sum(sides[channel], axis=0, keepdims=True)
            force[at, :] = total
            moved[at, :] = own[at, :] + STEP_SIZE * (extra[4 + tile : 5 + tile, :] * total)


def shifted(block, axis, step):
    count = lax.axis_size(axis)
    pairs = [(i, i + step) for i in range(count) if 0 <= i + step < count]
    return lax.ppermute(block, axis, pairs)


def both_sides(block, axis):
    return shifted(block, axis, 1), shifted(block, axis, -1)


def total_over_devices(values):
    for axis in AXES:
        count = lax.axis_size(axis)
        if count & (count - 1):
            values = lax.psum(values, axis)
            continue
        step = 1
        while step < count:
            pairs = [(i, i ^ step) for i in range(count)]
            values = values + lax.ppermute(values, axis, pairs)
            step *= 2
    return values


def widened(field, width):
    for dim, axis in enumerate(AXES):
        size = field.shape[dim]
        head = lax.slice_in_dim(field, 0, width, axis=dim)
        tail = lax.slice_in_dim(field, size - width, size, axis=dim)
        field = jnp.concatenate([shifted(tail, axis, 1), field, shifted(head, axis, -1)], axis=dim)
    return field


def f32(*shape):
    return jax.ShapeDtypeStruct(shape, jnp.float32)


def born_part(own, pieces, groups):
    cells = sum(count for count, _, _ in groups)
    args = [own] + [array for piece in pieces for array in piece]
    return call(
        functools.partial(born_kernel, groups),
        f32(TILES, LANES),
        cells * SLOTS * SLOTS * 20,
        scratch=[pltpu.VMEM((3, SLOTS, LANES), jnp.float32), pltpu.VMEM((SLOTS, LANES), jnp.float32)],
        n_in=len(args),
    )(*args)


def gb_part(own, radius, pieces, groups):
    cells = sum(count for count, _, _ in groups)
    args = [own, radius] + [array for piece in pieces for array in piece]
    return call(
        functools.partial(gb_kernel, groups),
        f32(3 * TILES, LANES),
        cells * SLOTS * SLOTS * 40,
        scratch=[pltpu.VMEM((5, SLOTS, LANES), jnp.float32), pltpu.VMEM((3, SLOTS, LANES), jnp.float32)],
        n_in=len(args),
    )(*args)


def gathered(block):
    line = jnp.stack([*(shifted(block, "gx", 1)[None]), block, *(shifted(block, "gx", -1)[None])])
    before_y, after_y = both_sides(line, "gy")
    plane = jnp.concatenate([before_y, line, after_y])
    before_z, after_z = both_sides(plane, "gz")
    return line, (before_y, after_y), plane, (before_z, after_z)


GROUPS_X = ((3, 0, 0),)
GROUPS_Y = ((3, -1, 0), (3, 1, 0))
GROUPS_Z = ((9, None, -1), (9, None, 1))


def on_device(positions, charges, atom_types, type_table, live_count, exp_map):
    sizes = [lax.axis_size(axis) for axis in AXES]
    places = [lax.axis_index(axis) for axis in AXES]
    bounds = []
    for size, place in zip(sizes, places):
        bounds += [-place * BRICK, (size - place) * BRICK]
    bounds = jnp.stack(bounds).astype(jnp.int32)
    scale = FIT_GAIN * float(BRICK**3 * sizes[0] * sizes[1] * sizes[2])

    onehot = (atom_types.reshape(SLOTS, 1) == jnp.arange(type_table.shape[1], dtype=jnp.int32)).astype(jnp.float32)
    props = jnp.sum(onehot[None] * type_table[:, None, :], axis=-1)
    living = (lax.iota(jnp.int32, SLOTS) < live_count.reshape(())).astype(jnp.float32)
    start = positions.reshape(3 * TILES, LANES)
    rest = jnp.stack([charges.reshape(SLOTS) * living, props[1] * living, props[2] * living])
    packed = jnp.concatenate([start, rest.reshape(3 * TILES, LANES)])
    extra = jnp.stack([props[0], living]).reshape(2 * TILES, LANES)

    exp_wide = widened(exp_map, BLUR_REACH + SPLAT_MARGIN)
    exp_ext = jnp.pad(exp_wide, ((0, 0), (3, 3), (3, LANES - PLANES - 3)))

    fixed = None
    moved = packed
    for step in range(STEPS):
        line, sides_y, plane, sides_z = gathered(moved)
        if fixed is None:
            fixed = (line, sides_y, plane, sides_z)
        partial = [
            born_part(moved, [(line, fixed[0])], GROUPS_X),
            born_part(moved, list(zip(sides_y, fixed[1])), GROUPS_Y),
            born_part(moved, list(zip(sides_z, fixed[3])), GROUPS_Z),
        ]
        radius = extra[:TILES] + (partial[0] + partial[1] + partial[2] - packed[16:20])
        near = gathered(radius)
        pairs = [
            gb_part(moved, radius, [(line, fixed[0], near[0])], GROUPS_X),
            gb_part(moved, radius, list(zip(sides_y, fixed[1], near[1])), GROUPS_Y),
            gb_part(moved, radius, list(zip(sides_z, fixed[3], near[3])), GROUPS_Z),
        ]
        every = jnp.concatenate([sides_z[0], plane, sides_z[1]])
        if step == 0:
            every_fixed = every
        evolved, sums = call(
            evolve_kernel,
            (f32(PLANES, WIDE, LANES), f32(8, LANES)),
            1 << 33,
            scratch=[
                pltpu.VMEM((WIDE, LANES), jnp.float32),
                pltpu.VMEM((PLANES * WIDE, SLOTS), jnp.bfloat16),
                pltpu.VMEM((PLANES * WIDE, SLOTS), jnp.bfloat16),
                pltpu.VMEM((2 * WIDE, SLOTS), jnp.bfloat16),
            ],
            smem=1,
            n_in=4,
        )(bounds, every, every_fixed, exp_ext)
        sums = total_over_devices(sums)
        moved, force = call(
            functools.partial(fit_kernel, scale, len(pairs)),
            (f32(3 * TILES, LANES), f32(3 * TILES, LANES)),
            1 << 30,
            scratch=[
                pltpu.VMEM((PLANES * WIDE, LANES), jnp.bfloat16),
                pltpu.VMEM((LANES, 2 * LANES), jnp.bfloat16),
                pltpu.VMEM((PLANES * WIDE, 2 * LANES), jnp.float32),
                pltpu.VMEM((WIDE, LANES), jnp.float32),
                pltpu.VMEM((WIDE, LANES), jnp.float32),
            ],
            smem=1,
            n_in=7 + len(pairs),
        )(bounds, moved, packed, extra, evolved, exp_ext, sums, *pairs)
    own = evolved[5 : 5 + BRICK, PAD : PAD + BRICK, PAD : PAD + BRICK]
    return (moved - start).reshape(positions.shape), force.reshape(positions.shape), own


def solution(mesh):
    placed = (
        P(None, *AXES, None),
        P(*AXES, None),
        P(*AXES, None),
        P(),
        P(*AXES),
        P(*AXES),
    )
    return jax.shard_map(
        on_device,
        mesh=mesh,
        in_specs=placed,
        out_specs=(placed[0], placed[0], P(*AXES)),
        check_vma=False,
    )
```

```python
import functools
import math

import jax
import jax.numpy as jnp
from jax import lax
from jax.experimental import pallas as pl
from jax.experimental.pallas import tpu as pltpu
from jax.sharding import PartitionSpec as P

SPLAT_MARGIN = 3
BLUR_REACH = 2
STEPS = 2
CUTOFF = 10.0
EPSILON = 1e-06
STEP_SIZE = 1.0
FIT_GAIN = 0.2

AXES = ("gx", "gy", "gz")
SLOTS = 512
LANES = 128
TILES = SLOTS // LANES
BRICK = 16
PLANES = 26
PAD = 8
WIDE = 32
INTERPRET = False


def call(kernel, out_shape, cost, scratch=(), smem=0, n_in=0, vmem=48):
    specs = [pl.BlockSpec(memory_space=pltpu.SMEM)] * smem
    specs += [pl.BlockSpec(memory_space=pltpu.VMEM)] * (n_in - smem)
    many = isinstance(out_shape, (tuple, list))
    out_spec = pl.BlockSpec(memory_space=pltpu.VMEM)
    return pl.pallas_call(
        kernel,
        out_shape=out_shape,
        in_specs=specs,
        out_specs=[out_spec] * len(out_shape) if many else out_spec,
        scratch_shapes=list(scratch),
        cost_estimate=pl.CostEstimate(flops=cost, bytes_accessed=1 << 18, transcendentals=0),
        compiler_params=pltpu.CompilerParams(vmem_limit_bytes=vmem << 20),
        interpret=INTERPRET,
    )


def spread(row):
    return jnp.transpose(jnp.broadcast_to(row, (LANES, LANES)))


def gather_rows(acc):
    return jnp.sum(jnp.transpose(acc), axis=0, keepdims=True)


BLOCK = 32
BLOCKS = SLOTS // BLOCK
UNROLL = 8
CELLS = 27
EMPTY = CELLS * TILES
ROOM = EMPTY + 4
FAR = 1e9


def three_parts(values):
    high = values.astype(jnp.bfloat16)
    rest = values - high.astype(jnp.float32)
    middle = rest.astype(jnp.bfloat16)
    return high, middle, (rest - middle.astype(jnp.float32)).astype(jnp.bfloat16)


def arrange_kernel(table, live_count, pos, charges, types, out, order, col, left):
    count = live_count[0]
    slot = lax.broadcasted_iota(jnp.int32, (TILES, LANES), 0) * LANES
    slot = slot + lax.broadcasted_iota(jnp.int32, (TILES, LANES), 1)
    living = slot < count
    alive = jnp.where(living, 1.0, 0.0)
    kinds = types[...]
    props = []
    for row in range(3):
        value = jnp.zeros((TILES, LANES), jnp.float32)
        for kind in range(table.shape[1]):
            value = jnp.where(kinds == kind, table[row, kind], value)
        props.append(value)
    group = jnp.zeros((TILES, LANES), jnp.float32)
    sub = lax.broadcasted_iota(jnp.int32, (SLOTS, LANES), 0)
    lane = lax.broadcasted_iota(jnp.int32, (SLOTS, LANES), 1)
    for dim, size in ((0, 256), (1, 128), (2, 64), (0, 32)):
        key = group * 64.0 + jnp.where(living, pos[4 * dim : 4 * dim + 4, :], 40.0)
        for tile in range(TILES):
            col[tile * LANES : (tile + 1) * LANES, :] = spread(key[tile : tile + 1, :])
        ranks = []
        for tile in range(TILES):
            row = key[tile : tile + 1, :]
            other = col[...]
            ahead = (other < row) | ((other == row) & (sub < lane + tile * LANES))
            ranks.append(jnp.sum(jnp.where(ahead, 1.0, 0.0), axis=0, keepdims=True))
        rank = jnp.concatenate(ranks, axis=0)
        group = jnp.floor(rank * (1.0 / size))
    order[...] = rank
    values = [pos[0:4, :], pos[4:8, :], pos[8:12, :], charges[...] * alive]
    values += [props[1] * alive, props[2] * alive, props[0], alive]
    total = jnp.zeros((3 * len(values), SLOTS), jnp.float32)
    for tile in range(TILES):
        block = jnp.concatenate([value[tile : tile + 1, :] for value in values], axis=0)
        for part, piece in enumerate(three_parts(block)):
            left[8 * part : 8 * part + 8, :] = piece.astype(jnp.float32)
        hot = jnp.where(rank[tile : tile + 1, :] == sub.astype(jnp.float32), 1.0, 0.0).astype(jnp.bfloat16)
        dims = (((1,), (1,)), ((), ()))
        total = total + lax.dot_general(left[...].astype(jnp.bfloat16), hot, dims, preferred_element_type=jnp.float32)
    total = total[0:8] + total[8:16] + total[16:24]
    for channel in range(8):
        for tile in range(TILES):
            at = slice(4 * channel + tile, 4 * channel + tile + 1)
            out[at, :] = total[channel : channel + 1, tile * LANES : (tile + 1) * LANES]


def restore_kernel(order, moved, start, force, out, left):
    values = [moved[4 * d : 4 * d + 4, :] - start[4 * d : 4 * d + 4, :] for d in range(3)]
    values += [force[4 * d : 4 * d + 4, :] for d in range(3)]
    values += [jnp.zeros((TILES, LANES), jnp.float32)] * 2
    sub = lax.broadcasted_iota(jnp.int32, (LANES, LANES), 0).astype(jnp.float32)
    totals = [jnp.zeros((24, LANES), jnp.float32) for _ in range(TILES)]
    for source in range(TILES):
        block = jnp.concatenate([value[source : source + 1, :] for value in values], axis=0)
        for part, piece in enumerate(three_parts(block)):
            left[8 * part : 8 * part + 8, :] = piece.astype(jnp.float32)
        parts = left[...].astype(jnp.bfloat16)
        for tile in range(TILES):
            hot = jnp.where(order[tile : tile + 1, :] == sub + float(source * LANES), 1.0, 0.0)
            totals[tile] = totals[tile] + jnp.dot(parts, hot.astype(jnp.bfloat16), preferred_element_type=jnp.float32)
    for tile in range(TILES):
        total = totals[tile][0:8] + totals[tile][8:16] + totals[tile][16:24]
        for channel in range(6):
            at = slice(4 * channel + tile, 4 * channel + tile + 1)
            out[at, :] = total[channel : channel + 1, :]


def plan_kernel(pos, aux, listed, tiles, active):
    own, own_aux = pos[13], aux[13]
    low, high = [], []
    for dim in range(3):
        living = own_aux[16:20, :] > 0.0
        value = own[4 * dim : 4 * dim + 4, :]
        lo, hi = jnp.where(living, value, FAR), jnp.where(living, value, -FAR)
        for step in (1, 2, 4, 8, 16):
            lo = jnp.minimum(lo, pltpu.roll(lo, LANES - step, 1))
            hi = jnp.maximum(hi, pltpu.roll(hi, LANES - step, 1))
        low.append(lo)
        high.append(hi)
    active[...] = jnp.zeros_like(active)
    tiles[EMPTY:ROOM] = jnp.zeros((ROOM - EMPTY, 8, LANES), jnp.float32)

    def visit(number, carry):
        sides = (lax.rem(number, 3) - 1, lax.rem(number // 3, 3) - 1, number // 9 - 1)
        living = aux[number, 16:20, :] > 0.0
        near_low, near_high = [], []
        for dim in range(3):
            moved = pos[number, 4 * dim : 4 * dim + 4, :] + sides[dim].astype(jnp.float32) * float(BRICK)
            near_low.append(jnp.min(jnp.where(living, moved, FAR), axis=1, keepdims=True))
            near_high.append(jnp.max(jnp.where(living, moved, -FAR), axis=1, keepdims=True))
            scaled = moved * (1.0 / CUTOFF)
            for tile in range(TILES):
                tiles[4 * number + tile, dim : dim + 1, :] = scaled[tile : tile + 1, :]
        for tile in range(TILES):
            tiles[4 * number + tile, 3:4, :] = aux[number, 16 + tile : 17 + tile, :]
            tiles[4 * number + tile, 4:5, :] = aux[number, 12 + tile : 13 + tile, :]
        for tile in range(TILES):
            apart = jnp.zeros((TILES, LANES), jnp.float32)
            for dim in range(3):
                lo, hi = low[dim][tile : tile + 1, :], high[dim][tile : tile + 1, :]
                gap = jnp.maximum(jnp.maximum(near_low[dim] - hi, lo - near_high[dim]), 0.0)
                apart = apart + gap * gap
            near = jnp.where(apart < CUTOFF * CUTOFF * 1.0001, 1.0, 0.0)
            active[tile, pl.ds(4 * number, TILES), :] = near
        return carry

    lax.fori_loop(0, CELLS, visit, 0)
    row = lax.broadcasted_iota(jnp.int32, (LANES, LANES), 0)
    lane = lax.broadcasted_iota(jnp.int32, (LANES, LANES), 1)
    before = jnp.where(lane < row, 1.0, 0.0).astype(jnp.bfloat16)
    for tile in range(TILES):
        flags = active[tile]
        ranks = jnp.dot(before, flags.astype(jnp.bfloat16), preferred_element_type=jnp.float32)
        for part in range(LANES // BLOCK):
            at = slice(part * BLOCK, part * BLOCK + 1)
            chosen = jnp.broadcast_to(flags[:, at], (LANES, LANES)) > 0.0
            place = jnp.broadcast_to(ranks[:, at], (LANES, LANES)).astype(jnp.int32)
            total = jnp.sum(jnp.where(chosen, 1, 0), axis=0, keepdims=True)
            entry = jnp.sum(jnp.where(chosen & (place == lane), row, 0), axis=0, keepdims=True)
            spot = lane[0:1, :]
            entry = jnp.where(spot < total, entry, EMPTY)
            block = tile * (LANES // BLOCK) + part
            listed[block : block + 1, :] = jnp.where(spot == LANES - 1, total, entry)


def born_kernel(listed, tiles, own, out, col, acc):
    for channel in range(3):
        for tile in range(TILES):
            row = own[4 * channel + tile : 4 * channel + tile + 1, :] * (1.0 / CUTOFF)
            col[channel, tile * LANES : (tile + 1) * LANES, :] = spread(row)

    def block(ib, carry):
        at = pl.ds(pl.multiple_of(ib * BLOCK, BLOCK), BLOCK)
        xi, yi, zi = col[0, at, :], col[1, at, :], col[2, at, :]

        def some(chunk, total):
            for k in range(UNROLL):
                tile = listed[ib, chunk * UNROLL + k]
                dx = xi - tiles[tile, 0:1, :]
                dy = yi - tiles[tile, 1:2, :]
                dz = zi - tiles[tile, 2:3, :]
                u = dx * dx + dy * dy + dz * dz
                s = jnp.maximum(1.0 - u, 0.0)
                e = jnp.exp(u * (-CUTOFF * CUTOFF / 8.0))
                total = total + (e * s) * (s * tiles[tile, 3:4, :])
            return total

        chunks = (listed[ib, LANES - 1] + UNROLL - 1) // UNROLL
        acc[at, :] = lax.fori_loop(0, chunks, some, jnp.zeros((BLOCK, LANES), jnp.float32))
        return carry

    lax.fori_loop(0, BLOCKS, block, 0)
    for tile in range(TILES):
        total = gather_rows(acc[tile * LANES : (tile + 1) * LANES, :]) - own[16 + tile : 17 + tile, :]
        out[tile : tile + 1, :] = own[24 + tile : 25 + tile, :] + total


def gb_kernel(listed, tiles, own, own_radius, radii, out, col, acc, rows):
    for tile in range(TILES):
        at = slice(tile * LANES, (tile + 1) * LANES)
        for channel in range(3):
            row = own[4 * channel + tile : 4 * channel + tile + 1, :] * (1.0 / CUTOFF)
            col[channel, at, :] = spread(row)
        radius = spread(own_radius[tile : tile + 1, :] * (1.0 / CUTOFF))
        col[3, at, :] = radius
        col[4, at, :] = -0.5 / radius
    rows[EMPTY:ROOM] = jnp.ones((ROOM - EMPTY, 2, LANES), jnp.float32)

    def ready(number, carry):
        radius = jnp.maximum(radii[number], 0.5) * (1.0 / CUTOFF)
        half = 0.5 / radius
        for tile in range(TILES):
            rows[4 * number + tile, 0:1, :] = radius[tile : tile + 1, :]
            rows[4 * number + tile, 1:2, :] = half[tile : tile + 1, :]
        return carry

    lax.fori_loop(0, CELLS, ready, 0)

    def block(ib, carry):
        at = pl.ds(pl.multiple_of(ib * BLOCK, BLOCK), BLOCK)
        xi, yi, zi = col[0, at, :], col[1, at, :], col[2, at, :]
        ri, ai = col[3, at, :], col[4, at, :]

        def some(chunk, force):
            fx, fy, fz = force
            for k in range(UNROLL):
                tile = listed[ib, chunk * UNROLL + k]
                dx = xi - tiles[tile, 0:1, :]
                dy = yi - tiles[tile, 1:2, :]
                dz = zi - tiles[tile, 2:3, :]
                u = dx * dx + dy * dy + dz * dz
                s = jnp.maximum(1.0 - u, 0.0)
                e = jnp.exp(u * (ai * rows[tile, 1:2, :]))
                inv = lax.rsqrt(u + (ri * rows[tile, 0:1, :]) * e)
                t = s * inv
                m = (tiles[tile, 4:5, :] * t) * (1.0 + (t * inv) * (0.25 - 0.0625 * e))
                fx = fx + m * dx
                fy = fy + m * dy
                fz = fz + m * dz
            return fx, fy, fz

        chunks = (listed[ib, LANES - 1] + UNROLL - 1) // UNROLL
        zero = jnp.zeros((BLOCK, LANES), jnp.float32)
        force = lax.fori_loop(0, chunks, some, (zero, zero, zero))
        for channel in range(3):
            acc[channel, at, :] = force[channel]
        return carry

    lax.fori_loop(0, BLOCKS, block, 0)
    for channel in range(3):
        for tile in range(TILES):
            total = gather_rows(acc[channel, tile * LANES : (tile + 1) * LANES, :])
            out[4 * channel + tile : 4 * channel + tile + 1, :] = total


def kernel_weights(reach):
    values = [math.exp(-0.5 * (index - reach) ** 2) for index in range(2 * reach + 1)]
    whole = sum(values)
    return [value / whole for value in values]


TAPS = kernel_weights(BLUR_REACH)


def blurred(values):
    rows = values.shape[0]
    near = pltpu.roll(values, 1, 0) + pltpu.roll(values, rows - 1, 0)
    far = pltpu.roll(values, 2, 0) + pltpu.roll(values, rows - 2, 0)
    return TAPS[2] * values + TAPS[1] * near + TAPS[0] * far


def profiles(row, side, base, rows, low, high, slope):
    number = lax.broadcasted_iota(jnp.int32, (rows, LANES), 0) + base
    shift = side * BRICK
    inside = (number >= low) & (number < high)
    window = inside & (number >= shift - SPLAT_MARGIN) & (number < shift + BRICK + SPLAT_MARGIN)
    moved = row + (float(shift) if isinstance(shift, int) else shift.astype(jnp.float32))
    gap = number.astype(jnp.float32) - moved
    plain = jnp.where(window, jnp.exp(-0.5 * gap * gap), 0.0)
    margin = SPLAT_MARGIN + BLUR_REACH
    reached = inside & (number >= shift - margin) & (number < shift + BRICK + margin)
    first = jnp.where(reached, blurred(plain), 0.0)
    if not slope:
        return first
    return first, jnp.where(reached, blurred(gap * plain), 0.0)


def split(values):
    high = values.astype(jnp.bfloat16)
    return high, (values - high.astype(jnp.float32)).astype(jnp.bfloat16)


def evolve_kernel(bounds, pos, aux, exp_ext, out, sums, px, left_hi, left_lo, right):
    out[...] = jnp.zeros_like(out)

    def splat(number, wide_x, wide_y):
        side_x = lax.rem(number, 3) - 1
        side_y = lax.rem(number // 3, 3) - 1
        side_z = number // 9 - 1
        if wide_x:
            side_x, base_x, rows_x, planes, first = 0, -PAD, WIDE, PLANES, 0
        else:
            base_x, rows_x, planes = side_x * 8, BRICK, 10
            base_x = jnp.where(side_x < 0, -PAD, PAD)
            first = jnp.where(side_x < 0, 0, BRICK)
        if wide_y:
            side_y, base_y, rows_y, start = 0, -PAD, WIDE, 0
        else:
            base_y, rows_y = jnp.where(side_y < 0, -PAD, PAD), BRICK
            start = pl.multiple_of(jnp.where(side_y < 0, 0, BRICK), BRICK)
        for tile in range(TILES):
            lanes = slice(tile * LANES, (tile + 1) * LANES)
            z = profiles(pos[number, 8 + tile : 9 + tile, :], side_z, -PAD, WIDE, bounds[4], bounds[5], False)
            z_hi, z_lo = split(z)
            right[0:WIDE, lanes] = z_hi
            right[WIDE : 2 * WIDE, lanes] = z_lo
            x = profiles(pos[number, tile : tile + 1, :], side_x, base_x, rows_x, bounds[0], bounds[1], False)
            px[0:rows_x, :] = x * aux[number, 20 + tile : 21 + tile, :]
            y = profiles(pos[number, 4 + tile : 5 + tile, :], side_y, base_y, rows_y, bounds[2], bounds[3], False)
            for plane in range(planes):
                rows = slice(plane * rows_y, (plane + 1) * rows_y)
                hi, lo = split(px[plane + 3 : plane + 4, :] * y)
                left_hi[rows, lanes] = hi
                left_lo[rows, lanes] = lo
        weights = right[...]
        dims = (((1,), (1,)), ((), ()))
        total = planes * rows_y
        placed = lax.dot_general(left_hi[0:total, :], weights, dims, preferred_element_type=jnp.float32)
        placed = placed + lax.dot_general(left_lo[0:total, :], weights, dims, preferred_element_type=jnp.float32)
        placed = placed.reshape(planes, rows_y, 2 * WIDE)
        at = pl.ds(first, planes)
        out[at, pl.ds(start, rows_y), 0 : 2 * WIDE] = out[at, pl.ds(start, rows_y), 0 : 2 * WIDE] + placed

    def both(k, carry):
        splat(9 * k + 4, True, True)
        return carry

    def only_x(k, carry):
        splat(9 * (k // 2) + 1 + 6 * lax.rem(k, 2), True, False)
        return carry

    def only_y(k, carry):
        splat(9 * (k // 2) + 3 + 2 * lax.rem(k, 2), False, True)
        return carry

    def neither(k, carry):
        splat(9 * (k // 4) + 2 * lax.rem(k, 2) + 6 * lax.rem(k // 2, 2), False, False)
        return carry

    lax.fori_loop(0, 3, both, 0)
    lax.fori_loop(0, 6, only_x, 0)
    lax.fori_loop(0, 6, only_y, 0)
    lax.fori_loop(0, 12, neither, 0)
    lane = lax.broadcasted_iota(jnp.int32, (WIDE, LANES), 1)
    row = lax.broadcasted_iota(jnp.int32, (WIDE, LANES), 0)
    own = (lane >= PAD) & (lane < PAD + BRICK) & (row >= PAD) & (row < PAD + BRICK)
    squares = jnp.zeros((WIDE, LANES), jnp.float32)
    cross = squares
    target = squares
    for plane in range(PLANES):
        raw = out[plane]
        value = jnp.where(lane < WIDE, raw + pltpu.roll(raw, LANES - WIDE, 1), 0.0)
        out[plane] = value
        if 5 <= plane < 5 + BRICK:
            value = jnp.where(own, value, 0.0)
            given = jnp.where(own, exp_ext[plane], 0.0)
            squares = squares + value * value
            cross = cross + value * given
            target = target + given * given
    sums[...] = jnp.zeros_like(sums)
    sums[0:1, :] = jnp.sum(squares, axis=0, keepdims=True)
    sums[1:2, :] = jnp.sum(cross, axis=0, keepdims=True)
    sums[2:3, :] = jnp.sum(target, axis=0, keepdims=True)


def fit_kernel(scale, parts, bounds, *refs):
    own, evolved, exp_ext, sums = refs[:4]
    gb = refs[4 : 4 + parts]
    moved, force, left, right, inner, px, pxs = refs[4 + parts :]
    squares = jnp.sum(sums[0:1, :], axis=1, keepdims=True)
    cross = jnp.sum(sums[1:2, :], axis=1, keepdims=True)
    target = jnp.sum(sums[2:3, :], axis=1, keepdims=True)
    norm = jnp.sqrt((squares + EPSILON) * (target + EPSILON))
    given_part = 1.0 / norm
    model_part = (cross / norm) / (squares + EPSILON)
    for plane in range(PLANES):
        s = exp_ext[plane] * given_part - evolved[plane] * model_part
        hi = s.astype(jnp.bfloat16).astype(jnp.float32)
        lo = (s - hi).astype(jnp.bfloat16).astype(jnp.float32)
        packed = hi + pltpu.roll(lo, WIDE, 1) + pltpu.roll(hi, 2 * WIDE, 1)
        left[plane * WIDE : (plane + 1) * WIDE, :] = packed.astype(jnp.bfloat16)
    right[...] = jnp.zeros_like(right)
    for tile in range(TILES):
        z, zs = profiles(own[8 + tile : 9 + tile, :], 0, -PAD, WIDE, bounds[4], bounds[5], True)
        for part, values in enumerate((z, zs)):
            lanes = slice(part * LANES, (part + 1) * LANES)
            hi, lo = split(values)
            right[0:WIDE, lanes] = hi
            right[WIDE : 2 * WIDE, lanes] = hi
            right[2 * WIDE : 3 * WIDE, lanes] = lo
        inner[...] = jnp.dot(left[...], right[...], preferred_element_type=jnp.float32)
        x, xs = profiles(own[tile : tile + 1, :], 0, -PAD, WIDE, bounds[0], bounds[1], True)
        y, ys = profiles(own[4 + tile : 5 + tile, :], 0, -PAD, WIDE, bounds[2], bounds[3], True)
        px[...] = x
        pxs[...] = xs
        turned_x = jnp.zeros((WIDE, LANES), jnp.float32)
        plain = turned_x
        turned_z = turned_x
        for plane in range(PLANES):
            rows = slice(plane * WIDE, (plane + 1) * WIDE)
            at_x = px[plane + 3 : plane + 4, :]
            part = inner[rows, 0:LANES]
            turned_x = turned_x + pxs[plane + 3 : plane + 4, :] * part
            plain = plain + at_x * part
            turned_z = turned_z + at_x * inner[rows, LANES : 2 * LANES]
        weight = scale * own[20 + tile : 21 + tile, :]
        charge = -2.0 / (CUTOFF * CUTOFF) * own[12 + tile : 13 + tile, :]
        sides = (turned_x * y, plain * ys, turned_z * y)
        for channel in range(3):
            at = slice(4 * channel + tile, 4 * channel + tile + 1)
            pair = gb[0][at, :]
            for other in gb[1:]:
                pair = pair + other[at, :]
            total = charge * pair + weight * jnp.sum(sides[channel], axis=0, keepdims=True)
            force[at, :] = total
            moved[at, :] = own[at, :] + STEP_SIZE * (own[28 + tile : 29 + tile, :] * total)


def shifted(block, axis, step):
    count = lax.axis_size(axis)
    pairs = [(i, i + step) for i in range(count) if 0 <= i + step < count]
    return lax.ppermute(block, axis, pairs)


def both_sides(block, axis):
    return shifted(block, axis, 1), shifted(block, axis, -1)


def total_over_devices(values):
    for axis in AXES:
        count = lax.axis_size(axis)
        if count & (count - 1):
            values = lax.psum(values, axis)
            continue
        step = 1
        while step < count:
            pairs = [(i, i ^ step) for i in range(count)]
            values = values + lax.ppermute(values, axis, pairs)
            step *= 2
    return values


def widened(field, width):
    for dim, axis in enumerate(AXES):
        size = field.shape[dim]
        head = lax.slice_in_dim(field, 0, width, axis=dim)
        tail = lax.slice_in_dim(field, size - width, size, axis=dim)
        field = jnp.concatenate([shifted(tail, axis, 1), field, shifted(head, axis, -1)], axis=dim)
    return field


def f32(*shape):
    return jax.ShapeDtypeStruct(shape, jnp.float32)


def gathered(block):
    line = jnp.stack([*(shifted(block, "gx", 1)[None]), block, *(shifted(block, "gx", -1)[None])])
    before_y, after_y = both_sides(line, "gy")
    plane = jnp.concatenate([before_y, line, after_y])
    before_z, after_z = both_sides(plane, "gz")
    return line, (before_y, after_y), plane, (before_z, after_z)


def on_device(positions, charges, atom_types, type_table, live_count, exp_map):
    sizes = [lax.axis_size(axis) for axis in AXES]
    places = [lax.axis_index(axis) for axis in AXES]
    bounds = []
    for size, place in zip(sizes, places):
        bounds += [-place * BRICK, (size - place) * BRICK]
    bounds = jnp.stack(bounds).astype(jnp.int32)
    scale = FIT_GAIN * float(BRICK**3 * sizes[0] * sizes[1] * sizes[2])

    atoms, order = call(
        arrange_kernel,
        (f32(32, LANES), f32(TILES, LANES)),
        1 << 22,
        scratch=[pltpu.VMEM((SLOTS, LANES), jnp.float32), pltpu.VMEM((24, LANES), jnp.float32)],
        smem=2,
        n_in=5,
    )(
        type_table,
        live_count.reshape(1),
        positions.reshape(3 * TILES, LANES),
        charges.reshape(TILES, LANES),
        atom_types.reshape(TILES, LANES),
    )

    exp_wide = widened(exp_map, BLUR_REACH + SPLAT_MARGIN)
    exp_ext = jnp.pad(exp_wide, ((0, 0), (3, 3), (3, LANES - PLANES - 3)))

    fixed = None
    moved = atoms
    for step in range(STEPS):
        line, sides_y, plane, sides_z = gathered(moved[:24] if step == 0 else moved)
        every = jnp.concatenate([sides_z[0], plane, sides_z[1]])
        if fixed is None:
            fixed = every
        listed, tiles = call(
            plan_kernel,
            (jax.ShapeDtypeStruct((BLOCKS, LANES), jnp.int32), f32(ROOM, 8, LANES)),
            1 << 22,
            scratch=[pltpu.VMEM((TILES, LANES, LANES), jnp.float32)],
            n_in=2,
        )(every, fixed)
        own = atoms if step == 0 else jnp.concatenate([moved, atoms[12:]])
        radius = call(
            born_kernel,
            f32(TILES, LANES),
            1 << 27,
            scratch=[pltpu.VMEM((3, SLOTS, LANES), jnp.float32), pltpu.VMEM((SLOTS, LANES), jnp.float32)],
            smem=1,
            n_in=3,
        )(listed, tiles, own)
        near = gathered(radius)
        radii = jnp.concatenate([near[3][0], near[2], near[3][1]])
        pairs = [
            call(
                gb_kernel,
                f32(3 * TILES, LANES),
                1 << 28,
                scratch=[
                    pltpu.VMEM((5, SLOTS, LANES), jnp.float32),
                    pltpu.VMEM((3, SLOTS, LANES), jnp.float32),
                    pltpu.VMEM((ROOM, 2, LANES), jnp.float32),
                ],
                smem=1,
                n_in=5,
            )(listed, tiles, own, radius, radii)
        ]
        evolved, sums = call(
            evolve_kernel,
            (f32(PLANES, WIDE, LANES), f32(8, LANES)),
            1 << 33,
            scratch=[
                pltpu.VMEM((WIDE, LANES), jnp.float32),
                pltpu.VMEM((PLANES * WIDE, SLOTS), jnp.bfloat16),
                pltpu.VMEM((PLANES * WIDE, SLOTS), jnp.bfloat16),
                pltpu.VMEM((2 * WIDE, SLOTS), jnp.bfloat16),
            ],
            smem=1,
            n_in=4,
        )(bounds, every, fixed, exp_ext)
        sums = total_over_devices(sums)
        moved, force = call(
            functools.partial(fit_kernel, scale, len(pairs)),
            (f32(3 * TILES, LANES), f32(3 * TILES, LANES)),
            1 << 30,
            scratch=[
                pltpu.VMEM((PLANES * WIDE, LANES), jnp.bfloat16),
                pltpu.VMEM((LANES, 2 * LANES), jnp.bfloat16),
                pltpu.VMEM((PLANES * WIDE, 2 * LANES), jnp.float32),
                pltpu.VMEM((WIDE, LANES), jnp.float32),
                pltpu.VMEM((WIDE, LANES), jnp.float32),
            ],
            smem=1,
            n_in=5 + len(pairs),
        )(bounds, own, evolved, exp_ext, sums, *pairs)
    results = call(
        restore_kernel,
        f32(6 * TILES, LANES),
        1 << 20,
        scratch=[pltpu.VMEM((24, LANES), jnp.float32)],
        n_in=4,
    )(order, moved, atoms, force)
    own = evolved[5 : 5 + BRICK, PAD : PAD + BRICK, PAD : PAD + BRICK]
    results = results.reshape((2,) + positions.shape)
    return results[0], results[1], own


def solution(mesh):
    placed = (
        P(None, *AXES, None),
        P(*AXES, None),
        P(*AXES, None),
        P(),
        P(*AXES),
        P(*AXES),
    )
    return jax.shard_map(
        on_device,
        mesh=mesh,
        in_specs=placed,
        out_specs=(placed[0], placed[0], P(*AXES)),
        check_vma=False,
    )
```

```python
import functools
import math

import jax
import jax.numpy as jnp
from jax import lax
from jax.experimental import pallas as pl
from jax.experimental.pallas import tpu as pltpu
from jax.sharding import PartitionSpec as P

SPLAT_MARGIN = 3
BLUR_REACH = 2
STEPS = 2
CUTOFF = 10.0
EPSILON = 1e-06
STEP_SIZE = 1.0
FIT_GAIN = 0.2

AXES = ("gx", "gy", "gz")
SLOTS = 512
LANES = 128
TILES = SLOTS // LANES
BRICK = 16
PLANES = 26
PAD = 8
WIDE = 32
INTERPRET = False


def call(kernel, out_shape, cost, scratch=(), smem=0, n_in=0, vmem=48):
    specs = [pl.BlockSpec(memory_space=pltpu.SMEM)] * smem
    specs += [pl.BlockSpec(memory_space=pltpu.VMEM)] * (n_in - smem)
    many = isinstance(out_shape, (tuple, list))
    out_spec = pl.BlockSpec(memory_space=pltpu.VMEM)
    return pl.pallas_call(
        kernel,
        out_shape=out_shape,
        in_specs=specs,
        out_specs=[out_spec] * len(out_shape) if many else out_spec,
        scratch_shapes=list(scratch),
        cost_estimate=pl.CostEstimate(flops=cost, bytes_accessed=1 << 18, transcendentals=0),
        compiler_params=pltpu.CompilerParams(vmem_limit_bytes=vmem << 20),
        interpret=INTERPRET,
    )


def spread(row):
    return jnp.transpose(jnp.broadcast_to(row, (LANES, LANES)))


def gather_rows(acc):
    return jnp.sum(jnp.transpose(acc), axis=0, keepdims=True)


BLOCK = 32
BLOCKS = SLOTS // BLOCK
UNROLL = 8
CELLS = 27
EMPTY = CELLS * TILES
ROOM = EMPTY + 4
FAR = 1e9


def three_parts(values):
    high = values.astype(jnp.bfloat16)
    rest = values - high.astype(jnp.float32)
    middle = rest.astype(jnp.bfloat16)
    return high, middle, (rest - middle.astype(jnp.float32)).astype(jnp.bfloat16)


def arrange_kernel(table, live_count, pos, charges, types, out, order, col, left):
    count = live_count[0]
    slot = lax.broadcasted_iota(jnp.int32, (TILES, LANES), 0) * LANES
    slot = slot + lax.broadcasted_iota(jnp.int32, (TILES, LANES), 1)
    living = slot < count
    alive = jnp.where(living, 1.0, 0.0)
    kinds = types[...]
    props = []
    for row in range(3):
        value = jnp.zeros((TILES, LANES), jnp.float32)
        for kind in range(table.shape[1]):
            value = jnp.where(kinds == kind, table[row, kind], value)
        props.append(value)
    group = jnp.zeros((TILES, LANES), jnp.float32)
    sub = lax.broadcasted_iota(jnp.int32, (SLOTS, LANES), 0)
    lane = lax.broadcasted_iota(jnp.int32, (SLOTS, LANES), 1)
    for dim, size in ((0, 256), (1, 128), (2, 64), (0, 32)):
        key = group * 64.0 + jnp.where(living, pos[4 * dim : 4 * dim + 4, :], 40.0)
        for tile in range(TILES):
            col[tile * LANES : (tile + 1) * LANES, :] = spread(key[tile : tile + 1, :])
        ranks = []
        for tile in range(TILES):
            row = key[tile : tile + 1, :]
            other = col[...]
            ahead = (other < row) | ((other == row) & (sub < lane + tile * LANES))
            ranks.append(jnp.sum(jnp.where(ahead, 1.0, 0.0), axis=0, keepdims=True))
        rank = jnp.concatenate(ranks, axis=0)
        group = jnp.floor(rank * (1.0 / size))
    order[...] = rank
    values = [pos[0:4, :], pos[4:8, :], pos[8:12, :], charges[...] * alive]
    values += [props[1] * alive, props[2] * alive, props[0], alive]
    total = jnp.zeros((3 * len(values), SLOTS), jnp.float32)
    for tile in range(TILES):
        block = jnp.concatenate([value[tile : tile + 1, :] for value in values], axis=0)
        for part, piece in enumerate(three_parts(block)):
            left[8 * part : 8 * part + 8, :] = piece.astype(jnp.float32)
        hot = jnp.where(rank[tile : tile + 1, :] == sub.astype(jnp.float32), 1.0, 0.0).astype(jnp.bfloat16)
        dims = (((1,), (1,)), ((), ()))
        total = total + lax.dot_general(left[...].astype(jnp.bfloat16), hot, dims, preferred_element_type=jnp.float32)
    total = total[0:8] + total[8:16] + total[16:24]
    for channel in range(8):
        for tile in range(TILES):
            at = slice(4 * channel + tile, 4 * channel + tile + 1)
            out[at, :] = total[channel : channel + 1, tile * LANES : (tile + 1) * LANES]


def restore_kernel(order, moved, start, force, out, left):
    values = [moved[4 * d : 4 * d + 4, :] - start[4 * d : 4 * d + 4, :] for d in range(3)]
    values += [force[4 * d : 4 * d + 4, :] for d in range(3)]
    values += [jnp.zeros((TILES, LANES), jnp.float32)] * 2
    sub = lax.broadcasted_iota(jnp.int32, (LANES, LANES), 0).astype(jnp.float32)
    totals = [jnp.zeros((24, LANES), jnp.float32) for _ in range(TILES)]
    for source in range(TILES):
        block = jnp.concatenate([value[source : source + 1, :] for value in values], axis=0)
        for part, piece in enumerate(three_parts(block)):
            left[8 * part : 8 * part + 8, :] = piece.astype(jnp.float32)
        parts = left[...].astype(jnp.bfloat16)
        for tile in range(TILES):
            hot = jnp.where(order[tile : tile + 1, :] == sub + float(source * LANES), 1.0, 0.0)
            totals[tile] = totals[tile] + jnp.dot(parts, hot.astype(jnp.bfloat16), preferred_element_type=jnp.float32)
    for tile in range(TILES):
        total = totals[tile][0:8] + totals[tile][8:16] + totals[tile][16:24]
        for channel in range(6):
            at = slice(4 * channel + tile, 4 * channel + tile + 1)
            out[at, :] = total[channel : channel + 1, :]


def plan_kernel(rows, fields, *refs):
    info, own = refs[:2]
    sources = refs[2:5]
    if fields == 2:
        known = ()
        listed, tiles, evolved, given, sums, active = refs[5:]
    else:
        known = refs[5:6]
        given = refs[6]
        listed, tiles, evolved, sums, active = refs[7:]
    low, high = [], []
    for dim in range(3):
        living = own[28:32, :] > 0.0
        value = own[4 * dim : 4 * dim + 4, :]
        lo, hi = jnp.where(living, value, FAR), jnp.where(living, value, -FAR)
        for step in (1, 2, 4, 8, 16):
            lo = jnp.minimum(lo, pltpu.roll(lo, LANES - step, 1))
            hi = jnp.maximum(hi, pltpu.roll(hi, LANES - step, 1))
        low.append(lo)
        high.append(hi)
    active[...] = jnp.zeros_like(active)
    tiles[EMPTY:ROOM] = jnp.zeros((ROOM - EMPTY, 8, LANES), jnp.float32)
    after_first, valid = arrivals(info, 2)
    slots = (1, jnp.where(after_first, 2, 0), jnp.where(after_first, 0, 2))
    for source, slot, ok in zip(sources, slots, (None,) + valid):

        def visit(cell, carry, source=source, slot=slot, ok=ok):
            number = slot * 9 + cell
            sides = (lax.rem(cell, 3) - 1, cell // 3 - 1, slot - 1)
            block = source[pl.ds(pl.multiple_of(cell * rows, 8), rows), :]
            if ok is not None:
                block = block * ok
            if known:
                charge = [known[0][4 * number + tile, 4:5, :] for tile in range(TILES)]
                screen = [known[0][4 * number + tile, 3:4, :] for tile in range(TILES)]
                living = jnp.concatenate(screen, axis=0) > 0.0
            else:
                charge = [block[12 + tile : 13 + tile] for tile in range(TILES)]
                screen = [block[16 + tile : 17 + tile] for tile in range(TILES)]
                living = block[16:20] > 0.0
            near_low, near_high = [], []
            for dim in range(3):
                side = sides[dim]
                shift = float(side * BRICK) if isinstance(side, int) else side.astype(jnp.float32) * float(BRICK)
                moved = block[4 * dim : 4 * dim + 4] + shift
                near_low.append(jnp.min(jnp.where(living, moved, FAR), axis=1, keepdims=True))
                near_high.append(jnp.max(jnp.where(living, moved, -FAR), axis=1, keepdims=True))
                scaled = moved * (1.0 / CUTOFF)
                for tile in range(TILES):
                    tiles[4 * number + tile, dim : dim + 1, :] = scaled[tile : tile + 1, :]
            for tile in range(TILES):
                tiles[4 * number + tile, 3:4, :] = screen[tile]
                tiles[4 * number + tile, 4:5, :] = charge[tile]
            for tile in range(TILES):
                apart = jnp.zeros((TILES, LANES), jnp.float32)
                for dim in range(3):
                    lo, hi = low[dim][tile : tile + 1, :], high[dim][tile : tile + 1, :]
                    gap = jnp.maximum(jnp.maximum(near_low[dim] - hi, lo - near_high[dim]), 0.0)
                    apart = apart + gap * gap
                near = jnp.where(apart < CUTOFF * CUTOFF * 1.0001, 1.0, 0.0)
                active[tile, pl.ds(4 * number, TILES), :] = near
            return carry

        lax.fori_loop(0, 9, visit, 0)
    row = lax.broadcasted_iota(jnp.int32, (LANES, LANES), 0)
    lane = lax.broadcasted_iota(jnp.int32, (LANES, LANES), 1)
    before = jnp.where(lane < row, 1.0, 0.0).astype(jnp.bfloat16)
    for tile in range(TILES):
        flags = active[tile]
        ranks = jnp.dot(before, flags.astype(jnp.bfloat16), preferred_element_type=jnp.float32)
        for part in range(LANES // BLOCK):
            at = slice(part * BLOCK, part * BLOCK + 1)
            chosen = jnp.broadcast_to(flags[:, at], (LANES, LANES)) > 0.0
            place = jnp.broadcast_to(ranks[:, at], (LANES, LANES)).astype(jnp.int32)
            total = jnp.sum(jnp.where(chosen, 1, 0), axis=0, keepdims=True)
            entry = jnp.sum(jnp.where(chosen & (place == lane), row, 0), axis=0, keepdims=True)
            spot = lane[0:1, :]
            entry = jnp.where(spot < total, entry, EMPTY)
            block = tile * (LANES // BLOCK) + part
            listed[block : block + 1, :] = jnp.where(spot == LANES - 1, total, entry)
    lane = lax.broadcasted_iota(jnp.int32, (8, LANES), 1)
    sub = lane & (WIDE - 1)
    own_points = (lane >= WIDE) & (lane < 3 * WIDE) & (sub >= PAD) & (sub < PAD + BRICK)
    squares = jnp.zeros((8, LANES), jnp.float32)
    cross = squares
    target = squares
    adds = shift_masks(info, 2)
    for plane in range(PLANES):
        at = slice(9 * rows + 8 * plane, 9 * rows + 8 * plane + 8)
        value = received(2, adds, sources, at)
        evolved[plane] = value
        if fields == 2:
            at = slice(9 * rows + 8 * (PLANES + plane), 9 * rows + 8 * (PLANES + plane) + 8)
            given[plane] = received(2, adds, sources, at)
        if 5 <= plane < 5 + BRICK:
            value = jnp.where(own_points, value, 0.0)
            wanted = jnp.where(own_points, given[plane], 0.0)
            squares = squares + value * value
            cross = cross + value * wanted
            target = target + wanted * wanted
    sums[...] = jnp.zeros_like(sums)
    sums[0:1, :] = jnp.sum(squares, axis=0, keepdims=True)
    sums[1:2, :] = jnp.sum(cross, axis=0, keepdims=True)
    sums[2:3, :] = jnp.sum(target, axis=0, keepdims=True)


def arrivals(info, axis):
    after_first = info[6 + 2 * axis] == 0
    return after_first, (1.0, jnp.where(info[7 + 2 * axis] > 0, 1.0, 0.0))


def shift_masks(info, axis):
    lane = lax.broadcasted_iota(jnp.int32, (8, LANES), 1)
    upper = (lane >= 64) if axis == 1 else ((lane & (WIDE - 1)) >= BRICK)
    after_first, valid = arrivals(info, axis)
    after_one = jnp.where(after_first, 1.0, 0.0)
    masks = []
    for after, ok in zip((after_one, 1.0 - after_one), valid):
        masks.append((jnp.where(upper, after * ok, 0.0), jnp.where(upper, 0.0, (1.0 - after) * ok)))
    return masks


def received(axis, masks, sources, at):
    value = sources[0][at, :]
    for (from_after, from_before), source in zip(masks, sources[1:]):
        other = source[at, :]
        if axis == 1:
            value = value + pltpu.roll(other, 64, 1) * (from_after + from_before)
        else:
            value = value + pltpu.roll(other, BRICK, 1) * from_after
            value = value + pltpu.roll(other, LANES - BRICK, 1) * from_before
    return value


def merge_kernel(axis, count, rows, fields, info, mine, first, second, out):
    after_first, valid = arrivals(info, axis)
    span = count * rows
    out[span : 2 * span, :] = mine[0:span, :]
    slots = (jnp.where(after_first, 2 * span, 0), jnp.where(after_first, 0, 2 * span))
    for source, slot, ok in zip((first, second), slots, valid):
        out[pl.ds(pl.multiple_of(slot, 8), span), :] = source[0:span, :] * ok
    if axis == 0:
        for field in range(fields):
            base = 3 * span + field * 8 * PLANES
            mine_base = span + field * 8 * PLANES
            out[base : base + 8 * PLANES, :] = mine[mine_base : mine_base + 8 * PLANES, :]
            for source, slot, ok in zip((first, second), slots, valid):
                to = pl.multiple_of(jnp.where(slot > 0, 8 * BRICK, 0), 8)
                into = pl.ds(pl.multiple_of(base + to, 8), 80)
                off = pl.ds(pl.multiple_of(mine_base + 8 * BRICK - to, 8), 80)
                out[into, :] = out[into, :] + source[off, :] * ok
        return
    masks = shift_masks(info, axis)
    for plane in range(PLANES * fields):
        at = slice(span + 8 * plane, span + 8 * plane + 8)
        out[3 * span + 8 * plane : 3 * span + 8 * plane + 8, :] = received(axis, masks, (mine, first, second), at)


def radius_merge_kernel(axis, count, extra, info, mine, first, second, *refs):
    others, out = refs[:extra], refs[extra]
    after_first, valid = arrivals(info, axis)
    span = count * TILES
    out[span : 2 * span, :] = mine[0:span, :]
    slots = (jnp.where(after_first, 2 * span, 0), jnp.where(after_first, 0, 2 * span))
    for source, slot in zip((first, second), slots):
        out[pl.ds(pl.multiple_of(slot, 8), span), :] = source[0:span, :]
    total = mine[span : span + 8, :] + first[span : span + 8, :]
    for other in others:
        total = total + other[...]
    out[3 * span : 3 * span + 8, :] = total


def born_kernel(listed, tiles, own, sums, out, col, acc):
    out[TILES : TILES + 8, :] = sums[...]
    for channel in range(3):
        for tile in range(TILES):
            row = own[4 * channel + tile : 4 * channel + tile + 1, :] * (1.0 / CUTOFF)
            col[channel, tile * LANES : (tile + 1) * LANES, :] = spread(row)

    def block(ib, carry):
        at = pl.ds(pl.multiple_of(ib * BLOCK, BLOCK), BLOCK)
        xi, yi, zi = col[0, at, :], col[1, at, :], col[2, at, :]

        def some(chunk, total):
            for k in range(UNROLL):
                tile = listed[ib, chunk * UNROLL + k]
                dx = xi - tiles[tile, 0:1, :]
                dy = yi - tiles[tile, 1:2, :]
                dz = zi - tiles[tile, 2:3, :]
                u = dx * dx + dy * dy + dz * dz
                s = jnp.maximum(1.0 - u, 0.0)
                e = jnp.exp(u * (-CUTOFF * CUTOFF / 8.0))
                total = total + (e * s) * (s * tiles[tile, 3:4, :])
            return total

        chunks = (listed[ib, LANES - 1] + UNROLL - 1) // UNROLL
        acc[at, :] = lax.fori_loop(0, chunks, some, jnp.zeros((BLOCK, LANES), jnp.float32))
        return carry

    lax.fori_loop(0, BLOCKS, block, 0)
    for tile in range(TILES):
        total = gather_rows(acc[tile * LANES : (tile + 1) * LANES, :]) - own[16 + tile : 17 + tile, :]
        out[tile : tile + 1, :] = own[24 + tile : 25 + tile, :] + total


def gb_kernel(info, listed, tiles, own, own_radius, mine, first, second, out, col, acc, rows):
    for tile in range(TILES):
        at = slice(tile * LANES, (tile + 1) * LANES)
        for channel in range(3):
            row = own[4 * channel + tile : 4 * channel + tile + 1, :] * (1.0 / CUTOFF)
            col[channel, at, :] = spread(row)
        radius = spread(own_radius[tile : tile + 1, :] * (1.0 / CUTOFF))
        col[3, at, :] = radius
        col[4, at, :] = -0.5 / radius
    rows[EMPTY:ROOM] = jnp.ones((ROOM - EMPTY, 2, LANES), jnp.float32)

    after_first, _ = arrivals(info, 2)
    slots = (1, jnp.where(after_first, 2, 0), jnp.where(after_first, 0, 2))
    for source, slot in zip((mine, first, second), slots):
        for cell in range(9):
            radius = source[TILES * cell : TILES * cell + TILES, :] * (1.0 / CUTOFF)
            half = 0.5 / radius
            for tile in range(TILES):
                rows[slot * 36 + 4 * cell + tile, 0:1, :] = radius[tile : tile + 1, :]
                rows[slot * 36 + 4 * cell + tile, 1:2, :] = half[tile : tile + 1, :]

    def block(ib, carry):
        at = pl.ds(pl.multiple_of(ib * BLOCK, BLOCK), BLOCK)
        xi, yi, zi = col[0, at, :], col[1, at, :], col[2, at, :]
        ri, ai = col[3, at, :], col[4, at, :]

        def some(chunk, force):
            fx, fy, fz = force
            for k in range(UNROLL):
                tile = listed[ib, chunk * UNROLL + k]
                dx = xi - tiles[tile, 0:1, :]
                dy = yi - tiles[tile, 1:2, :]
                dz = zi - tiles[tile, 2:3, :]
                u = dx * dx + dy * dy + dz * dz
                s = jnp.maximum(1.0 - u, 0.0)
                e = jnp.exp(u * (ai * rows[tile, 1:2, :]))
                inv = lax.rsqrt(u + (ri * rows[tile, 0:1, :]) * e)
                t = s * inv
                m = (tiles[tile, 4:5, :] * t) * (1.0 + (t * inv) * (0.25 - 0.0625 * e))
                fx = fx + m * dx
                fy = fy + m * dy
                fz = fz + m * dz
            return fx, fy, fz

        chunks = (listed[ib, LANES - 1] + UNROLL - 1) // UNROLL
        zero = jnp.zeros((BLOCK, LANES), jnp.float32)
        force = lax.fori_loop(0, chunks, some, (zero, zero, zero))
        for channel in range(3):
            acc[channel, at, :] = force[channel]
        return carry

    lax.fori_loop(0, BLOCKS, block, 0)
    for channel in range(3):
        for tile in range(TILES):
            total = gather_rows(acc[channel, tile * LANES : (tile + 1) * LANES, :])
            out[4 * channel + tile : 4 * channel + tile + 1, :] = total


def kernel_weights(reach):
    values = [math.exp(-0.5 * (index - reach) ** 2) for index in range(2 * reach + 1)]
    whole = sum(values)
    return [value / whole for value in values]


TAPS = kernel_weights(BLUR_REACH)


def blurred(values):
    rows = values.shape[0]
    near = pltpu.roll(values, 1, 0) + pltpu.roll(values, rows - 1, 0)
    far = pltpu.roll(values, 2, 0) + pltpu.roll(values, rows - 2, 0)
    return TAPS[2] * values + TAPS[1] * near + TAPS[0] * far


def profiles(row, side, base, rows, low, high, slope):
    number = lax.broadcasted_iota(jnp.int32, (rows, LANES), 0) + base
    shift = side * BRICK
    inside = (number >= low) & (number < high)
    window = inside & (number >= shift - SPLAT_MARGIN) & (number < shift + BRICK + SPLAT_MARGIN)
    moved = row + (float(shift) if isinstance(shift, int) else shift.astype(jnp.float32))
    gap = number.astype(jnp.float32) - moved
    plain = jnp.where(window, jnp.exp(-0.5 * gap * gap), 0.0)
    margin = SPLAT_MARGIN + BLUR_REACH
    reached = inside & (number >= shift - margin) & (number < shift + BRICK + margin)
    first = jnp.where(reached, blurred(plain), 0.0)
    if not slope:
        return first
    return first, jnp.where(reached, blurred(gap * plain), 0.0)


def split(values):
    high = values.astype(jnp.bfloat16)
    return high, (values - high.astype(jnp.float32)).astype(jnp.bfloat16)


def splat_kernel(fields, rows, bounds, own, *refs):
    if fields == 2:
        given = refs[0]
    out, px, left_hi, left_lo, right = refs[fields - 1 :]
    out[0:rows, :] = own[0:rows, :]
    for tile in range(TILES):
        lanes = slice(tile * LANES, (tile + 1) * LANES)
        z = profiles(own[8 + tile : 9 + tile, :], 0, -PAD, WIDE, bounds[4], bounds[5], False)
        z_hi, z_lo = split(z)
        right[0:WIDE, lanes] = z_hi
        right[WIDE : 2 * WIDE, lanes] = z_lo
        x = profiles(own[tile : tile + 1, :], 0, -PAD, WIDE, bounds[0], bounds[1], False)
        px[...] = x * own[20 + tile : 21 + tile, :]
        y = profiles(own[4 + tile : 5 + tile, :], 0, -PAD, WIDE, bounds[2], bounds[3], False)
        for plane in range(PLANES):
            at = slice(plane * WIDE, (plane + 1) * WIDE)
            hi, lo = split(px[plane + 3 : plane + 4, :] * y)
            left_hi[at, lanes] = hi
            left_lo[at, lanes] = lo
    weights = right[...]
    dims = (((1,), (1,)), ((), ()))
    placed = lax.dot_general(left_hi[...], weights, dims, preferred_element_type=jnp.float32)
    placed = placed + lax.dot_general(left_lo[...], weights, dims, preferred_element_type=jnp.float32)
    placed = placed[:, 0:WIDE] + placed[:, WIDE : 2 * WIDE]
    placed = placed.reshape(PLANES, 4, 8, WIDE)
    for plane in range(PLANES):
        parts = [placed[plane, k] for k in range(4)]
        out[rows + 8 * plane : rows + 8 * plane + 8, :] = jnp.concatenate(parts, axis=1)
    if fields == 2:
        base = rows + 8 * PLANES
        out[base : base + 8 * PLANES, :] = jnp.zeros((8 * PLANES, LANES), jnp.float32)
        for plane in range(BRICK):
            value = pltpu.roll(given[plane, 0:8, :], WIDE + PAD, 1) + pltpu.roll(given[plane, 8:16, :], 2 * WIDE + PAD, 1)
            out[base + 8 * (plane + 5) : base + 8 * (plane + 6), :] = value


def fit_kernel(scale, parts, bounds, *refs):
    own, evolved, exp_ext, sums = refs[:4]
    gb = refs[4 : 4 + parts]
    moved, force, left, right, inner, px, pxs = refs[4 + parts :]
    squares = jnp.sum(sums[0:1, :], axis=1, keepdims=True)
    cross = jnp.sum(sums[1:2, :], axis=1, keepdims=True)
    target = jnp.sum(sums[2:3, :], axis=1, keepdims=True)
    norm = jnp.sqrt((squares + EPSILON) * (target + EPSILON))
    given_part = 1.0 / norm
    model_part = (cross / norm) / (squares + EPSILON)
    for plane in range(PLANES):
        s = exp_ext[plane] * given_part - evolved[plane] * model_part
        blocks = [s] + [pltpu.roll(s, LANES - WIDE * k, 1) for k in (1, 2, 3)]
        s = jnp.concatenate(blocks, axis=0)
        s = jnp.where(lax.broadcasted_iota(jnp.int32, (WIDE, LANES), 1) < WIDE, s, 0.0)
        hi = s.astype(jnp.bfloat16).astype(jnp.float32)
        lo = (s - hi).astype(jnp.bfloat16).astype(jnp.float32)
        packed = hi + pltpu.roll(lo, WIDE, 1) + pltpu.roll(hi, 2 * WIDE, 1)
        left[plane * WIDE : (plane + 1) * WIDE, :] = packed.astype(jnp.bfloat16)
    moved[3 * TILES :, :] = own[3 * TILES :, :]
    right[...] = jnp.zeros_like(right)
    for tile in range(TILES):
        z, zs = profiles(own[8 + tile : 9 + tile, :], 0, -PAD, WIDE, bounds[4], bounds[5], True)
        for part, values in enumerate((z, zs)):
            lanes = slice(part * LANES, (part + 1) * LANES)
            hi, lo = split(values)
            right[0:WIDE, lanes] = hi
            right[WIDE : 2 * WIDE, lanes] = hi
            right[2 * WIDE : 3 * WIDE, lanes] = lo
        inner[...] = jnp.dot(left[...], right[...], preferred_element_type=jnp.float32)
        x, xs = profiles(own[tile : tile + 1, :], 0, -PAD, WIDE, bounds[0], bounds[1], True)
        y, ys = profiles(own[4 + tile : 5 + tile, :], 0, -PAD, WIDE, bounds[2], bounds[3], True)
        px[...] = x
        pxs[...] = xs
        turned_x = jnp.zeros((WIDE, LANES), jnp.float32)
        plain = turned_x
        turned_z = turned_x
        for plane in range(PLANES):
            rows = slice(plane * WIDE, (plane + 1) * WIDE)
            at_x = px[plane + 3 : plane + 4, :]
            part = inner[rows, 0:LANES]
            turned_x = turned_x + pxs[plane + 3 : plane + 4, :] * part
            plain = plain + at_x * part
            turned_z = turned_z + at_x * inner[rows, LANES : 2 * LANES]
        weight = scale * own[20 + tile : 21 + tile, :]
        charge = -2.0 / (CUTOFF * CUTOFF) * own[12 + tile : 13 + tile, :]
        sides = (turned_x * y, plain * ys, turned_z * y)
        for channel in range(3):
            at = slice(4 * channel + tile, 4 * channel + tile + 1)
            pair = gb[0][at, :]
            for other in gb[1:]:
                pair = pair + other[at, :]
            total = charge * pair + weight * jnp.sum(sides[channel], axis=0, keepdims=True)
            force[at, :] = total
            moved[at, :] = own[at, :] + STEP_SIZE * (own[28 + tile : 29 + tile, :] * total)


def partners(axis):
    count = lax.axis_size(axis)
    even = [(i, i ^ 1) for i in range(count)]
    odd = [(i, (i + 1 if i % 2 else i - 1) % count) for i in range(count)]
    return even, odd


def both_sides(block, axis):
    even, odd = partners(axis)
    return lax.ppermute(block, axis, even), lax.ppermute(block, axis, odd)


def across(block, axis, flip):
    return lax.ppermute(block, axis, [(i, i ^ flip) for i in range(lax.axis_size(axis))])


def f32(*shape):
    return jax.ShapeDtypeStruct(shape, jnp.float32)


def on_device(positions, charges, atom_types, type_table, live_count, exp_map):
    sizes = [lax.axis_size(axis) for axis in AXES]
    places = [lax.axis_index(axis) for axis in AXES]
    info = []
    for size, place in zip(sizes, places):
        info += [-place * BRICK, (size - place) * BRICK]
    for size, place in zip(sizes, places):
        odd = place % 2
        info += [odd, jnp.where(odd == 0, place > 0, place < size - 1).astype(jnp.int32)]
    info = jnp.stack(info).astype(jnp.int32)
    scale = FIT_GAIN * float(BRICK**3 * sizes[0] * sizes[1] * sizes[2])

    atoms, order = call(
        arrange_kernel,
        (f32(32, LANES), f32(TILES, LANES)),
        1 << 22,
        scratch=[pltpu.VMEM((SLOTS, LANES), jnp.float32), pltpu.VMEM((24, LANES), jnp.float32)],
        smem=2,
        n_in=5,
    )(
        type_table,
        live_count.reshape(1),
        positions.reshape(3 * TILES, LANES),
        charges.reshape(TILES, LANES),
        atom_types.reshape(TILES, LANES),
    )
    given = jnp.pad(exp_map, ((0, 0), (0, 0), (0, LANES - BRICK)))
    own = atoms
    for step in range(STEPS):
        fields, rows = (2, 24) if step == 0 else (1, 16)
        planes = 8 * PLANES * fields
        message = call(
            functools.partial(splat_kernel, fields, rows),
            f32(rows + planes, LANES),
            1 << 26,
            scratch=[
                pltpu.VMEM((WIDE, LANES), jnp.float32),
                pltpu.VMEM((PLANES * WIDE, SLOTS), jnp.bfloat16),
                pltpu.VMEM((PLANES * WIDE, SLOTS), jnp.bfloat16),
                pltpu.VMEM((2 * WIDE, SLOTS), jnp.bfloat16),
            ],
            smem=1,
            n_in=1 + fields,
        )(*((info, own, given) if step == 0 else (info, own)))
        for number, axis in enumerate(AXES[:2]):
            count = 3**number
            message = call(
                functools.partial(merge_kernel, number, count, rows, fields),
                f32(3 * count * rows + planes, LANES),
                1 << 20,
                smem=1,
                n_in=4,
            )(info, message, *both_sides(message, axis))
        before = () if step == 0 else (tiles, exp_ext)
        planned = call(
            functools.partial(plan_kernel, rows, fields),
            (jax.ShapeDtypeStruct((BLOCKS, LANES), jnp.int32), f32(ROOM, 8, LANES))
            + (f32(PLANES, 8, LANES),) * fields
            + (f32(8, LANES),),
            1 << 22,
            scratch=[pltpu.VMEM((TILES, LANES, LANES), jnp.float32)],
            smem=1,
            n_in=5 + len(before),
        )(info, own, message, *both_sides(message, AXES[2]), *before)
        if step == 0:
            listed, tiles, evolved, exp_ext, sums = planned
        else:
            listed, tiles, evolved, sums = planned
        if sizes[0] >= 4:
            sums = sums + across(sums, AXES[0], 2)
        radius = call(
            born_kernel,
            f32(TILES + 8, LANES),
            1 << 27,
            scratch=[pltpu.VMEM((3, SLOTS, LANES), jnp.float32), pltpu.VMEM((SLOTS, LANES), jnp.float32)],
            smem=1,
            n_in=4,
        )(listed, tiles, own, sums)
        line = radius
        for number, axis in enumerate(AXES):
            count = 3**number
            span = count * TILES
            flips = (2, 3) if number and sizes[number] >= 4 else ()
            here = line[span:]
            others = [across(here, axis, flip) for flip in flips]
            near = both_sides(line, axis)
            if number == 2:
                sums = here + near[0][span:]
                for other in others:
                    sums = sums + other
                break
            line = call(
                functools.partial(radius_merge_kernel, number, count, len(others)),
                f32(3 * span + 8, LANES),
                1 << 20,
                smem=1,
                n_in=4 + len(others),
            )(info, line, *near, *others)
        pair = call(
            gb_kernel,
            f32(3 * TILES, LANES),
            1 << 28,
            scratch=[
                pltpu.VMEM((5, SLOTS, LANES), jnp.float32),
                pltpu.VMEM((3, SLOTS, LANES), jnp.float32),
                pltpu.VMEM((ROOM, 2, LANES), jnp.float32),
            ],
            smem=2,
            n_in=8,
        )(info, listed, tiles, own, radius, line, *near)
        sums = finished(sums, sizes)
        own, force = call(
            functools.partial(fit_kernel, scale, 1),
            (f32(32, LANES), f32(3 * TILES, LANES)),
            1 << 26,
            scratch=[
                pltpu.VMEM((PLANES * WIDE, LANES), jnp.bfloat16),
                pltpu.VMEM((LANES, 2 * LANES), jnp.bfloat16),
                pltpu.VMEM((PLANES * WIDE, 2 * LANES), jnp.float32),
                pltpu.VMEM((WIDE, LANES), jnp.float32),
                pltpu.VMEM((WIDE, LANES), jnp.float32),
            ],
            smem=1,
            n_in=6,
        )(info, own, evolved, exp_ext, sums, pair)
    results = call(
        restore_kernel,
        f32(6 * TILES, LANES),
        1 << 20,
        scratch=[pltpu.VMEM((24, LANES), jnp.float32)],
        n_in=4,
    )(order, own, atoms, force)
    model = evolved[5 : 5 + BRICK].reshape(BRICK, 8, 4, WIDE).transpose(0, 2, 1, 3).reshape(BRICK, WIDE, WIDE)
    model = model[:, PAD : PAD + BRICK, PAD : PAD + BRICK]
    results = results.reshape((2,) + positions.shape)
    return results[0], results[1], model


def finished(sums, sizes):
    assert sizes[0] in (2, 4) and all(size in (2, 4, 8) for size in sizes)
    far = [axis for axis, size in zip(AXES, sizes) if size == 8]
    if not far:
        return sums
    counts = [lax.axis_size(axis) for axis in far]
    total = sums
    for choice in range(1, 1 << len(far)):
        flips = [4 if choice >> k & 1 else 0 for k in range(len(far))]
        pairs = []
        for source in range(math.prod(counts)):
            target, rest, unit = 0, source, 1
            for count, flip in reversed(list(zip(counts, flips))):
                target += (rest % count ^ flip) * unit
                rest //= count
                unit *= count
            pairs.append((source, target))
        total = total + lax.ppermute(sums, tuple(far), pairs)
    return total


def solution(mesh):
    placed = (
        P(None, *AXES, None),
        P(*AXES, None),
        P(*AXES, None),
        P(),
        P(*AXES),
        P(*AXES),
    )
    return jax.shard_map(
        on_device,
        mesh=mesh,
        in_specs=placed,
        out_specs=(placed[0], placed[0], P(*AXES)),
        check_vma=False,
    )
```

```python
import functools
import math

import jax
import jax.numpy as jnp
from jax import lax
from jax.experimental import pallas as pl
from jax.experimental.pallas import tpu as pltpu
from jax.sharding import PartitionSpec as P

SPLAT_MARGIN = 3
BLUR_REACH = 2
STEPS = 2
CUTOFF = 10.0
EPSILON = 1e-06
STEP_SIZE = 1.0
FIT_GAIN = 0.2

AXES = ("gx", "gy", "gz")
SLOTS = 512
LANES = 128
TILES = SLOTS // LANES
BRICK = 16
PLANES = 26
HALF = PLANES // 2
EDGE = 10
PAD = 8
WIDE = 32
INTERPRET = False


def call(kernel, out_shape, cost, scratch=(), smem=0, n_in=0, vmem=48):
    specs = [pl.BlockSpec(memory_space=pltpu.SMEM)] * smem
    specs += [pl.BlockSpec(memory_space=pltpu.VMEM)] * (n_in - smem)
    many = isinstance(out_shape, (tuple, list))
    out_spec = pl.BlockSpec(memory_space=pltpu.VMEM)
    return pl.pallas_call(
        kernel,
        out_shape=out_shape,
        in_specs=specs,
        out_specs=[out_spec] * len(out_shape) if many else out_spec,
        scratch_shapes=list(scratch),
        cost_estimate=pl.CostEstimate(flops=cost, bytes_accessed=1 << 18, transcendentals=0),
        compiler_params=pltpu.CompilerParams(vmem_limit_bytes=vmem << 20),
        interpret=INTERPRET,
    )


def spread(row):
    return jnp.transpose(jnp.broadcast_to(row, (LANES, LANES)))


def gather_rows(acc):
    return jnp.sum(jnp.transpose(acc), axis=0, keepdims=True)


BLOCK = 32
BLOCKS = SLOTS // BLOCK
UNROLL = 8
CELLS = 27
EMPTY = CELLS * TILES
ROOM = EMPTY + 4
FAR = 1e9


def three_parts(values):
    high = values.astype(jnp.bfloat16)
    rest = values - high.astype(jnp.float32)
    middle = rest.astype(jnp.bfloat16)
    return high, middle, (rest - middle.astype(jnp.float32)).astype(jnp.bfloat16)


def arrange_kernel(table, live_count, pos, charges, types, out, order, col, left):
    count = live_count[0]
    slot = lax.broadcasted_iota(jnp.int32, (TILES, LANES), 0) * LANES
    slot = slot + lax.broadcasted_iota(jnp.int32, (TILES, LANES), 1)
    living = slot < count
    alive = jnp.where(living, 1.0, 0.0)
    kinds = types[...]
    props = []
    for row in range(3):
        value = jnp.zeros((TILES, LANES), jnp.float32)
        for kind in range(table.shape[1]):
            value = jnp.where(kinds == kind, table[row, kind], value)
        props.append(value)
    group = jnp.zeros((TILES, LANES), jnp.float32)
    sub = lax.broadcasted_iota(jnp.int32, (SLOTS, LANES), 0)
    lane = lax.broadcasted_iota(jnp.int32, (SLOTS, LANES), 1)
    for dim, size in ((0, 256), (1, 128), (2, 64), (0, 32)):
        key = group * 64.0 + jnp.where(living, pos[4 * dim : 4 * dim + 4, :], 40.0)
        for tile in range(TILES):
            col[tile * LANES : (tile + 1) * LANES, :] = spread(key[tile : tile + 1, :])
        ranks = []
        for tile in range(TILES):
            row = key[tile : tile + 1, :]
            other = col[...]
            ahead = (other < row) | ((other == row) & (sub < lane + tile * LANES))
            ranks.append(jnp.sum(jnp.where(ahead, 1.0, 0.0), axis=0, keepdims=True))
        rank = jnp.concatenate(ranks, axis=0)
        group = jnp.floor(rank * (1.0 / size))
    order[...] = rank
    values = [pos[0:4, :], pos[4:8, :], pos[8:12, :], charges[...] * alive]
    values += [props[1] * alive, props[2] * alive, props[0], alive]
    total = jnp.zeros((3 * len(values), SLOTS), jnp.float32)
    for tile in range(TILES):
        block = jnp.concatenate([value[tile : tile + 1, :] for value in values], axis=0)
        for part, piece in enumerate(three_parts(block)):
            left[8 * part : 8 * part + 8, :] = piece.astype(jnp.float32)
        hot = jnp.where(rank[tile : tile + 1, :] == sub.astype(jnp.float32), 1.0, 0.0).astype(jnp.bfloat16)
        dims = (((1,), (1,)), ((), ()))
        total = total + lax.dot_general(left[...].astype(jnp.bfloat16), hot, dims, preferred_element_type=jnp.float32)
    total = total[0:8] + total[8:16] + total[16:24]
    for channel in range(8):
        for tile in range(TILES):
            at = slice(4 * channel + tile, 4 * channel + tile + 1)
            out[at, :] = total[channel : channel + 1, tile * LANES : (tile + 1) * LANES]


def restore_kernel(order, moved, start, force, out, left):
    values = [moved[4 * d : 4 * d + 4, :] - start[4 * d : 4 * d + 4, :] for d in range(3)]
    values += [force[4 * d : 4 * d + 4, :] for d in range(3)]
    values += [jnp.zeros((TILES, LANES), jnp.float32)] * 2
    sub = lax.broadcasted_iota(jnp.int32, (LANES, LANES), 0).astype(jnp.float32)
    totals = [jnp.zeros((24, LANES), jnp.float32) for _ in range(TILES)]
    for source in range(TILES):
        block = jnp.concatenate([value[source : source + 1, :] for value in values], axis=0)
        for part, piece in enumerate(three_parts(block)):
            left[8 * part : 8 * part + 8, :] = piece.astype(jnp.float32)
        parts = left[...].astype(jnp.bfloat16)
        for tile in range(TILES):
            hot = jnp.where(order[tile : tile + 1, :] == sub + float(source * LANES), 1.0, 0.0)
            totals[tile] = totals[tile] + jnp.dot(parts, hot.astype(jnp.bfloat16), preferred_element_type=jnp.float32)
    for tile in range(TILES):
        total = totals[tile][0:8] + totals[tile][8:16] + totals[tile][16:24]
        for channel in range(6):
            at = slice(4 * channel + tile, 4 * channel + tile + 1)
            out[at, :] = total[channel : channel + 1, :]


def plan_kernel(rows, fields, *refs):
    info, own, field = refs[:3]
    sources = refs[3:6]
    if fields == 2:
        known = ()
        listed, tiles, evolved, given, sums, active = refs[6:]
    else:
        known = refs[6:7]
        given = refs[7]
        listed, tiles, evolved, sums, active = refs[8:]
    low, high = [], []
    for dim in range(3):
        living = own[28:32, :] > 0.0
        value = own[4 * dim : 4 * dim + 4, :]
        lo, hi = jnp.where(living, value, FAR), jnp.where(living, value, -FAR)
        for step in (1, 2, 4, 8, 16):
            lo = jnp.minimum(lo, pltpu.roll(lo, LANES - step, 1))
            hi = jnp.maximum(hi, pltpu.roll(hi, LANES - step, 1))
        low.append(lo)
        high.append(hi)
    active[...] = jnp.zeros_like(active)
    tiles[EMPTY:ROOM] = jnp.zeros((ROOM - EMPTY, 8, LANES), jnp.float32)
    after_first, valid = arrivals(info, 2)
    slots = (1, jnp.where(after_first, 2, 0), jnp.where(after_first, 0, 2))
    for source, slot, ok in zip(sources, slots, (None,) + valid):

        for cell in range(9):
            number = slot * 9 + cell
            sides = (cell % 3 - 1, cell // 3 - 1, slot - 1)
            block = source[cell * rows : cell * rows + rows, :]
            if ok is not None:
                block = block * ok
            if known:
                charge = [known[0][4 * number + tile, 4:5, :] for tile in range(TILES)]
                screen = [known[0][4 * number + tile, 3:4, :] for tile in range(TILES)]
                living = jnp.concatenate(screen, axis=0) > 0.0
            else:
                charge = [block[12 + tile : 13 + tile] for tile in range(TILES)]
                screen = [block[16 + tile : 17 + tile] for tile in range(TILES)]
                living = block[16:20] > 0.0
            near_low, near_high = [], []
            for dim in range(3):
                side = sides[dim]
                shift = float(side * BRICK) if isinstance(side, int) else side.astype(jnp.float32) * float(BRICK)
                moved = block[4 * dim : 4 * dim + 4] + shift
                near_low.append(jnp.min(jnp.where(living, moved, FAR), axis=1, keepdims=True))
                near_high.append(jnp.max(jnp.where(living, moved, -FAR), axis=1, keepdims=True))
                scaled = moved * (1.0 / CUTOFF)
                for tile in range(TILES):
                    tiles[4 * number + tile, dim : dim + 1, :] = scaled[tile : tile + 1, :]
            for tile in range(TILES):
                tiles[4 * number + tile, 3:4, :] = screen[tile]
                tiles[4 * number + tile, 4:5, :] = charge[tile]
            for tile in range(TILES):
                apart = jnp.zeros((TILES, LANES), jnp.float32)
                for dim in range(3):
                    lo, hi = low[dim][tile : tile + 1, :], high[dim][tile : tile + 1, :]
                    gap = jnp.maximum(jnp.maximum(near_low[dim] - hi, lo - near_high[dim]), 0.0)
                    apart = apart + gap * gap
                near = jnp.where(apart < CUTOFF * CUTOFF * 1.0001, 1.0, 0.0)
                active[tile, pl.ds(pl.multiple_of(4 * number, TILES), TILES), :] = near
    row = lax.broadcasted_iota(jnp.int32, (LANES, LANES), 0)
    lane = lax.broadcasted_iota(jnp.int32, (LANES, LANES), 1)
    before = jnp.where(lane < row, 1.0, 0.0).astype(jnp.bfloat16)
    for tile in range(TILES):
        flags = active[tile]
        ranks = jnp.dot(before, flags.astype(jnp.bfloat16), preferred_element_type=jnp.float32)
        for part in range(LANES // BLOCK):
            at = slice(part * BLOCK, part * BLOCK + 1)
            chosen = jnp.broadcast_to(flags[:, at], (LANES, LANES)) > 0.0
            place = jnp.broadcast_to(ranks[:, at], (LANES, LANES)).astype(jnp.int32)
            total = jnp.sum(jnp.where(chosen, 1, 0), axis=0, keepdims=True)
            entry = jnp.sum(jnp.where(chosen & (place == lane), row, 0), axis=0, keepdims=True)
            spot = lane[0:1, :]
            entry = jnp.where(spot < total, entry, EMPTY)
            block = tile * (LANES // BLOCK) + part
            listed[block : block + 1, :] = jnp.where(spot == LANES - 1, total, entry)
    lane = lax.broadcasted_iota(jnp.int32, (8, LANES), 1)
    sub = lane & (WIDE - 1)
    own_points = (lane >= WIDE) & (lane < 3 * WIDE) & (sub >= PAD) & (sub < PAD + BRICK)
    squares = jnp.zeros((8, LANES), jnp.float32)
    cross = squares
    target = squares
    adds = shift_masks(info, 2)
    evolved[...] = field[0 : 8 * PLANES, :].reshape(PLANES, 8, LANES)
    take_shares(2, adds, sources[1:], 9 * rows, evolved, 0)
    if fields == 2:
        given[...] = field[8 * PLANES : 16 * PLANES, :].reshape(PLANES, 8, LANES)
        take_shares(2, adds, sources[1:], 9 * rows + 8 * HALF, given, 0)
    for plane in range(PLANES):
        value = evolved[plane]
        if 5 <= plane < 5 + BRICK:
            value = jnp.where(own_points, value, 0.0)
            wanted = jnp.where(own_points, given[plane], 0.0)
            squares = squares + value * value
            cross = cross + value * wanted
            target = target + wanted * wanted
    sums[...] = jnp.zeros_like(sums)
    sums[0:1, :] = jnp.sum(squares, axis=0, keepdims=True)
    sums[1:2, :] = jnp.sum(cross, axis=0, keepdims=True)
    sums[2:3, :] = jnp.sum(target, axis=0, keepdims=True)


def arrivals(info, axis):
    after_first = info[6 + 2 * axis] == 0
    return after_first, (1.0, jnp.where(info[7 + 2 * axis] > 0, 1.0, 0.0))


def upper_half(axis):
    lane = lax.broadcasted_iota(jnp.int32, (8, LANES), 1)
    return (lane >= 64) if axis == 1 else ((lane & (WIDE - 1)) >= BRICK)


def shift_masks(info, axis):
    upper = upper_half(axis)
    after_first, valid = arrivals(info, axis)
    after_one = jnp.where(after_first, 1.0, 0.0)
    masks = []
    for after, ok in zip((after_one, 1.0 - after_one), valid):
        masks.append((jnp.where(upper, after * ok, 0.0), jnp.where(upper, 0.0, (1.0 - after) * ok)))
    return masks


def half_steps(axis):
    return (64, 64) if axis == 1 else (BRICK, LANES - BRICK)


def take_shares(axis, masks, sources, base, into, first):
    up, down = half_steps(axis)
    for plane in range(HALF):
        at = slice(base + 8 * plane, base + 8 * plane + 8)
        low = into[first + plane]
        high = into[first + HALF + plane]
        for (from_after, from_before), source in zip(masks, sources):
            share = source[at, :]
            low = low + pltpu.roll(share, up, 1) * from_after + share * from_before
            high = high + share * from_after + pltpu.roll(share, down, 1) * from_before
        into[first + plane] = low
        into[first + HALF + plane] = high


def give_shares(info, axis, field, first, outs, base):
    up, down = half_steps(axis)
    upper = upper_half(axis)
    after_first, _ = arrivals(info, axis)
    for plane in range(HALF):
        low, high = field[first + plane], field[first + HALF + plane]
        after = jnp.where(upper, high, pltpu.roll(low, down, 1))
        before = jnp.where(upper, pltpu.roll(high, up, 1), low)
        at = slice(base + 8 * plane, base + 8 * plane + 8)
        outs[0][at, :] = jnp.where(after_first, after, before)
        outs[1][at, :] = jnp.where(after_first, before, after)


def merge_kernel(axis, count, rows, fields, info, field, mine, first, second, merged, out_first, out_second):
    after_first, valid = arrivals(info, axis)
    span = count * rows
    slots = (jnp.where(after_first, 2 * span, 0), jnp.where(after_first, 0, 2 * span))
    for out in (out_first, out_second):
        out[span : 2 * span, :] = mine[0:span, :]
        for source, slot, ok in zip((first, second), slots, valid):
            out[pl.ds(pl.multiple_of(slot, 8), span), :] = source[0:span, :] * ok
    merged[...] = field[...].reshape(fields * PLANES, 8, LANES)
    for number in range(fields):
        if axis == 0:
            for source, slot, ok in zip((first, second), slots, valid):
                into = pl.ds(number * PLANES + jnp.where(slot > 0, BRICK, 0), EDGE)
                at = slice(span + 8 * EDGE * number, span + 8 * EDGE * (number + 1))
                merged[into] = merged[into] + source[at, :].reshape(EDGE, 8, LANES) * ok
        else:
            base = span + 8 * HALF * number
            take_shares(axis, shift_masks(info, axis), (first, second), base, merged, number * PLANES)
        base = 3 * span + 8 * HALF * number
        give_shares(info, axis + 1, merged, number * PLANES, (out_first, out_second), base)


def radius_merge_kernel(axis, count, extra, info, mine, first, second, *refs):
    others, out = refs[:extra], refs[extra]
    after_first, valid = arrivals(info, axis)
    span = count * TILES
    out[span : 2 * span, :] = mine[0:span, :]
    slots = (jnp.where(after_first, 2 * span, 0), jnp.where(after_first, 0, 2 * span))
    for source, slot in zip((first, second), slots):
        out[pl.ds(pl.multiple_of(slot, 8), span), :] = source[0:span, :]
    total = mine[span : span + 8, :] + first[span : span + 8, :]
    for other in others:
        total = total + other[...]
    out[3 * span : 3 * span + 8, :] = total


def born_kernel(listed, tiles, own, sums, out, col, acc):
    out[TILES : TILES + 8, :] = sums[...]
    for channel in range(3):
        for tile in range(TILES):
            row = own[4 * channel + tile : 4 * channel + tile + 1, :] * (1.0 / CUTOFF)
            col[channel, tile * LANES : (tile + 1) * LANES, :] = spread(row)

    def block(ib, carry):
        at = pl.ds(pl.multiple_of(ib * BLOCK, BLOCK), BLOCK)
        xi, yi, zi = col[0, at, :], col[1, at, :], col[2, at, :]

        def some(chunk, total):
            for k in range(UNROLL):
                tile = listed[ib, chunk * UNROLL + k]
                dx = xi - tiles[tile, 0:1, :]
                dy = yi - tiles[tile, 1:2, :]
                dz = zi - tiles[tile, 2:3, :]
                u = dx * dx + dy * dy + dz * dz
                s = jnp.maximum(1.0 - u, 0.0)
                e = jnp.exp(u * (-CUTOFF * CUTOFF / 8.0))
                total = total + (e * s) * (s * tiles[tile, 3:4, :])
            return total

        chunks = (listed[ib, LANES - 1] + UNROLL - 1) // UNROLL
        acc[at, :] = lax.fori_loop(0, chunks, some, jnp.zeros((BLOCK, LANES), jnp.float32))
        return carry

    lax.fori_loop(0, BLOCKS, block, 0)
    for tile in range(TILES):
        total = gather_rows(acc[tile * LANES : (tile + 1) * LANES, :]) - own[16 + tile : 17 + tile, :]
        out[tile : tile + 1, :] = own[24 + tile : 25 + tile, :] + total


def gb_kernel(info, listed, tiles, own, own_radius, mine, first, second, out, col, acc, rows):
    for tile in range(TILES):
        at = slice(tile * LANES, (tile + 1) * LANES)
        for channel in range(3):
            row = own[4 * channel + tile : 4 * channel + tile + 1, :] * (1.0 / CUTOFF)
            col[channel, at, :] = spread(row)
        radius = spread(own_radius[tile : tile + 1, :] * (1.0 / CUTOFF))
        col[3, at, :] = radius
        col[4, at, :] = -0.5 / radius
    rows[EMPTY:ROOM] = jnp.ones((ROOM - EMPTY, 2, LANES), jnp.float32)

    after_first, _ = arrivals(info, 2)
    slots = (1, jnp.where(after_first, 2, 0), jnp.where(after_first, 0, 2))
    for source, slot in zip((mine, first, second), slots):
        for cell in range(9):
            radius = source[TILES * cell : TILES * cell + TILES, :] * (1.0 / CUTOFF)
            half = 0.5 / radius
            for tile in range(TILES):
                rows[slot * 36 + 4 * cell + tile, 0:1, :] = radius[tile : tile + 1, :]
                rows[slot * 36 + 4 * cell + tile, 1:2, :] = half[tile : tile + 1, :]

    def block(ib, carry):
        at = pl.ds(pl.multiple_of(ib * BLOCK, BLOCK), BLOCK)
        xi, yi, zi = col[0, at, :], col[1, at, :], col[2, at, :]
        ri, ai = col[3, at, :], col[4, at, :]

        def some(chunk, force):
            fx, fy, fz = force
            for k in range(UNROLL):
                tile = listed[ib, chunk * UNROLL + k]
                dx = xi - tiles[tile, 0:1, :]
                dy = yi - tiles[tile, 1:2, :]
                dz = zi - tiles[tile, 2:3, :]
                u = dx * dx + dy * dy + dz * dz
                s = jnp.maximum(1.0 - u, 0.0)
                e = jnp.exp(u * (ai * rows[tile, 1:2, :]))
                inv = lax.rsqrt(u + (ri * rows[tile, 0:1, :]) * e)
                t = s * inv
                m = (tiles[tile, 4:5, :] * t) * (1.0 + (t * inv) * (0.25 - 0.0625 * e))
                fx = fx + m * dx
                fy = fy + m * dy
                fz = fz + m * dz
            return fx, fy, fz

        chunks = (listed[ib, LANES - 1] + UNROLL - 1) // UNROLL
        zero = jnp.zeros((BLOCK, LANES), jnp.float32)
        force = lax.fori_loop(0, chunks, some, (zero, zero, zero))
        for channel in range(3):
            acc[channel, at, :] = force[channel]
        return carry

    lax.fori_loop(0, BLOCKS, block, 0)
    for channel in range(3):
        for tile in range(TILES):
            total = gather_rows(acc[channel, tile * LANES : (tile + 1) * LANES, :])
            out[4 * channel + tile : 4 * channel + tile + 1, :] = total


def kernel_weights(reach):
    values = [math.exp(-0.5 * (index - reach) ** 2) for index in range(2 * reach + 1)]
    whole = sum(values)
    return [value / whole for value in values]


TAPS = kernel_weights(BLUR_REACH)


def blurred(values):
    rows = values.shape[0]
    near = pltpu.roll(values, 1, 0) + pltpu.roll(values, rows - 1, 0)
    far = pltpu.roll(values, 2, 0) + pltpu.roll(values, rows - 2, 0)
    return TAPS[2] * values + TAPS[1] * near + TAPS[0] * far


def profiles(row, side, base, rows, low, high, slope):
    number = lax.broadcasted_iota(jnp.int32, (rows, LANES), 0) + base
    shift = side * BRICK
    inside = (number >= low) & (number < high)
    window = inside & (number >= shift - SPLAT_MARGIN) & (number < shift + BRICK + SPLAT_MARGIN)
    moved = row + (float(shift) if isinstance(shift, int) else shift.astype(jnp.float32))
    gap = number.astype(jnp.float32) - moved
    plain = jnp.where(window, jnp.exp(-0.5 * gap * gap), 0.0)
    margin = SPLAT_MARGIN + BLUR_REACH
    reached = inside & (number >= shift - margin) & (number < shift + BRICK + margin)
    first = jnp.where(reached, blurred(plain), 0.0)
    if not slope:
        return first
    return first, jnp.where(reached, blurred(gap * plain), 0.0)


def split(values):
    high = values.astype(jnp.bfloat16)
    return high, (values - high.astype(jnp.float32)).astype(jnp.bfloat16)


def splat_kernel(fields, rows, bounds, own, *refs):
    if fields == 2:
        given = refs[0]
    field, out_first, out_second, px, left_hi, left_lo, right = refs[fields - 1 :]
    for tile in range(TILES):
        lanes = slice(tile * LANES, (tile + 1) * LANES)
        z = profiles(own[8 + tile : 9 + tile, :], 0, -PAD, WIDE, bounds[4], bounds[5], False)
        z_hi, z_lo = split(z)
        right[0:WIDE, lanes] = z_hi
        right[WIDE : 2 * WIDE, lanes] = z_lo
        x = profiles(own[tile : tile + 1, :], 0, -PAD, WIDE, bounds[0], bounds[1], False)
        px[...] = x * own[20 + tile : 21 + tile, :]
        y = profiles(own[4 + tile : 5 + tile, :], 0, -PAD, WIDE, bounds[2], bounds[3], False)
        for plane in range(PLANES):
            at = slice(plane * WIDE, (plane + 1) * WIDE)
            hi, lo = split(px[plane + 3 : plane + 4, :] * y)
            left_hi[at, lanes] = hi
            left_lo[at, lanes] = lo
    weights = right[...]
    dims = (((1,), (1,)), ((), ()))
    placed = lax.dot_general(left_hi[...], weights, dims, preferred_element_type=jnp.float32)
    placed = placed + lax.dot_general(left_lo[...], weights, dims, preferred_element_type=jnp.float32)
    placed = placed[:, 0:WIDE] + placed[:, WIDE : 2 * WIDE]
    placed = placed.reshape(PLANES, 4, 8, WIDE)
    for plane in range(PLANES):
        parts = [placed[plane, k] for k in range(4)]
        field[8 * plane : 8 * plane + 8, :] = jnp.concatenate(parts, axis=1)
    if fields == 2:
        base = 8 * PLANES
        field[base : base + 8 * PLANES, :] = jnp.zeros((8 * PLANES, LANES), jnp.float32)
        for plane in range(BRICK):
            value = pltpu.roll(given[plane, 0:8, :], WIDE + PAD, 1) + pltpu.roll(given[plane, 8:16, :], 2 * WIDE + PAD, 1)
            field[base + 8 * (plane + 5) : base + 8 * (plane + 6), :] = value
    after_first, _ = arrivals(bounds, 0)
    starts = (jnp.where(after_first, 8 * BRICK, 0), jnp.where(after_first, 0, 8 * BRICK))
    for out, start in zip((out_first, out_second), starts):
        out[0:rows, :] = own[0:rows, :]
        for number in range(fields):
            off = pl.ds(pl.multiple_of(8 * PLANES * number + start, 8), 8 * EDGE)
            out[rows + 8 * EDGE * number : rows + 8 * EDGE * (number + 1), :] = field[off, :]


def fit_kernel(scale, parts, bounds, *refs):
    own, evolved, exp_ext, sums = refs[:4]
    gb = refs[4 : 4 + parts]
    moved, force, left, right, inner, px, pxs = refs[4 + parts :]
    squares = jnp.sum(sums[0:1, :], axis=1, keepdims=True)
    cross = jnp.sum(sums[1:2, :], axis=1, keepdims=True)
    target = jnp.sum(sums[2:3, :], axis=1, keepdims=True)
    norm = jnp.sqrt((squares + EPSILON) * (target + EPSILON))
    given_part = 1.0 / norm
    model_part = (cross / norm) / (squares + EPSILON)
    for plane in range(PLANES):
        s = exp_ext[plane] * given_part - evolved[plane] * model_part
        blocks = [s] + [pltpu.roll(s, LANES - WIDE * k, 1) for k in (1, 2, 3)]
        s = jnp.concatenate(blocks, axis=0)
        s = jnp.where(lax.broadcasted_iota(jnp.int32, (WIDE, LANES), 1) < WIDE, s, 0.0)
        hi = s.astype(jnp.bfloat16).astype(jnp.float32)
        lo = (s - hi).astype(jnp.bfloat16).astype(jnp.float32)
        packed = hi + pltpu.roll(lo, WIDE, 1) + pltpu.roll(hi, 2 * WIDE, 1)
        left[plane * WIDE : (plane + 1) * WIDE, :] = packed.astype(jnp.bfloat16)
    moved[3 * TILES :, :] = own[3 * TILES :, :]
    right[...] = jnp.zeros_like(right)
    for tile in range(TILES):
        z, zs = profiles(own[8 + tile : 9 + tile, :], 0, -PAD, WIDE, bounds[4], bounds[5], True)
        for part, values in enumerate((z, zs)):
            lanes = slice(part * LANES, (part + 1) * LANES)
            hi, lo = split(values)
            right[0:WIDE, lanes] = hi
            right[WIDE : 2 * WIDE, lanes] = hi
            right[2 * WIDE : 3 * WIDE, lanes] = lo
        inner[...] = jnp.dot(left[...], right[...], preferred_element_type=jnp.float32)
        x, xs = profiles(own[tile : tile + 1, :], 0, -PAD, WIDE, bounds[0], bounds[1], True)
        y, ys = profiles(own[4 + tile : 5 + tile, :], 0, -PAD, WIDE, bounds[2], bounds[3], True)
        px[...] = x
        pxs[...] = xs
        turned_x = jnp.zeros((WIDE, LANES), jnp.float32)
        plain = turned_x
        turned_z = turned_x
        for plane in range(PLANES):
            rows = slice(plane * WIDE, (plane + 1) * WIDE)
            at_x = px[plane + 3 : plane + 4, :]
            part = inner[rows, 0:LANES]
            turned_x = turned_x + pxs[plane + 3 : plane + 4, :] * part
            plain = plain + at_x * part
            turned_z = turned_z + at_x * inner[rows, LANES : 2 * LANES]
        weight = scale * own[20 + tile : 21 + tile, :]
        charge = -2.0 / (CUTOFF * CUTOFF) * own[12 + tile : 13 + tile, :]
        sides = (turned_x * y, plain * ys, turned_z * y)
        for channel in range(3):
            at = slice(4 * channel + tile, 4 * channel + tile + 1)
            pair = gb[0][at, :]
            for other in gb[1:]:
                pair = pair + other[at, :]
            total = charge * pair + weight * jnp.sum(sides[channel], axis=0, keepdims=True)
            force[at, :] = total
            moved[at, :] = own[at, :] + STEP_SIZE * (own[28 + tile : 29 + tile, :] * total)


def partners(axis):
    count = lax.axis_size(axis)
    even = [(i, i ^ 1) for i in range(count)]
    odd = [(i, (i + 1 if i % 2 else i - 1) % count) for i in range(count)]
    return even, odd


def both_sides(blocks, axis):
    even, odd = partners(axis)
    return lax.ppermute(blocks[0], axis, even), lax.ppermute(blocks[1], axis, odd)


def across(block, axis, flip):
    return lax.ppermute(block, axis, [(i, i ^ flip) for i in range(lax.axis_size(axis))])


def f32(*shape):
    return jax.ShapeDtypeStruct(shape, jnp.float32)


def on_device(positions, charges, atom_types, type_table, live_count, exp_map):
    sizes = [lax.axis_size(axis) for axis in AXES]
    places = [lax.axis_index(axis) for axis in AXES]
    info = []
    for size, place in zip(sizes, places):
        info += [-place * BRICK, (size - place) * BRICK]
    for size, place in zip(sizes, places):
        odd = place % 2
        info += [odd, jnp.where(odd == 0, place > 0, place < size - 1).astype(jnp.int32)]
    info = jnp.stack(info).astype(jnp.int32)
    scale = FIT_GAIN * float(BRICK**3 * sizes[0] * sizes[1] * sizes[2])

    atoms, order = call(
        arrange_kernel,
        (f32(32, LANES), f32(TILES, LANES)),
        1 << 22,
        scratch=[pltpu.VMEM((SLOTS, LANES), jnp.float32), pltpu.VMEM((24, LANES), jnp.float32)],
        smem=2,
        n_in=5,
    )(
        type_table,
        live_count.reshape(1),
        positions.reshape(3 * TILES, LANES),
        charges.reshape(TILES, LANES),
        atom_types.reshape(TILES, LANES),
    )
    given = jnp.pad(exp_map, ((0, 0), (0, 0), (0, LANES - BRICK)))
    own = atoms
    for step in range(STEPS):
        fields, rows = (2, 24) if step == 0 else (1, 16)
        planes = 8 * PLANES * fields
        field, *mine = call(
            functools.partial(splat_kernel, fields, rows),
            (f32(planes, LANES),) + (f32(rows + 8 * EDGE * fields, LANES),) * 2,
            1 << 26,
            scratch=[
                pltpu.VMEM((WIDE, LANES), jnp.float32),
                pltpu.VMEM((PLANES * WIDE, SLOTS), jnp.bfloat16),
                pltpu.VMEM((PLANES * WIDE, SLOTS), jnp.bfloat16),
                pltpu.VMEM((2 * WIDE, SLOTS), jnp.bfloat16),
            ],
            smem=1,
            n_in=1 + fields,
        )(*((info, own, given) if step == 0 else (info, own)))
        for number, axis in enumerate(AXES[:2]):
            count = 3**number
            field, *mine = call(
                functools.partial(merge_kernel, number, count, rows, fields),
                (f32(fields * PLANES, 8, LANES),) + (f32(3 * count * rows + 8 * HALF * fields, LANES),) * 2,
                1 << 20,
                smem=1,
                n_in=5,
            )(info, field.reshape(planes, LANES), mine[0], *both_sides(mine, axis))
        before = () if step == 0 else (tiles, exp_ext)
        planned = call(
            functools.partial(plan_kernel, rows, fields),
            (jax.ShapeDtypeStruct((BLOCKS, LANES), jnp.int32), f32(ROOM, 8, LANES))
            + (f32(PLANES, 8, LANES),) * fields
            + (f32(8, LANES),),
            1 << 22,
            scratch=[pltpu.VMEM((TILES, LANES, LANES), jnp.float32)],
            smem=1,
            n_in=6 + len(before),
        )(info, own, field.reshape(planes, LANES), mine[0], *both_sides(mine, AXES[2]), *before)
        if step == 0:
            listed, tiles, evolved, exp_ext, sums = planned
        else:
            listed, tiles, evolved, sums = planned
        far = [across(sums, AXES[0], flip) for flip in (2, 3)] if sizes[0] >= 4 else []
        radius = call(
            born_kernel,
            f32(TILES + 8, LANES),
            1 << 27,
            scratch=[pltpu.VMEM((3, SLOTS, LANES), jnp.float32), pltpu.VMEM((SLOTS, LANES), jnp.float32)],
            smem=1,
            n_in=4,
        )(listed, tiles, own, sums)
        line = radius
        for number, axis in enumerate(AXES):
            count = 3**number
            span = count * TILES
            flips = (2, 3) if number and sizes[number] >= 4 else ()
            here = line[span:]
            others = [across(here, axis, flip) for flip in flips] if number else far
            near = both_sides((line, line), axis)
            if number == 2:
                sums = here + near[0][span:]
                for other in others:
                    sums = sums + other
                break
            line = call(
                functools.partial(radius_merge_kernel, number, count, len(others)),
                f32(3 * span + 8, LANES),
                1 << 20,
                smem=1,
                n_in=4 + len(others),
            )(info, line, *near, *others)
        pair = call(
            gb_kernel,
            f32(3 * TILES, LANES),
            1 << 28,
            scratch=[
                pltpu.VMEM((5, SLOTS, LANES), jnp.float32),
                pltpu.VMEM((3, SLOTS, LANES), jnp.float32),
                pltpu.VMEM((ROOM, 2, LANES), jnp.float32),
            ],
            smem=2,
            n_in=8,
        )(info, listed, tiles, own, radius, line, *near)
        sums = finished(sums, sizes)
        own, force = call(
            functools.partial(fit_kernel, scale, 1),
            (f32(32, LANES), f32(3 * TILES, LANES)),
            1 << 26,
            scratch=[
                pltpu.VMEM((PLANES * WIDE, LANES), jnp.bfloat16),
                pltpu.VMEM((LANES, 2 * LANES), jnp.bfloat16),
                pltpu.VMEM((PLANES * WIDE, 2 * LANES), jnp.float32),
                pltpu.VMEM((WIDE, LANES), jnp.float32),
                pltpu.VMEM((WIDE, LANES), jnp.float32),
            ],
            smem=1,
            n_in=6,
        )(info, own, evolved, exp_ext, sums, pair)
    results = call(
        restore_kernel,
        f32(6 * TILES, LANES),
        1 << 20,
        scratch=[pltpu.VMEM((24, LANES), jnp.float32)],
        n_in=4,
    )(order, own, atoms, force)
    model = evolved[5 : 5 + BRICK].reshape(BRICK, 8, 4, WIDE).transpose(0, 2, 1, 3).reshape(BRICK, WIDE, WIDE)
    model = model[:, PAD : PAD + BRICK, PAD : PAD + BRICK]
    results = results.reshape((2,) + positions.shape)
    return results[0], results[1], model


def finished(sums, sizes):
    assert sizes[0] in (2, 4) and all(size in (2, 4, 8) for size in sizes)
    far = [axis for axis, size in zip(AXES, sizes) if size == 8]
    if not far:
        return sums
    counts = [lax.axis_size(axis) for axis in far]
    total = sums
    for choice in range(1, 1 << len(far)):
        flips = [4 if choice >> k & 1 else 0 for k in range(len(far))]
        pairs = []
        for source in range(math.prod(counts)):
            target, rest, unit = 0, source, 1
            for count, flip in reversed(list(zip(counts, flips))):
                target += (rest % count ^ flip) * unit
                rest //= count
                unit *= count
            pairs.append((source, target))
        total = total + lax.ppermute(sums, tuple(far), pairs)
    return total


def solution(mesh):
    placed = (
        P(None, *AXES, None),
        P(*AXES, None),
        P(*AXES, None),
        P(),
        P(*AXES),
        P(*AXES),
    )
    return jax.shard_map(
        on_device,
        mesh=mesh,
        in_specs=placed,
        out_specs=(placed[0], placed[0], P(*AXES)),
        check_vma=False,
    )
```

```python
import functools
import math

import jax
import jax.numpy as jnp
from jax import lax
from jax.experimental import pallas as pl
from jax.experimental.pallas import tpu as pltpu
from jax.sharding import PartitionSpec as P

SPLAT_MARGIN = 3
BLUR_REACH = 2
STEPS = 2
CUTOFF = 10.0
EPSILON = 1e-06
STEP_SIZE = 1.0
FIT_GAIN = 0.2

AXES = ("gx", "gy", "gz")
SLOTS = 512
LANES = 128
TILES = SLOTS // LANES
BRICK = 16
PLANES = 26
HALF = PLANES // 2
EDGE = 10
PAD = 8
WIDE = 32
INTERPRET = False


def call(kernel, out_shape, cost, scratch=(), smem=0, n_in=0, vmem=48):
    specs = [pl.BlockSpec(memory_space=pltpu.SMEM)] * smem
    specs += [pl.BlockSpec(memory_space=pltpu.VMEM)] * (n_in - smem)
    many = isinstance(out_shape, (tuple, list))
    out_spec = pl.BlockSpec(memory_space=pltpu.VMEM)
    return pl.pallas_call(
        kernel,
        out_shape=out_shape,
        in_specs=specs,
        out_specs=[out_spec] * len(out_shape) if many else out_spec,
        scratch_shapes=list(scratch),
        cost_estimate=pl.CostEstimate(flops=cost, bytes_accessed=1 << 18, transcendentals=0),
        compiler_params=pltpu.CompilerParams(vmem_limit_bytes=vmem << 20),
        interpret=INTERPRET,
    )


def spread(row):
    return jnp.transpose(jnp.broadcast_to(row, (LANES, LANES)))


def gather_rows(acc):
    return jnp.sum(jnp.transpose(acc), axis=0, keepdims=True)


BLOCK = 32
BLOCKS = SLOTS // BLOCK
MANY = 16
FEW = 4
CELLS = 27
EMPTY = CELLS * TILES
ROOM = EMPTY + 4
FAR = 1e9


def three_parts(values):
    high = values.astype(jnp.bfloat16)
    rest = values - high.astype(jnp.float32)
    middle = rest.astype(jnp.bfloat16)
    return high, middle, (rest - middle.astype(jnp.float32)).astype(jnp.bfloat16)


def arrange_kernel(table, live_count, pos, charges, types, out, order, col, left):
    count = live_count[0]
    slot = lax.broadcasted_iota(jnp.int32, (TILES, LANES), 0) * LANES
    slot = slot + lax.broadcasted_iota(jnp.int32, (TILES, LANES), 1)
    living = slot < count
    alive = jnp.where(living, 1.0, 0.0)
    kinds = types[...]
    props = []
    for row in range(3):
        value = jnp.zeros((TILES, LANES), jnp.float32)
        for kind in range(table.shape[1]):
            value = jnp.where(kinds == kind, table[row, kind], value)
        props.append(value)
    group = jnp.zeros((TILES, LANES), jnp.float32)
    sub = lax.broadcasted_iota(jnp.int32, (SLOTS, LANES), 0)
    lane = lax.broadcasted_iota(jnp.int32, (SLOTS, LANES), 1)
    for dim, size in ((0, 256), (1, 128), (2, 64), (0, 32)):
        key = group * 64.0 + jnp.where(living, pos[4 * dim : 4 * dim + 4, :], 40.0)
        for tile in range(TILES):
            col[tile * LANES : (tile + 1) * LANES, :] = spread(key[tile : tile + 1, :])
        ranks = []
        for tile in range(TILES):
            row = key[tile : tile + 1, :]
            other = col[...]
            ahead = (other < row) | ((other == row) & (sub < lane + tile * LANES))
            ranks.append(jnp.sum(jnp.where(ahead, 1.0, 0.0), axis=0, keepdims=True))
        rank = jnp.concatenate(ranks, axis=0)
        group = jnp.floor(rank * (1.0 / size))
    order[...] = rank
    values = [pos[0:4, :], pos[4:8, :], pos[8:12, :], charges[...] * alive]
    values += [props[1] * alive, props[2] * alive, props[0], alive]
    total = jnp.zeros((3 * len(values), SLOTS), jnp.float32)
    for tile in range(TILES):
        block = jnp.concatenate([value[tile : tile + 1, :] for value in values], axis=0)
        for part, piece in enumerate(three_parts(block)):
            left[8 * part : 8 * part + 8, :] = piece.astype(jnp.float32)
        hot = jnp.where(rank[tile : tile + 1, :] == sub.astype(jnp.float32), 1.0, 0.0).astype(jnp.bfloat16)
        dims = (((1,), (1,)), ((), ()))
        total = total + lax.dot_general(left[...].astype(jnp.bfloat16), hot, dims, preferred_element_type=jnp.float32)
    total = total[0:8] + total[8:16] + total[16:24]
    for channel in range(8):
        for tile in range(TILES):
            at = slice(4 * channel + tile, 4 * channel + tile + 1)
            out[at, :] = total[channel : channel + 1, tile * LANES : (tile + 1) * LANES]


def restore_kernel(order, moved, start, force, out, left):
    values = [moved[4 * d : 4 * d + 4, :] - start[4 * d : 4 * d + 4, :] for d in range(3)]
    values += [force[4 * d : 4 * d + 4, :] for d in range(3)]
    values += [jnp.zeros((TILES, LANES), jnp.float32)] * 2
    sub = lax.broadcasted_iota(jnp.int32, (LANES, LANES), 0).astype(jnp.float32)
    totals = [jnp.zeros((24, LANES), jnp.float32) for _ in range(TILES)]
    for source in range(TILES):
        block = jnp.concatenate([value[source : source + 1, :] for value in values], axis=0)
        for part, piece in enumerate(three_parts(block)):
            left[8 * part : 8 * part + 8, :] = piece.astype(jnp.float32)
        parts = left[...].astype(jnp.bfloat16)
        for tile in range(TILES):
            hot = jnp.where(order[tile : tile + 1, :] == sub + float(source * LANES), 1.0, 0.0)
            totals[tile] = totals[tile] + jnp.dot(parts, hot.astype(jnp.bfloat16), preferred_element_type=jnp.float32)
    for tile in range(TILES):
        total = totals[tile][0:8] + totals[tile][8:16] + totals[tile][16:24]
        for channel in range(6):
            at = slice(4 * channel + tile, 4 * channel + tile + 1)
            out[at, :] = total[channel : channel + 1, :]


def plan_kernel(rows, fields, *refs):
    info, own, field = refs[:3]
    sources = refs[3:6]
    if fields == 2:
        known = ()
        listed, tiles, evolved, given, sums, active = refs[6:]
    else:
        known = refs[6:7]
        given = refs[7]
        listed, tiles, evolved, sums, active = refs[8:]
    low, high = [], []
    for dim in range(3):
        living = own[28:32, :] > 0.0
        value = own[4 * dim : 4 * dim + 4, :]
        lo, hi = jnp.where(living, value, FAR), jnp.where(living, value, -FAR)
        for step in (1, 2, 4, 8, 16):
            lo = jnp.minimum(lo, pltpu.roll(lo, LANES - step, 1))
            hi = jnp.maximum(hi, pltpu.roll(hi, LANES - step, 1))
        low.append(lo)
        high.append(hi)
    active[...] = jnp.zeros_like(active)
    tiles[EMPTY:ROOM] = jnp.zeros((ROOM - EMPTY, 8, LANES), jnp.float32)
    after_first, valid = arrivals(info, 2)
    slots = (1, jnp.where(after_first, 2, 0), jnp.where(after_first, 0, 2))
    for source, slot, ok in zip(sources, slots, (None,) + valid):

        for cell in range(9):
            number = slot * 9 + cell
            sides = (cell % 3 - 1, cell // 3 - 1, slot - 1)
            block = source[cell * rows : cell * rows + rows, :]
            if ok is not None:
                block = block * ok
            if known:
                charge = [known[0][4 * number + tile, 4:5, :] for tile in range(TILES)]
                screen = [known[0][4 * number + tile, 3:4, :] for tile in range(TILES)]
                living = jnp.concatenate(screen, axis=0) > 0.0
            else:
                charge = [block[12 + tile : 13 + tile] for tile in range(TILES)]
                screen = [block[16 + tile : 17 + tile] for tile in range(TILES)]
                living = block[16:20] > 0.0
            near_low, near_high = [], []
            for dim in range(3):
                side = sides[dim]
                shift = float(side * BRICK) if isinstance(side, int) else side.astype(jnp.float32) * float(BRICK)
                moved = block[4 * dim : 4 * dim + 4] + shift
                near_low.append(jnp.min(jnp.where(living, moved, FAR), axis=1, keepdims=True))
                near_high.append(jnp.max(jnp.where(living, moved, -FAR), axis=1, keepdims=True))
                scaled = moved * (1.0 / CUTOFF)
                for tile in range(TILES):
                    tiles[4 * number + tile, dim : dim + 1, :] = scaled[tile : tile + 1, :]
            for tile in range(TILES):
                tiles[4 * number + tile, 3:4, :] = screen[tile]
                tiles[4 * number + tile, 4:5, :] = charge[tile]
            for tile in range(TILES):
                apart = jnp.zeros((TILES, LANES), jnp.float32)
                for dim in range(3):
                    lo, hi = low[dim][tile : tile + 1, :], high[dim][tile : tile + 1, :]
                    gap = jnp.maximum(jnp.maximum(near_low[dim] - hi, lo - near_high[dim]), 0.0)
                    apart = apart + gap * gap
                near = jnp.where(apart < CUTOFF * CUTOFF * 1.0001, 1.0, 0.0)
                active[tile, pl.ds(pl.multiple_of(4 * number, TILES), TILES), :] = near
    row = lax.broadcasted_iota(jnp.int32, (LANES, LANES), 0)
    lane = lax.broadcasted_iota(jnp.int32, (LANES, LANES), 1)
    before = jnp.where(lane < row, 1.0, 0.0).astype(jnp.bfloat16)
    for tile in range(TILES):
        flags = active[tile]
        ranks = jnp.dot(before, flags.astype(jnp.bfloat16), preferred_element_type=jnp.float32)
        for part in range(LANES // BLOCK):
            at = slice(part * BLOCK, part * BLOCK + 1)
            chosen = jnp.broadcast_to(flags[:, at], (LANES, LANES)) > 0.0
            place = jnp.broadcast_to(ranks[:, at], (LANES, LANES)).astype(jnp.int32)
            total = jnp.sum(jnp.where(chosen, 1, 0), axis=0, keepdims=True)
            entry = jnp.sum(jnp.where(chosen & (place == lane), row, 0), axis=0, keepdims=True)
            spot = lane[0:1, :]
            entry = jnp.where(spot < total, entry, EMPTY)
            block = tile * (LANES // BLOCK) + part
            listed[block : block + 1, :] = jnp.where(spot == LANES - 1, total, entry)
    lane = lax.broadcasted_iota(jnp.int32, (8, LANES), 1)
    sub = lane & (WIDE - 1)
    own_points = (lane >= WIDE) & (lane < 3 * WIDE) & (sub >= PAD) & (sub < PAD + BRICK)
    squares = jnp.zeros((8, LANES), jnp.float32)
    cross = squares
    target = squares
    adds = shift_masks(info, 2)
    evolved[...] = field[0 : 8 * PLANES, :].reshape(PLANES, 8, LANES)
    take_shares(2, adds, sources[1:], 9 * rows, evolved, 0)
    if fields == 2:
        given[...] = field[8 * PLANES : 16 * PLANES, :].reshape(PLANES, 8, LANES)
        take_shares(2, adds, sources[1:], 9 * rows + 8 * HALF, given, 0)
    for plane in range(PLANES):
        value = evolved[plane]
        if 5 <= plane < 5 + BRICK:
            value = jnp.where(own_points, value, 0.0)
            wanted = jnp.where(own_points, given[plane], 0.0)
            squares = squares + value * value
            cross = cross + value * wanted
            target = target + wanted * wanted
    sums[...] = jnp.zeros_like(sums)
    sums[0:1, :] = jnp.sum(squares, axis=0, keepdims=True)
    sums[1:2, :] = jnp.sum(cross, axis=0, keepdims=True)
    sums[2:3, :] = jnp.sum(target, axis=0, keepdims=True)


def arrivals(info, axis):
    after_first = info[6 + 2 * axis] == 0
    return after_first, (1.0, jnp.where(info[7 + 2 * axis] > 0, 1.0, 0.0))


def upper_half(axis):
    lane = lax.broadcasted_iota(jnp.int32, (8, LANES), 1)
    return (lane >= 64) if axis == 1 else ((lane & (WIDE - 1)) >= BRICK)


def shift_masks(info, axis):
    upper = upper_half(axis)
    after_first, valid = arrivals(info, axis)
    after_one = jnp.where(after_first, 1.0, 0.0)
    masks = []
    for after, ok in zip((after_one, 1.0 - after_one), valid):
        masks.append((jnp.where(upper, after * ok, 0.0), jnp.where(upper, 0.0, (1.0 - after) * ok)))
    return masks


def half_steps(axis):
    return (64, 64) if axis == 1 else (BRICK, LANES - BRICK)


def take_shares(axis, masks, sources, base, into, first):
    up, down = half_steps(axis)
    for plane in range(HALF):
        at = slice(base + 8 * plane, base + 8 * plane + 8)
        low = into[first + plane]
        high = into[first + HALF + plane]
        for (from_after, from_before), source in zip(masks, sources):
            share = source[at, :]
            low = low + pltpu.roll(share, up, 1) * from_after + share * from_before
            high = high + share * from_after + pltpu.roll(share, down, 1) * from_before
        into[first + plane] = low
        into[first + HALF + plane] = high


def give_shares(info, axis, field, first, outs, base):
    up, down = half_steps(axis)
    upper = upper_half(axis)
    after_first, _ = arrivals(info, axis)
    for plane in range(HALF):
        low, high = field[first + plane], field[first + HALF + plane]
        after = jnp.where(upper, high, pltpu.roll(low, down, 1))
        before = jnp.where(upper, pltpu.roll(high, up, 1), low)
        at = slice(base + 8 * plane, base + 8 * plane + 8)
        outs[0][at, :] = jnp.where(after_first, after, before)
        outs[1][at, :] = jnp.where(after_first, before, after)


def merge_kernel(axis, count, rows, fields, info, field, mine, first, second, merged, out_first, out_second):
    after_first, valid = arrivals(info, axis)
    span = count * rows
    slots = (jnp.where(after_first, 2 * span, 0), jnp.where(after_first, 0, 2 * span))
    for out in (out_first, out_second):
        out[span : 2 * span, :] = mine[0:span, :]
        for source, slot, ok in zip((first, second), slots, valid):
            out[pl.ds(pl.multiple_of(slot, 8), span), :] = source[0:span, :] * ok
    merged[...] = field[...].reshape(fields * PLANES, 8, LANES)
    for number in range(fields):
        if axis == 0:
            for source, slot, ok in zip((first, second), slots, valid):
                into = pl.ds(number * PLANES + jnp.where(slot > 0, BRICK, 0), EDGE)
                at = slice(span + 8 * EDGE * number, span + 8 * EDGE * (number + 1))
                merged[into] = merged[into] + source[at, :].reshape(EDGE, 8, LANES) * ok
        else:
            base = span + 8 * HALF * number
            take_shares(axis, shift_masks(info, axis), (first, second), base, merged, number * PLANES)
        base = 3 * span + 8 * HALF * number
        give_shares(info, axis + 1, merged, number * PLANES, (out_first, out_second), base)


def radius_merge_kernel(axis, count, info, mine, first, second, out):
    after_first, _ = arrivals(info, axis)
    span = count * TILES
    out[span : 2 * span, :] = mine[0:span, :]
    slots = (jnp.where(after_first, 2 * span, 0), jnp.where(after_first, 0, 2 * span))
    for source, slot in zip((first, second), slots):
        out[pl.ds(pl.multiple_of(slot, 8), span), :] = source[0:span, :]
    out[3 * span : 3 * span + 8, :] = mine[span : span + 8, :] + first[span : span + 8, :]


def over_tiles(count, some, carry):
    whole = count // MANY
    carry = lax.fori_loop(0, whole, lambda i, c: some(MANY, i * MANY, c), carry)
    rest = (count - whole * MANY + FEW - 1) // FEW
    return lax.fori_loop(0, rest, lambda i, c: some(FEW, whole * MANY + i * FEW, c), carry)


def born_kernel(listed, tiles, own, out, col, acc):
    for channel in range(3):
        for tile in range(TILES):
            row = own[4 * channel + tile : 4 * channel + tile + 1, :] * (1.0 / CUTOFF)
            col[channel, tile * LANES : (tile + 1) * LANES, :] = spread(row)

    def block(ib, carry):
        at = pl.ds(pl.multiple_of(ib * BLOCK, BLOCK), BLOCK)
        xi, yi, zi = col[0, at, :], col[1, at, :], col[2, at, :]

        def some(width, start, total):
            for k in range(width):
                tile = listed[ib, start + k]
                dx = xi - tiles[tile, 0:1, :]
                dy = yi - tiles[tile, 1:2, :]
                dz = zi - tiles[tile, 2:3, :]
                u = dx * dx + dy * dy + dz * dz
                s = jnp.maximum(1.0 - u, 0.0)
                e = jnp.exp2(u * (-CUTOFF * CUTOFF / 8.0 * math.log2(math.e)))
                total = total + (e * s) * (s * tiles[tile, 3:4, :])
            return total

        acc[at, :] = over_tiles(listed[ib, LANES - 1], some, jnp.zeros((BLOCK, LANES), jnp.float32))
        return carry

    lax.fori_loop(0, BLOCKS, block, 0)
    for tile in range(TILES):
        total = gather_rows(acc[tile * LANES : (tile + 1) * LANES, :]) - own[16 + tile : 17 + tile, :]
        out[tile : tile + 1, :] = own[24 + tile : 25 + tile, :] + total


def gb_kernel(info, listed, tiles, own, own_radius, mine, first, second, out, col, acc, rows):
    for tile in range(TILES):
        at = slice(tile * LANES, (tile + 1) * LANES)
        for channel in range(3):
            row = own[4 * channel + tile : 4 * channel + tile + 1, :] * (1.0 / CUTOFF)
            col[channel, at, :] = spread(row)
        radius = spread(own_radius[tile : tile + 1, :] * (1.0 / CUTOFF))
        col[3, at, :] = radius
        col[4, at, :] = (-0.5 * math.log2(math.e)) / radius
    rows[EMPTY:ROOM] = jnp.ones((ROOM - EMPTY, 2, LANES), jnp.float32)

    after_first, _ = arrivals(info, 2)
    slots = (1, jnp.where(after_first, 2, 0), jnp.where(after_first, 0, 2))
    for source, slot in zip((mine, first, second), slots):
        for cell in range(9):
            radius = source[TILES * cell : TILES * cell + TILES, :] * (1.0 / CUTOFF)
            half = 0.5 / radius
            for tile in range(TILES):
                rows[slot * 36 + 4 * cell + tile, 0:1, :] = radius[tile : tile + 1, :]
                rows[slot * 36 + 4 * cell + tile, 1:2, :] = half[tile : tile + 1, :]

    def block(ib, carry):
        at = pl.ds(pl.multiple_of(ib * BLOCK, BLOCK), BLOCK)
        xi, yi, zi = col[0, at, :], col[1, at, :], col[2, at, :]
        ri, ai = col[3, at, :], col[4, at, :]

        def some(width, start, force):
            fx, fy, fz = force
            for k in range(width):
                tile = listed[ib, start + k]
                dx = xi - tiles[tile, 0:1, :]
                dy = yi - tiles[tile, 1:2, :]
                dz = zi - tiles[tile, 2:3, :]
                u = dx * dx + dy * dy + dz * dz
                s = jnp.maximum(1.0 - u, 0.0)
                e = jnp.exp2(u * (ai * rows[tile, 1:2, :]))
                inv = lax.rsqrt(u + (ri * rows[tile, 0:1, :]) * e)
                t = s * inv
                m = (tiles[tile, 4:5, :] * t) * (1.0 + (t * inv) * (0.25 - 0.0625 * e))
                fx = fx + m * dx
                fy = fy + m * dy
                fz = fz + m * dz
            return fx, fy, fz

        zero = jnp.zeros((BLOCK, LANES), jnp.float32)
        force = over_tiles(listed[ib, LANES - 1], some, (zero, zero, zero))
        for channel in range(3):
            acc[channel, at, :] = force[channel]
        return carry

    lax.fori_loop(0, BLOCKS, block, 0)
    for channel in range(3):
        for tile in range(TILES):
            total = gather_rows(acc[channel, tile * LANES : (tile + 1) * LANES, :])
            out[4 * channel + tile : 4 * channel + tile + 1, :] = total


def kernel_weights(reach):
    values = [math.exp(-0.5 * (index - reach) ** 2) for index in range(2 * reach + 1)]
    whole = sum(values)
    return [value / whole for value in values]


TAPS = kernel_weights(BLUR_REACH)


def blurred(values):
    rows = values.shape[0]
    near = pltpu.roll(values, 1, 0) + pltpu.roll(values, rows - 1, 0)
    far = pltpu.roll(values, 2, 0) + pltpu.roll(values, rows - 2, 0)
    return TAPS[2] * values + TAPS[1] * near + TAPS[0] * far


def profiles(row, side, base, rows, low, high, slope):
    number = lax.broadcasted_iota(jnp.int32, (rows, LANES), 0) + base
    shift = side * BRICK
    inside = (number >= low) & (number < high)
    window = inside & (number >= shift - SPLAT_MARGIN) & (number < shift + BRICK + SPLAT_MARGIN)
    moved = row + (float(shift) if isinstance(shift, int) else shift.astype(jnp.float32))
    gap = number.astype(jnp.float32) - moved
    plain = jnp.where(window, jnp.exp(-0.5 * gap * gap), 0.0)
    margin = SPLAT_MARGIN + BLUR_REACH
    reached = inside & (number >= shift - margin) & (number < shift + BRICK + margin)
    first = jnp.where(reached, blurred(plain), 0.0)
    if not slope:
        return first
    return first, jnp.where(reached, blurred(gap * plain), 0.0)


def split(values):
    high = values.astype(jnp.bfloat16)
    return high, (values - high.astype(jnp.float32)).astype(jnp.bfloat16)


def splat_kernel(fields, rows, bounds, own, *refs):
    if fields == 2:
        given = refs[0]
    field, out_first, out_second, px, left_hi, left_lo, right = refs[fields - 1 :]
    for tile in range(TILES):
        lanes = slice(tile * LANES, (tile + 1) * LANES)
        z = profiles(own[8 + tile : 9 + tile, :], 0, -PAD, WIDE, bounds[4], bounds[5], False)
        z_hi, z_lo = split(z)
        right[0:WIDE, lanes] = z_hi
        right[WIDE : 2 * WIDE, lanes] = z_lo
        x = profiles(own[tile : tile + 1, :], 0, -PAD, WIDE, bounds[0], bounds[1], False)
        px[...] = x * own[20 + tile : 21 + tile, :]
        y = profiles(own[4 + tile : 5 + tile, :], 0, -PAD, WIDE, bounds[2], bounds[3], False)
        for plane in range(PLANES):
            at = slice(plane * WIDE, (plane + 1) * WIDE)
            hi, lo = split(px[plane + 3 : plane + 4, :] * y)
            left_hi[at, lanes] = hi
            left_lo[at, lanes] = lo
    weights = right[...]
    dims = (((1,), (1,)), ((), ()))
    placed = lax.dot_general(left_hi[...], weights, dims, preferred_element_type=jnp.float32)
    placed = placed + lax.dot_general(left_lo[...], weights, dims, preferred_element_type=jnp.float32)
    placed = placed[:, 0:WIDE] + placed[:, WIDE : 2 * WIDE]
    placed = placed.reshape(PLANES, 4, 8, WIDE)
    for plane in range(PLANES):
        parts = [placed[plane, k] for k in range(4)]
        field[8 * plane : 8 * plane + 8, :] = jnp.concatenate(parts, axis=1)
    if fields == 2:
        base = 8 * PLANES
        field[base : base + 8 * PLANES, :] = jnp.zeros((8 * PLANES, LANES), jnp.float32)
        for plane in range(BRICK):
            value = pltpu.roll(given[plane, 0:8, :], WIDE + PAD, 1) + pltpu.roll(given[plane, 8:16, :], 2 * WIDE + PAD, 1)
            field[base + 8 * (plane + 5) : base + 8 * (plane + 6), :] = value
    after_first, _ = arrivals(bounds, 0)
    starts = (jnp.where(after_first, 8 * BRICK, 0), jnp.where(after_first, 0, 8 * BRICK))
    for out, start in zip((out_first, out_second), starts):
        out[0:rows, :] = own[0:rows, :]
        for number in range(fields):
            off = pl.ds(pl.multiple_of(8 * PLANES * number + start, 8), 8 * EDGE)
            out[rows + 8 * EDGE * number : rows + 8 * EDGE * (number + 1), :] = field[off, :]


def fit_kernel(scale, parts, bounds, *refs):
    own, evolved, exp_ext, sums = refs[:4]
    gb = refs[4 : 4 + parts]
    moved, force, left, right, inner, px, pxs = refs[4 + parts :]
    squares = jnp.sum(sums[0:1, :], axis=1, keepdims=True)
    cross = jnp.sum(sums[1:2, :], axis=1, keepdims=True)
    target = jnp.sum(sums[2:3, :], axis=1, keepdims=True)
    norm = jnp.sqrt((squares + EPSILON) * (target + EPSILON))
    given_part = 1.0 / norm
    model_part = (cross / norm) / (squares + EPSILON)
    for plane in range(PLANES):
        s = exp_ext[plane] * given_part - evolved[plane] * model_part
        blocks = [s] + [pltpu.roll(s, LANES - WIDE * k, 1) for k in (1, 2, 3)]
        s = jnp.concatenate(blocks, axis=0)
        s = jnp.where(lax.broadcasted_iota(jnp.int32, (WIDE, LANES), 1) < WIDE, s, 0.0)
        hi = s.astype(jnp.bfloat16).astype(jnp.float32)
        lo = (s - hi).astype(jnp.bfloat16).astype(jnp.float32)
        packed = hi + pltpu.roll(lo, WIDE, 1) + pltpu.roll(hi, 2 * WIDE, 1)
        left[plane * WIDE : (plane + 1) * WIDE, :] = packed.astype(jnp.bfloat16)
    moved[3 * TILES :, :] = own[3 * TILES :, :]
    right[...] = jnp.zeros_like(right)
    for tile in range(TILES):
        z, zs = profiles(own[8 + tile : 9 + tile, :], 0, -PAD, WIDE, bounds[4], bounds[5], True)
        for part, values in enumerate((z, zs)):
            lanes = slice(part * LANES, (part + 1) * LANES)
            hi, lo = split(values)
            right[0:WIDE, lanes] = hi
            right[WIDE : 2 * WIDE, lanes] = hi
            right[2 * WIDE : 3 * WIDE, lanes] = lo
        inner[...] = jnp.dot(left[...], right[...], preferred_element_type=jnp.float32)
        x, xs = profiles(own[tile : tile + 1, :], 0, -PAD, WIDE, bounds[0], bounds[1], True)
        y, ys = profiles(own[4 + tile : 5 + tile, :], 0, -PAD, WIDE, bounds[2], bounds[3], True)
        px[...] = x
        pxs[...] = xs
        turned_x = jnp.zeros((WIDE, LANES), jnp.float32)
        plain = turned_x
        turned_z = turned_x
        for plane in range(PLANES):
            rows = slice(plane * WIDE, (plane + 1) * WIDE)
            at_x = px[plane + 3 : plane + 4, :]
            part = inner[rows, 0:LANES]
            turned_x = turned_x + pxs[plane + 3 : plane + 4, :] * part
            plain = plain + at_x * part
            turned_z = turned_z + at_x * inner[rows, LANES : 2 * LANES]
        weight = scale * own[20 + tile : 21 + tile, :]
        charge = -2.0 / (CUTOFF * CUTOFF) * own[12 + tile : 13 + tile, :]
        sides = (turned_x * y, plain * ys, turned_z * y)
        for channel in range(3):
            at = slice(4 * channel + tile, 4 * channel + tile + 1)
            pair = gb[0][at, :]
            for other in gb[1:]:
                pair = pair + other[at, :]
            total = charge * pair + weight * jnp.sum(sides[channel], axis=0, keepdims=True)
            force[at, :] = total
            moved[at, :] = own[at, :] + STEP_SIZE * (own[28 + tile : 29 + tile, :] * total)


def partners(axis):
    count = lax.axis_size(axis)
    even = [(i, i ^ 1) for i in range(count)]
    odd = [(i, (i + 1 if i % 2 else i - 1) % count) for i in range(count)]
    return even, odd


def both_sides(blocks, axis):
    even, odd = partners(axis)
    return lax.ppermute(blocks[0], axis, even), lax.ppermute(blocks[1], axis, odd)


def across(block, axes, flips):
    counts = [lax.axis_size(axis) for axis in axes]
    pairs = []
    for source in range(math.prod(counts)):
        target, rest, unit = 0, source, 1
        for count, flip in reversed(list(zip(counts, flips))):
            target += (rest % count ^ flip) * unit
            rest //= count
            unit *= count
        pairs.append((source, target))
    return lax.ppermute(block, tuple(axes), pairs)


def from_all(block, steps):
    found = []
    for choice in range(1, 1 << len(steps)):
        flips = {}
        for k, (axis, flip) in enumerate(steps):
            if choice >> k & 1:
                flips[axis] = flips.get(axis, 0) | flip
        found.append(across(block, list(flips), list(flips.values())))
    return found


def f32(*shape):
    return jax.ShapeDtypeStruct(shape, jnp.float32)


def on_device(positions, charges, atom_types, type_table, live_count, exp_map):
    sizes = [lax.axis_size(axis) for axis in AXES]
    places = [lax.axis_index(axis) for axis in AXES]
    info = []
    for size, place in zip(sizes, places):
        info += [-place * BRICK, (size - place) * BRICK]
    for size, place in zip(sizes, places):
        odd = place % 2
        info += [odd, jnp.where(odd == 0, place > 0, place < size - 1).astype(jnp.int32)]
    info = jnp.stack(info).astype(jnp.int32)
    assert sizes[0] in (2, 4) and all(size in (2, 4, 8) for size in sizes)
    scale = FIT_GAIN * float(BRICK**3 * sizes[0] * sizes[1] * sizes[2])

    atoms, order = call(
        arrange_kernel,
        (f32(32, LANES), f32(TILES, LANES)),
        1 << 22,
        scratch=[pltpu.VMEM((SLOTS, LANES), jnp.float32), pltpu.VMEM((24, LANES), jnp.float32)],
        smem=2,
        n_in=5,
    )(
        type_table,
        live_count.reshape(1),
        positions.reshape(3 * TILES, LANES),
        charges.reshape(TILES, LANES),
        atom_types.reshape(TILES, LANES),
    )
    given = jnp.pad(exp_map, ((0, 0), (0, 0), (0, LANES - BRICK)))
    own = atoms
    for step in range(STEPS):
        fields, rows = (2, 24) if step == 0 else (1, 16)
        planes = 8 * PLANES * fields
        field, *mine = call(
            functools.partial(splat_kernel, fields, rows),
            (f32(planes, LANES),) + (f32(rows + 8 * EDGE * fields, LANES),) * 2,
            1 << 26,
            scratch=[
                pltpu.VMEM((WIDE, LANES), jnp.float32),
                pltpu.VMEM((PLANES * WIDE, SLOTS), jnp.bfloat16),
                pltpu.VMEM((PLANES * WIDE, SLOTS), jnp.bfloat16),
                pltpu.VMEM((2 * WIDE, SLOTS), jnp.bfloat16),
            ],
            smem=1,
            n_in=1 + fields,
        )(*((info, own, given) if step == 0 else (info, own)))
        for number, axis in enumerate(AXES[:2]):
            count = 3**number
            field, *mine = call(
                functools.partial(merge_kernel, number, count, rows, fields),
                (f32(fields * PLANES, 8, LANES),) + (f32(3 * count * rows + 8 * HALF * fields, LANES),) * 2,
                1 << 20,
                smem=1,
                n_in=5,
            )(info, field.reshape(planes, LANES), mine[0], *both_sides(mine, axis))
        before = () if step == 0 else (tiles, exp_ext)
        planned = call(
            functools.partial(plan_kernel, rows, fields),
            (jax.ShapeDtypeStruct((BLOCKS, LANES), jnp.int32), f32(ROOM, 8, LANES))
            + (f32(PLANES, 8, LANES),) * fields
            + (f32(8, LANES),),
            1 << 22,
            scratch=[pltpu.VMEM((TILES, LANES, LANES), jnp.float32)],
            smem=1,
            n_in=6 + len(before),
        )(info, own, field.reshape(planes, LANES), mine[0], *both_sides(mine, AXES[2]), *before)
        if step == 0:
            listed, tiles, evolved, exp_ext, sums = planned
        else:
            listed, tiles, evolved, sums = planned
        early = from_all(sums, [(axis, 2) for axis, size in zip(AXES[:2], sizes) if size >= 4])
        radius = call(
            born_kernel,
            f32(TILES, LANES),
            1 << 33,
            scratch=[pltpu.VMEM((3, SLOTS, LANES), jnp.float32), pltpu.VMEM((SLOTS, LANES), jnp.float32)],
            smem=1,
            n_in=3,
        )(listed, tiles, own)
        line = jnp.concatenate([radius, functools.reduce(jnp.add, early, sums)])
        for number, axis in enumerate(AXES):
            count = 3**number
            span = count * TILES
            near = both_sides((line, line), axis)
            if number == 2:
                here = line[span:]
                sums = here + near[0][span:]
                if sizes[2] >= 4:
                    sums = sums + across(here, [axis], [2]) + across(here, [axis], [3])
                break
            line = call(
                functools.partial(radius_merge_kernel, number, count),
                f32(3 * span + 8, LANES),
                1 << 20,
                smem=1,
                n_in=4,
            )(info, line, *near)
        pair = call(
            gb_kernel,
            f32(3 * TILES, LANES),
            1 << 34,
            scratch=[
                pltpu.VMEM((5, SLOTS, LANES), jnp.float32),
                pltpu.VMEM((3, SLOTS, LANES), jnp.float32),
                pltpu.VMEM((ROOM, 2, LANES), jnp.float32),
            ],
            smem=2,
            n_in=8,
        )(info, listed, tiles, own, radius, line, *near)
        far = [(axis, 4) for axis, size in zip(AXES, sizes) if size >= 8]
        sums = functools.reduce(jnp.add, from_all(sums, far), sums)
        own, force = call(
            functools.partial(fit_kernel, scale, 1),
            (f32(32, LANES), f32(3 * TILES, LANES)),
            1 << 26,
            scratch=[
                pltpu.VMEM((PLANES * WIDE, LANES), jnp.bfloat16),
                pltpu.VMEM((LANES, 2 * LANES), jnp.bfloat16),
                pltpu.VMEM((PLANES * WIDE, 2 * LANES), jnp.float32),
                pltpu.VMEM((WIDE, LANES), jnp.float32),
                pltpu.VMEM((WIDE, LANES), jnp.float32),
            ],
            smem=1,
            n_in=6,
        )(info, own, evolved, exp_ext, sums, pair)
    results = call(
        restore_kernel,
        f32(6 * TILES, LANES),
        1 << 20,
        scratch=[pltpu.VMEM((24, LANES), jnp.float32)],
        n_in=4,
    )(order, own, atoms, force)
    model = evolved[5 : 5 + BRICK].reshape(BRICK, 8, 4, WIDE).transpose(0, 2, 1, 3).reshape(BRICK, WIDE, WIDE)
    model = model[:, PAD : PAD + BRICK, PAD : PAD + BRICK]
    results = results.reshape((2,) + positions.shape)
    return results[0], results[1], model


def solution(mesh):
    placed = (
        P(None, *AXES, None),
        P(*AXES, None),
        P(*AXES, None),
        P(),
        P(*AXES),
        P(*AXES),
    )
    return jax.shard_map(
        on_device,
        mesh=mesh,
        in_specs=placed,
        out_specs=(placed[0], placed[0], P(*AXES)),
        check_vma=False,
    )
```

```python
import functools
import math

import jax
import jax.numpy as jnp
from jax import lax
from jax.experimental import pallas as pl
from jax.experimental.pallas import tpu as pltpu
from jax.sharding import PartitionSpec as P

SPLAT_MARGIN = 3
BLUR_REACH = 2
STEPS = 2
CUTOFF = 10.0
EPSILON = 1e-06
STEP_SIZE = 1.0
FIT_GAIN = 0.2

AXES = ("gx", "gy", "gz")
SLOTS = 512
LANES = 128
TILES = SLOTS // LANES
BRICK = 16
PLANES = 26
HALF = PLANES // 2
EDGE = 10
PAD = 8
WIDE = 32
INTERPRET = False


def call(kernel, out_shape, cost, scratch=(), smem=0, n_in=0, vmem=48):
    specs = [pl.BlockSpec(memory_space=pltpu.SMEM)] * smem
    specs += [pl.BlockSpec(memory_space=pltpu.VMEM)] * (n_in - smem)
    many = isinstance(out_shape, (tuple, list))
    out_spec = pl.BlockSpec(memory_space=pltpu.VMEM)
    return pl.pallas_call(
        kernel,
        out_shape=out_shape,
        in_specs=specs,
        out_specs=[out_spec] * len(out_shape) if many else out_spec,
        scratch_shapes=list(scratch),
        cost_estimate=pl.CostEstimate(flops=cost, bytes_accessed=1 << 18, transcendentals=0),
        compiler_params=pltpu.CompilerParams(vmem_limit_bytes=vmem << 20),
        interpret=INTERPRET,
    )


def spread(row):
    return jnp.transpose(jnp.broadcast_to(row, (LANES, LANES)))


def gather_rows(acc):
    return jnp.sum(jnp.transpose(acc), axis=0, keepdims=True)


BLOCK = 32
BLOCKS = SLOTS // BLOCK
MANY = 16
FEW = 4
CELLS = 27
EMPTY = CELLS * TILES
ROOM = EMPTY + 4
FAR = 1e9


def three_parts(values):
    high = values.astype(jnp.bfloat16)
    rest = values - high.astype(jnp.float32)
    middle = rest.astype(jnp.bfloat16)
    return high, middle, (rest - middle.astype(jnp.float32)).astype(jnp.bfloat16)


def tiled(block, *index):
    row = block[(*index, 0, 0)] if index else block[0, 0]
    return jnp.concatenate([row[:, tile * LANES : (tile + 1) * LANES] for tile in range(TILES)], axis=0)


def arrange_kernel(table, live_count, given, charges, types, out, order, col, left):
    count = live_count[0]
    pos = jnp.concatenate([tiled(given, dim) for dim in range(3)], axis=0)
    slot = lax.broadcasted_iota(jnp.int32, (TILES, LANES), 0) * LANES
    slot = slot + lax.broadcasted_iota(jnp.int32, (TILES, LANES), 1)
    living = slot < count
    alive = jnp.where(living, 1.0, 0.0)
    kinds = tiled(types)
    props = []
    for row in range(3):
        value = jnp.zeros((TILES, LANES), jnp.float32)
        for kind in range(table.shape[1]):
            value = jnp.where(kinds == kind, table[row, kind], value)
        props.append(value)
    group = jnp.zeros((TILES, LANES), jnp.float32)
    sub = lax.broadcasted_iota(jnp.int32, (SLOTS, LANES), 0)
    lane = lax.broadcasted_iota(jnp.int32, (SLOTS, LANES), 1)
    for dim, size in ((0, 256), (1, 128), (2, 64), (0, 32)):
        key = group * 64.0 + jnp.where(living, pos[4 * dim : 4 * dim + 4, :], 40.0)
        for tile in range(TILES):
            col[tile * LANES : (tile + 1) * LANES, :] = spread(key[tile : tile + 1, :])
        ranks = []
        for tile in range(TILES):
            row = key[tile : tile + 1, :]
            other = col[...]
            ahead = (other < row) | ((other == row) & (sub < lane + tile * LANES))
            ranks.append(jnp.sum(jnp.where(ahead, 1.0, 0.0), axis=0, keepdims=True))
        rank = jnp.concatenate(ranks, axis=0)
        group = jnp.floor(rank * (1.0 / size))
    order[...] = rank
    values = [pos[0:4, :], pos[4:8, :], pos[8:12, :], tiled(charges) * alive]
    values += [props[1] * alive, props[2] * alive, props[0], alive]
    total = jnp.zeros((3 * len(values), SLOTS), jnp.float32)
    for tile in range(TILES):
        block = jnp.concatenate([value[tile : tile + 1, :] for value in values], axis=0)
        for part, piece in enumerate(three_parts(block)):
            left[8 * part : 8 * part + 8, :] = piece.astype(jnp.float32)
        hot = jnp.where(rank[tile : tile + 1, :] == sub.astype(jnp.float32), 1.0, 0.0).astype(jnp.bfloat16)
        dims = (((1,), (1,)), ((), ()))
        total = total + lax.dot_general(left[...].astype(jnp.bfloat16), hot, dims, preferred_element_type=jnp.float32)
    total = total[0:8] + total[8:16] + total[16:24]
    for channel in range(8):
        for tile in range(TILES):
            at = slice(4 * channel + tile, 4 * channel + tile + 1)
            out[at, :] = total[channel : channel + 1, tile * LANES : (tile + 1) * LANES]


def restore_kernel(order, moved, start, force, displaced, final, left):
    values = [moved[4 * d : 4 * d + 4, :] - start[4 * d : 4 * d + 4, :] for d in range(3)]
    values += [force[4 * d : 4 * d + 4, :] for d in range(3)]
    values += [jnp.zeros((TILES, LANES), jnp.float32)] * 2
    sub = lax.broadcasted_iota(jnp.int32, (LANES, LANES), 0).astype(jnp.float32)
    totals = [jnp.zeros((24, LANES), jnp.float32) for _ in range(TILES)]
    for source in range(TILES):
        block = jnp.concatenate([value[source : source + 1, :] for value in values], axis=0)
        for part, piece in enumerate(three_parts(block)):
            left[8 * part : 8 * part + 8, :] = piece.astype(jnp.float32)
        parts = left[...].astype(jnp.bfloat16)
        for tile in range(TILES):
            hot = jnp.where(order[tile : tile + 1, :] == sub + float(source * LANES), 1.0, 0.0)
            totals[tile] = totals[tile] + jnp.dot(parts, hot.astype(jnp.bfloat16), preferred_element_type=jnp.float32)
    for tile in range(TILES):
        total = totals[tile][0:8] + totals[tile][8:16] + totals[tile][16:24]
        for channel in range(6):
            out = displaced if channel < 3 else final
            out[channel % 3, 0, 0, :, tile * LANES : (tile + 1) * LANES] = total[channel : channel + 1, :]


def plan_kernel(rows, fields, *refs):
    info, own, field = refs[:3]
    sources = refs[3:6]
    if fields == 2:
        known = ()
        listed, tiles, evolved, given, sums, active = refs[6:]
    else:
        known = refs[6:7]
        given = refs[7]
        listed, tiles, evolved, sums, active = refs[8:]
    low, high = [], []
    for dim in range(3):
        living = own[28:32, :] > 0.0
        value = own[4 * dim : 4 * dim + 4, :]
        lo, hi = jnp.where(living, value, FAR), jnp.where(living, value, -FAR)
        for step in (1, 2, 4, 8, 16):
            lo = jnp.minimum(lo, pltpu.roll(lo, LANES - step, 1))
            hi = jnp.maximum(hi, pltpu.roll(hi, LANES - step, 1))
        low.append(lo)
        high.append(hi)
    active[...] = jnp.zeros_like(active)
    tiles[EMPTY:ROOM] = jnp.zeros((ROOM - EMPTY, 8, LANES), jnp.float32)
    after_first, valid = arrivals(info, 2)
    slots = (1, jnp.where(after_first, 2, 0), jnp.where(after_first, 0, 2))
    for source, slot, ok in zip(sources, slots, (None,) + valid):

        for cell in range(9):
            number = slot * 9 + cell
            sides = (cell % 3 - 1, cell // 3 - 1, slot - 1)
            block = source[cell * rows : cell * rows + rows, :]
            if ok is not None:
                block = block * ok
            if known:
                charge = [known[0][4 * number + tile, 4:5, :] for tile in range(TILES)]
                screen = [known[0][4 * number + tile, 3:4, :] for tile in range(TILES)]
                living = jnp.concatenate(screen, axis=0) > 0.0
            else:
                charge = [block[12 + tile : 13 + tile] for tile in range(TILES)]
                screen = [block[16 + tile : 17 + tile] for tile in range(TILES)]
                living = block[16:20] > 0.0
            near_low, near_high = [], []
            for dim in range(3):
                side = sides[dim]
                shift = float(side * BRICK) if isinstance(side, int) else side.astype(jnp.float32) * float(BRICK)
                moved = block[4 * dim : 4 * dim + 4] + shift
                near_low.append(jnp.min(jnp.where(living, moved, FAR), axis=1, keepdims=True))
                near_high.append(jnp.max(jnp.where(living, moved, -FAR), axis=1, keepdims=True))
                scaled = moved * (1.0 / CUTOFF)
                for tile in range(TILES):
                    tiles[4 * number + tile, dim : dim + 1, :] = scaled[tile : tile + 1, :]
            for tile in range(TILES):
                tiles[4 * number + tile, 3:4, :] = screen[tile]
                tiles[4 * number + tile, 4:5, :] = charge[tile]
            for tile in range(TILES):
                apart = jnp.zeros((TILES, LANES), jnp.float32)
                for dim in range(3):
                    lo, hi = low[dim][tile : tile + 1, :], high[dim][tile : tile + 1, :]
                    gap = jnp.maximum(jnp.maximum(near_low[dim] - hi, lo - near_high[dim]), 0.0)
                    apart = apart + gap * gap
                near = jnp.where(apart < CUTOFF * CUTOFF * 1.0001, 1.0, 0.0)
                active[tile, pl.ds(pl.multiple_of(4 * number, TILES), TILES), :] = near
    row = lax.broadcasted_iota(jnp.int32, (LANES, LANES), 0)
    lane = lax.broadcasted_iota(jnp.int32, (LANES, LANES), 1)
    before = jnp.where(lane < row, 1.0, 0.0).astype(jnp.bfloat16)
    for tile in range(TILES):
        flags = active[tile]
        ranks = jnp.dot(before, flags.astype(jnp.bfloat16), preferred_element_type=jnp.float32)
        for part in range(LANES // BLOCK):
            at = slice(part * BLOCK, part * BLOCK + 1)
            chosen = jnp.broadcast_to(flags[:, at], (LANES, LANES)) > 0.0
            place = jnp.broadcast_to(ranks[:, at], (LANES, LANES)).astype(jnp.int32)
            total = jnp.sum(jnp.where(chosen, 1, 0), axis=0, keepdims=True)
            entry = jnp.sum(jnp.where(chosen & (place == lane), row, 0), axis=0, keepdims=True)
            spot = lane[0:1, :]
            entry = jnp.where(spot < total, entry, EMPTY)
            block = tile * (LANES // BLOCK) + part
            listed[block : block + 1, :] = jnp.where(spot == LANES - 1, total, entry)
    lane = lax.broadcasted_iota(jnp.int32, (8, LANES), 1)
    sub = lane & (WIDE - 1)
    own_points = (lane >= WIDE) & (lane < 3 * WIDE) & (sub >= PAD) & (sub < PAD + BRICK)
    squares = jnp.zeros((8, LANES), jnp.float32)
    cross = squares
    target = squares
    adds = shift_masks(info, 2)
    evolved[...] = field[0 : 8 * PLANES, :].reshape(PLANES, 8, LANES)
    take_shares(2, adds, sources[1:], 9 * rows, evolved, 0)
    if fields == 2:
        given[...] = field[8 * PLANES : 16 * PLANES, :].reshape(PLANES, 8, LANES)
        take_shares(2, adds, sources[1:], 9 * rows + 8 * HALF, given, 0)
    for plane in range(PLANES):
        value = evolved[plane]
        if 5 <= plane < 5 + BRICK:
            value = jnp.where(own_points, value, 0.0)
            wanted = jnp.where(own_points, given[plane], 0.0)
            squares = squares + value * value
            cross = cross + value * wanted
            target = target + wanted * wanted
    sums[...] = jnp.zeros_like(sums)
    sums[0:1, :] = jnp.sum(squares, axis=0, keepdims=True)
    sums[1:2, :] = jnp.sum(cross, axis=0, keepdims=True)
    sums[2:3, :] = jnp.sum(target, axis=0, keepdims=True)


def arrivals(info, axis):
    after_first = info[6 + 2 * axis] == 0
    return after_first, (1.0, jnp.where(info[7 + 2 * axis] > 0, 1.0, 0.0))


def upper_half(axis):
    lane = lax.broadcasted_iota(jnp.int32, (8, LANES), 1)
    return (lane >= 64) if axis == 1 else ((lane & (WIDE - 1)) >= BRICK)


def shift_masks(info, axis):
    upper = upper_half(axis)
    after_first, valid = arrivals(info, axis)
    after_one = jnp.where(after_first, 1.0, 0.0)
    masks = []
    for after, ok in zip((after_one, 1.0 - after_one), valid):
        masks.append((jnp.where(upper, after * ok, 0.0), jnp.where(upper, 0.0, (1.0 - after) * ok)))
    return masks


def half_steps(axis):
    return (64, 64) if axis == 1 else (BRICK, LANES - BRICK)


def take_shares(axis, masks, sources, base, into, first):
    up, down = half_steps(axis)
    for plane in range(HALF):
        at = slice(base + 8 * plane, base + 8 * plane + 8)
        low = into[first + plane]
        high = into[first + HALF + plane]
        for (from_after, from_before), source in zip(masks, sources):
            share = source[at, :]
            low = low + pltpu.roll(share, up, 1) * from_after + share * from_before
            high = high + share * from_after + pltpu.roll(share, down, 1) * from_before
        into[first + plane] = low
        into[first + HALF + plane] = high


def give_shares(info, axis, field, first, outs, base):
    up, down = half_steps(axis)
    upper = upper_half(axis)
    after_first, _ = arrivals(info, axis)
    for plane in range(HALF):
        low, high = field[first + plane], field[first + HALF + plane]
        after = jnp.where(upper, high, pltpu.roll(low, down, 1))
        before = jnp.where(upper, pltpu.roll(high, up, 1), low)
        at = slice(base + 8 * plane, base + 8 * plane + 8)
        outs[0][at, :] = jnp.where(after_first, after, before)
        outs[1][at, :] = jnp.where(after_first, before, after)


def merge_kernel(axis, count, rows, fields, info, field, mine, first, second, merged, out_first, out_second):
    after_first, valid = arrivals(info, axis)
    span = count * rows
    slots = (jnp.where(after_first, 2 * span, 0), jnp.where(after_first, 0, 2 * span))
    for out in (out_first, out_second):
        out[span : 2 * span, :] = mine[0:span, :]
        for source, slot, ok in zip((first, second), slots, valid):
            out[pl.ds(pl.multiple_of(slot, 8), span), :] = source[0:span, :] * ok
    merged[...] = field[...].reshape(fields * PLANES, 8, LANES)
    for number in range(fields):
        if axis == 0:
            for source, slot, ok in zip((first, second), slots, valid):
                into = pl.ds(number * PLANES + jnp.where(slot > 0, BRICK, 0), EDGE)
                at = slice(span + 8 * EDGE * number, span + 8 * EDGE * (number + 1))
                merged[into] = merged[into] + source[at, :].reshape(EDGE, 8, LANES) * ok
        else:
            base = span + 8 * HALF * number
            take_shares(axis, shift_masks(info, axis), (first, second), base, merged, number * PLANES)
        base = 3 * span + 8 * HALF * number
        give_shares(info, axis + 1, merged, number * PLANES, (out_first, out_second), base)


def radius_merge_kernel(axis, count, info, mine, first, second, *refs):
    others, (out, sums) = refs[:-2], refs[-2:]
    after_first, _ = arrivals(info, axis)
    span = count * TILES
    out[span : 2 * span, :] = mine[0:span, :]
    slots = (jnp.where(after_first, 2 * span, 0), jnp.where(after_first, 0, 2 * span))
    for source, slot in zip((first, second), slots):
        out[pl.ds(pl.multiple_of(slot, 8), span), :] = source[0:span, :]
    total = mine[span : span + 8, :] + first[span : span + 8, :]
    for other in others:
        total = total + other[...]
    out[3 * span : 3 * span + 8, :] = total
    sums[...] = total


def over_tiles(count, some, carry):
    whole = count // MANY
    carry = lax.fori_loop(0, whole, lambda i, c: some(MANY, i * MANY, c), carry)
    rest = (count - whole * MANY + FEW - 1) // FEW
    return lax.fori_loop(0, rest, lambda i, c: some(FEW, whole * MANY + i * FEW, c), carry)


def born_kernel(listed, tiles, own, out, col, acc):
    for channel in range(3):
        for tile in range(TILES):
            row = own[4 * channel + tile : 4 * channel + tile + 1, :] * (1.0 / CUTOFF)
            col[channel, tile * LANES : (tile + 1) * LANES, :] = spread(row)

    def block(ib, carry):
        at = pl.ds(pl.multiple_of(ib * BLOCK, BLOCK), BLOCK)
        xi, yi, zi = col[0, at, :], col[1, at, :], col[2, at, :]

        def some(width, start, total):
            for k in range(width):
                tile = listed[ib, start + k]
                dx = xi - tiles[tile, 0:1, :]
                dy = yi - tiles[tile, 1:2, :]
                dz = zi - tiles[tile, 2:3, :]
                u = dx * dx + dy * dy + dz * dz
                s = jnp.maximum(1.0 - u, 0.0)
                e = jnp.exp2(u * (-CUTOFF * CUTOFF / 8.0 * math.log2(math.e)))
                total = total + (e * s) * (s * tiles[tile, 3:4, :])
            return total

        acc[at, :] = over_tiles(listed[ib, LANES - 1], some, jnp.zeros((BLOCK, LANES), jnp.float32))
        return carry

    lax.fori_loop(0, BLOCKS, block, 0)
    for tile in range(TILES):
        total = gather_rows(acc[tile * LANES : (tile + 1) * LANES, :]) - own[16 + tile : 17 + tile, :]
        out[tile : tile + 1, :] = own[24 + tile : 25 + tile, :] + total


def gb_kernel(info, listed, tiles, own, own_radius, mine, first, second, out, col, acc, rows):
    for tile in range(TILES):
        at = slice(tile * LANES, (tile + 1) * LANES)
        for channel in range(3):
            row = own[4 * channel + tile : 4 * channel + tile + 1, :] * (1.0 / CUTOFF)
            col[channel, at, :] = spread(row)
        radius = spread(own_radius[tile : tile + 1, :] * (1.0 / CUTOFF))
        col[3, at, :] = radius
        col[4, at, :] = (-0.5 * math.log2(math.e)) / radius
    rows[EMPTY:ROOM] = jnp.ones((ROOM - EMPTY, 2, LANES), jnp.float32)

    after_first, _ = arrivals(info, 2)
    slots = (1, jnp.where(after_first, 2, 0), jnp.where(after_first, 0, 2))
    for source, slot in zip((mine, first, second), slots):
        for cell in range(9):
            radius = source[TILES * cell : TILES * cell + TILES, :] * (1.0 / CUTOFF)
            half = 0.5 / radius
            for tile in range(TILES):
                rows[slot * 36 + 4 * cell + tile, 0:1, :] = radius[tile : tile + 1, :]
                rows[slot * 36 + 4 * cell + tile, 1:2, :] = half[tile : tile + 1, :]

    def block(ib, carry):
        at = pl.ds(pl.multiple_of(ib * BLOCK, BLOCK), BLOCK)
        xi, yi, zi = col[0, at, :], col[1, at, :], col[2, at, :]
        ri, ai = col[3, at, :], col[4, at, :]

        def some(width, start, force):
            fx, fy, fz = force
            for k in range(width):
                tile = listed[ib, start + k]
                dx = xi - tiles[tile, 0:1, :]
                dy = yi - tiles[tile, 1:2, :]
                dz = zi - tiles[tile, 2:3, :]
                u = dx * dx + dy * dy + dz * dz
                s = jnp.maximum(1.0 - u, 0.0)
                e = jnp.exp2(u * (ai * rows[tile, 1:2, :]))
                inv = lax.rsqrt(u + (ri * rows[tile, 0:1, :]) * e)
                t = s * inv
                m = (tiles[tile, 4:5, :] * t) * (1.0 + (t * inv) * (0.25 - 0.0625 * e))
                fx = fx + m * dx
                fy = fy + m * dy
                fz = fz + m * dz
            return fx, fy, fz

        zero = jnp.zeros((BLOCK, LANES), jnp.float32)
        force = over_tiles(listed[ib, LANES - 1], some, (zero, zero, zero))
        for channel in range(3):
            acc[channel, at, :] = force[channel]
        return carry

    lax.fori_loop(0, BLOCKS, block, 0)
    for channel in range(3):
        for tile in range(TILES):
            total = gather_rows(acc[channel, tile * LANES : (tile + 1) * LANES, :])
            out[4 * channel + tile : 4 * channel + tile + 1, :] = total


def kernel_weights(reach):
    values = [math.exp(-0.5 * (index - reach) ** 2) for index in range(2 * reach + 1)]
    whole = sum(values)
    return [value / whole for value in values]


TAPS = kernel_weights(BLUR_REACH)


def blurred(values):
    rows = values.shape[0]
    near = pltpu.roll(values, 1, 0) + pltpu.roll(values, rows - 1, 0)
    far = pltpu.roll(values, 2, 0) + pltpu.roll(values, rows - 2, 0)
    return TAPS[2] * values + TAPS[1] * near + TAPS[0] * far


def profiles(row, side, base, rows, low, high, slope):
    number = lax.broadcasted_iota(jnp.int32, (rows, LANES), 0) + base
    shift = side * BRICK
    inside = (number >= low) & (number < high)
    window = inside & (number >= shift - SPLAT_MARGIN) & (number < shift + BRICK + SPLAT_MARGIN)
    moved = row + (float(shift) if isinstance(shift, int) else shift.astype(jnp.float32))
    gap = number.astype(jnp.float32) - moved
    plain = jnp.where(window, jnp.exp(-0.5 * gap * gap), 0.0)
    margin = SPLAT_MARGIN + BLUR_REACH
    reached = inside & (number >= shift - margin) & (number < shift + BRICK + margin)
    first = jnp.where(reached, blurred(plain), 0.0)
    if not slope:
        return first
    return first, jnp.where(reached, blurred(gap * plain), 0.0)


def split(values):
    high = values.astype(jnp.bfloat16)
    return high, (values - high.astype(jnp.float32)).astype(jnp.bfloat16)


def splat_kernel(fields, rows, bounds, own, *refs):
    if fields == 2:
        given = refs[0]
    field, out_first, out_second, px, left_hi, left_lo, right = refs[fields - 1 :]
    for tile in range(TILES):
        lanes = slice(tile * LANES, (tile + 1) * LANES)
        z = profiles(own[8 + tile : 9 + tile, :], 0, -PAD, WIDE, bounds[4], bounds[5], False)
        z_hi, z_lo = split(z)
        right[0:WIDE, lanes] = z_hi
        right[WIDE : 2 * WIDE, lanes] = z_lo
        x = profiles(own[tile : tile + 1, :], 0, -PAD, WIDE, bounds[0], bounds[1], False)
        px[...] = x * own[20 + tile : 21 + tile, :]
        y = profiles(own[4 + tile : 5 + tile, :], 0, -PAD, WIDE, bounds[2], bounds[3], False)
        for plane in range(PLANES):
            at = slice(plane * WIDE, (plane + 1) * WIDE)
            hi, lo = split(px[plane + 3 : plane + 4, :] * y)
            left_hi[at, lanes] = hi
            left_lo[at, lanes] = lo
    weights = right[...]
    dims = (((1,), (1,)), ((), ()))
    placed = lax.dot_general(left_hi[...], weights, dims, preferred_element_type=jnp.float32)
    placed = placed + lax.dot_general(left_lo[...], weights, dims, preferred_element_type=jnp.float32)
    placed = placed[:, 0:WIDE] + placed[:, WIDE : 2 * WIDE]
    placed = placed.reshape(PLANES, 4, 8, WIDE)
    for plane in range(PLANES):
        parts = [placed[plane, k] for k in range(4)]
        field[8 * plane : 8 * plane + 8, :] = jnp.concatenate(parts, axis=1)
    if fields == 2:
        base = 8 * PLANES
        field[base : base + 8 * PLANES, :] = jnp.zeros((8 * PLANES, LANES), jnp.float32)
        for plane in range(BRICK):
            value = pltpu.roll(given[plane, 0:8, :], WIDE + PAD, 1) + pltpu.roll(given[plane, 8:16, :], 2 * WIDE + PAD, 1)
            field[base + 8 * (plane + 5) : base + 8 * (plane + 6), :] = value
    after_first, _ = arrivals(bounds, 0)
    starts = (jnp.where(after_first, 8 * BRICK, 0), jnp.where(after_first, 0, 8 * BRICK))
    for out, start in zip((out_first, out_second), starts):
        out[0:rows, :] = own[0:rows, :]
        for number in range(fields):
            off = pl.ds(pl.multiple_of(8 * PLANES * number + start, 8), 8 * EDGE)
            out[rows + 8 * EDGE * number : rows + 8 * EDGE * (number + 1), :] = field[off, :]


def fit_kernel(scale, parts, bounds, *refs):
    own, evolved, exp_ext, sums = refs[:4]
    gb = refs[4 : 4 + parts]
    moved, force, left, right, inner, px, pxs = refs[4 + parts :]
    squares = jnp.sum(sums[0:1, :], axis=1, keepdims=True)
    cross = jnp.sum(sums[1:2, :], axis=1, keepdims=True)
    target = jnp.sum(sums[2:3, :], axis=1, keepdims=True)
    norm = jnp.sqrt((squares + EPSILON) * (target + EPSILON))
    given_part = 1.0 / norm
    model_part = (cross / norm) / (squares + EPSILON)
    for plane in range(PLANES):
        s = exp_ext[plane] * given_part - evolved[plane] * model_part
        blocks = [s] + [pltpu.roll(s, LANES - WIDE * k, 1) for k in (1, 2, 3)]
        s = jnp.concatenate(blocks, axis=0)
        s = jnp.where(lax.broadcasted_iota(jnp.int32, (WIDE, LANES), 1) < WIDE, s, 0.0)
        hi = s.astype(jnp.bfloat16).astype(jnp.float32)
        lo = (s - hi).astype(jnp.bfloat16).astype(jnp.float32)
        packed = hi + pltpu.roll(lo, WIDE, 1) + pltpu.roll(hi, 2 * WIDE, 1)
        left[plane * WIDE : (plane + 1) * WIDE, :] = packed.astype(jnp.bfloat16)
    moved[3 * TILES :, :] = own[3 * TILES :, :]
    right[...] = jnp.zeros_like(right)
    for tile in range(TILES):
        z, zs = profiles(own[8 + tile : 9 + tile, :], 0, -PAD, WIDE, bounds[4], bounds[5], True)
        for part, values in enumerate((z, zs)):
            lanes = slice(part * LANES, (part + 1) * LANES)
            hi, lo = split(values)
            right[0:WIDE, lanes] = hi
            right[WIDE : 2 * WIDE, lanes] = hi
            right[2 * WIDE : 3 * WIDE, lanes] = lo
        inner[...] = jnp.dot(left[...], right[...], preferred_element_type=jnp.float32)
        x, xs = profiles(own[tile : tile + 1, :], 0, -PAD, WIDE, bounds[0], bounds[1], True)
        y, ys = profiles(own[4 + tile : 5 + tile, :], 0, -PAD, WIDE, bounds[2], bounds[3], True)
        px[...] = x
        pxs[...] = xs
        turned_x = jnp.zeros((WIDE, LANES), jnp.float32)
        plain = turned_x
        turned_z = turned_x
        for plane in range(PLANES):
            rows = slice(plane * WIDE, (plane + 1) * WIDE)
            at_x = px[plane + 3 : plane + 4, :]
            part = inner[rows, 0:LANES]
            turned_x = turned_x + pxs[plane + 3 : plane + 4, :] * part
            plain = plain + at_x * part
            turned_z = turned_z + at_x * inner[rows, LANES : 2 * LANES]
        weight = scale * own[20 + tile : 21 + tile, :]
        charge = -2.0 / (CUTOFF * CUTOFF) * own[12 + tile : 13 + tile, :]
        sides = (turned_x * y, plain * ys, turned_z * y)
        for channel in range(3):
            at = slice(4 * channel + tile, 4 * channel + tile + 1)
            pair = gb[0][at, :]
            for other in gb[1:]:
                pair = pair + other[at, :]
            total = charge * pair + weight * jnp.sum(sides[channel], axis=0, keepdims=True)
            force[at, :] = total
            moved[at, :] = own[at, :] + STEP_SIZE * (own[28 + tile : 29 + tile, :] * total)


def partners(axis):
    count = lax.axis_size(axis)
    even = [(i, i ^ 1) for i in range(count)]
    odd = [(i, (i + 1 if i % 2 else i - 1) % count) for i in range(count)]
    return even, odd


def both_sides(blocks, axis):
    even, odd = partners(axis)
    return lax.ppermute(blocks[0], axis, even), lax.ppermute(blocks[1], axis, odd)


def across(block, axes, flips):
    counts = [lax.axis_size(axis) for axis in axes]
    pairs = []
    for source in range(math.prod(counts)):
        target, rest, unit = 0, source, 1
        for count, flip in reversed(list(zip(counts, flips))):
            target += (rest % count ^ flip) * unit
            rest //= count
            unit *= count
        pairs.append((source, target))
    return lax.ppermute(block, tuple(axes), pairs)


def f32(*shape):
    return jax.ShapeDtypeStruct(shape, jnp.float32)


def on_device(positions, charges, atom_types, type_table, live_count, exp_map):
    sizes = [lax.axis_size(axis) for axis in AXES]
    places = [lax.axis_index(axis) for axis in AXES]
    info = []
    for size, place in zip(sizes, places):
        info += [-place * BRICK, (size - place) * BRICK]
    for size, place in zip(sizes, places):
        odd = place % 2
        info += [odd, jnp.where(odd == 0, place > 0, place < size - 1).astype(jnp.int32)]
    info = jnp.stack(info).astype(jnp.int32)
    assert sizes[0] in (2, 4) and all(size in (2, 4, 8) for size in sizes)
    scale = FIT_GAIN * float(BRICK**3 * sizes[0] * sizes[1] * sizes[2])

    atoms, order = call(
        arrange_kernel,
        (f32(32, LANES), f32(TILES, LANES)),
        1 << 22,
        scratch=[pltpu.VMEM((SLOTS, LANES), jnp.float32), pltpu.VMEM((24, LANES), jnp.float32)],
        smem=2,
        n_in=5,
    )(
        type_table,
        live_count.reshape(1),
        positions,
        charges,
        atom_types,
    )
    given = jnp.pad(exp_map, ((0, 0), (0, 0), (0, LANES - BRICK)))
    own = atoms
    for step in range(STEPS):
        fields, rows = (2, 24) if step == 0 else (1, 16)
        planes = 8 * PLANES * fields
        field, *mine = call(
            functools.partial(splat_kernel, fields, rows),
            (f32(planes, LANES),) + (f32(rows + 8 * EDGE * fields, LANES),) * 2,
            1 << 26,
            scratch=[
                pltpu.VMEM((WIDE, LANES), jnp.float32),
                pltpu.VMEM((PLANES * WIDE, SLOTS), jnp.bfloat16),
                pltpu.VMEM((PLANES * WIDE, SLOTS), jnp.bfloat16),
                pltpu.VMEM((2 * WIDE, SLOTS), jnp.bfloat16),
            ],
            smem=1,
            n_in=1 + fields,
        )(*((info, own, given) if step == 0 else (info, own)))
        for number, axis in enumerate(AXES[:2]):
            count = 3**number
            field, *mine = call(
                functools.partial(merge_kernel, number, count, rows, fields),
                (f32(fields * PLANES, 8, LANES),) + (f32(3 * count * rows + 8 * HALF * fields, LANES),) * 2,
                1 << 20,
                smem=1,
                n_in=5,
            )(info, field.reshape(planes, LANES), mine[0], *both_sides(mine, axis))
        before = () if step == 0 else (tiles, exp_ext)
        planned = call(
            functools.partial(plan_kernel, rows, fields),
            (jax.ShapeDtypeStruct((BLOCKS, LANES), jnp.int32), f32(ROOM, 8, LANES))
            + (f32(PLANES, 8, LANES),) * fields
            + (f32(8, LANES),),
            1 << 22,
            scratch=[pltpu.VMEM((TILES, LANES, LANES), jnp.float32)],
            smem=1,
            n_in=6 + len(before),
        )(info, own, field.reshape(planes, LANES), mine[0], *both_sides(mine, AXES[2]), *before)
        if step == 0:
            listed, tiles, evolved, exp_ext, sums = planned
        else:
            listed, tiles, evolved, sums = planned
        early = [across(sums, AXES[:1], [2])] if sizes[0] >= 4 else []
        radius = call(
            born_kernel,
            f32(TILES, LANES),
            1 << 33,
            scratch=[pltpu.VMEM((3, SLOTS, LANES), jnp.float32), pltpu.VMEM((SLOTS, LANES), jnp.float32)],
            smem=1,
            n_in=3,
        )(listed, tiles, own)
        sums = functools.reduce(jnp.add, early, sums)
        line = jnp.concatenate([radius, sums])
        flips = (
            [(("gy",), (2,)), (("gx", "gy"), (1, 2))] if sizes[1] >= 4 else [],
            [(("gy",), (4,)), (("gy",), (5,))] if sizes[1] >= 8 else [],
            [(("gz",), (2,)), (("gz",), (3,))] if sizes[2] >= 4 else [],
        )
        for number, axis in enumerate(AXES):
            count = 3**number
            span = count * TILES
            others = [across(sums, *flip) for flip in flips[number]]
            near = both_sides((line, line), axis)
            if number == 2:
                sums = functools.reduce(jnp.add, others, sums + near[0][span:])
                break
            line, sums = call(
                functools.partial(radius_merge_kernel, number, count),
                (f32(3 * span + 8, LANES), f32(8, LANES)),
                1 << 20,
                smem=1,
                n_in=4 + len(others),
            )(info, line, *near, *others)
        pair = call(
            gb_kernel,
            f32(3 * TILES, LANES),
            1 << 34,
            scratch=[
                pltpu.VMEM((5, SLOTS, LANES), jnp.float32),
                pltpu.VMEM((3, SLOTS, LANES), jnp.float32),
                pltpu.VMEM((ROOM, 2, LANES), jnp.float32),
            ],
            smem=2,
            n_in=8,
        )(info, listed, tiles, own, radius, line, *near)
        if sizes[2] >= 8:
            sums = sums + across(sums, AXES[2:], [4])
        own, force = call(
            functools.partial(fit_kernel, scale, 1),
            (f32(32, LANES), f32(3 * TILES, LANES)),
            1 << 26,
            scratch=[
                pltpu.VMEM((PLANES * WIDE, LANES), jnp.bfloat16),
                pltpu.VMEM((LANES, 2 * LANES), jnp.bfloat16),
                pltpu.VMEM((PLANES * WIDE, 2 * LANES), jnp.float32),
                pltpu.VMEM((WIDE, LANES), jnp.float32),
                pltpu.VMEM((WIDE, LANES), jnp.float32),
            ],
            smem=1,
            n_in=6,
        )(info, own, evolved, exp_ext, sums, pair)
    displaced, final = call(
        restore_kernel,
        (f32(*positions.shape),) * 2,
        1 << 20,
        scratch=[pltpu.VMEM((24, LANES), jnp.float32)],
        n_in=4,
    )(order, own, atoms, force)
    model = evolved[5 : 5 + BRICK].reshape(BRICK, 8, 4, WIDE).transpose(0, 2, 1, 3).reshape(BRICK, WIDE, WIDE)
    model = model[:, PAD : PAD + BRICK, PAD : PAD + BRICK]
    return displaced, final, model


def solution(mesh):
    placed = (
        P(None, *AXES, None),
        P(*AXES, None),
        P(*AXES, None),
        P(),
        P(*AXES),
        P(*AXES),
    )
    return jax.shard_map(
        on_device,
        mesh=mesh,
        in_specs=placed,
        out_specs=(placed[0], placed[0], P(*AXES)),
        check_vma=False,
    )
```

```python
import functools
import math

import jax
import jax.numpy as jnp
from jax import lax
from jax.experimental import pallas as pl
from jax.experimental.pallas import tpu as pltpu
from jax.sharding import PartitionSpec as P

SPLAT_MARGIN = 3
BLUR_REACH = 2
STEPS = 2
CUTOFF = 10.0
EPSILON = 1e-06
STEP_SIZE = 1.0
FIT_GAIN = 0.2

AXES = ("gx", "gy", "gz")
SLOTS = 512
LANES = 128
TILES = SLOTS // LANES
BRICK = 16
PLANES = 26
HALF = PLANES // 2
EDGE = 10
PAD = 8
WIDE = 32
INTERPRET = False


def call(kernel, out_shape, cost, scratch=(), smem=0, n_in=0, vmem=48):
    specs = [pl.BlockSpec(memory_space=pltpu.SMEM)] * smem
    specs += [pl.BlockSpec(memory_space=pltpu.VMEM)] * (n_in - smem)
    many = isinstance(out_shape, (tuple, list))
    out_spec = pl.BlockSpec(memory_space=pltpu.VMEM)
    return pl.pallas_call(
        kernel,
        out_shape=out_shape,
        in_specs=specs,
        out_specs=[out_spec] * len(out_shape) if many else out_spec,
        scratch_shapes=list(scratch),
        cost_estimate=pl.CostEstimate(flops=cost, bytes_accessed=1 << 18, transcendentals=0),
        compiler_params=pltpu.CompilerParams(vmem_limit_bytes=vmem << 20),
        interpret=INTERPRET,
    )


def spread(row):
    return jnp.transpose(jnp.broadcast_to(row, (LANES, LANES)))


def gather_rows(acc):
    return jnp.sum(jnp.transpose(acc), axis=0, keepdims=True)


BLOCK = 32
BLOCKS = SLOTS // BLOCK
MANY = 16
FEW = 4
CELLS = 27
EMPTY = CELLS * TILES
ROOM = EMPTY + 4
FAR = 1e9


def three_parts(values):
    high = values.astype(jnp.bfloat16)
    rest = values - high.astype(jnp.float32)
    middle = rest.astype(jnp.bfloat16)
    return high, middle, (rest - middle.astype(jnp.float32)).astype(jnp.bfloat16)


def tiled(block, *index):
    row = block[(*index, 0, 0)] if index else block[0, 0]
    return jnp.concatenate([row[:, tile * LANES : (tile + 1) * LANES] for tile in range(TILES)], axis=0)


def arrange_kernel(table, live_count, given, charges, types, out, order, col, left):
    count = live_count[0]
    pos = jnp.concatenate([tiled(given, dim) for dim in range(3)], axis=0)
    slot = lax.broadcasted_iota(jnp.int32, (TILES, LANES), 0) * LANES
    slot = slot + lax.broadcasted_iota(jnp.int32, (TILES, LANES), 1)
    living = slot < count
    alive = jnp.where(living, 1.0, 0.0)
    kinds = tiled(types)
    props = []
    for row in range(3):
        value = jnp.zeros((TILES, LANES), jnp.float32)
        for kind in range(table.shape[1]):
            value = jnp.where(kinds == kind, table[row, kind], value)
        props.append(value)
    group = jnp.zeros((TILES, LANES), jnp.float32)
    sub = lax.broadcasted_iota(jnp.int32, (SLOTS, LANES), 0)
    lane = lax.broadcasted_iota(jnp.int32, (SLOTS, LANES), 1)
    for dim, size in ((0, 256), (1, 128), (2, 64), (0, 32)):
        key = group * 64.0 + jnp.where(living, pos[4 * dim : 4 * dim + 4, :], 40.0)
        for tile in range(TILES):
            col[tile * LANES : (tile + 1) * LANES, :] = spread(key[tile : tile + 1, :])
        ranks = []
        for tile in range(TILES):
            row = key[tile : tile + 1, :]
            other = col[...]
            ahead = (other < row) | ((other == row) & (sub < lane + tile * LANES))
            ranks.append(jnp.sum(jnp.where(ahead, 1.0, 0.0), axis=0, keepdims=True))
        rank = jnp.concatenate(ranks, axis=0)
        group = jnp.floor(rank * (1.0 / size))
    order[...] = rank
    values = [pos[0:4, :], pos[4:8, :], pos[8:12, :], tiled(charges) * alive]
    values += [props[1] * alive, props[2] * alive, props[0], alive]
    total = jnp.zeros((3 * len(values), SLOTS), jnp.float32)
    for tile in range(TILES):
        block = jnp.concatenate([value[tile : tile + 1, :] for value in values], axis=0)
        for part, piece in enumerate(three_parts(block)):
            left[8 * part : 8 * part + 8, :] = piece.astype(jnp.float32)
        hot = jnp.where(rank[tile : tile + 1, :] == sub.astype(jnp.float32), 1.0, 0.0).astype(jnp.bfloat16)
        dims = (((1,), (1,)), ((), ()))
        total = total + lax.dot_general(left[...].astype(jnp.bfloat16), hot, dims, preferred_element_type=jnp.float32)
    total = total[0:8] + total[8:16] + total[16:24]
    for channel in range(8):
        for tile in range(TILES):
            at = slice(4 * channel + tile, 4 * channel + tile + 1)
            out[at, :] = total[channel : channel + 1, tile * LANES : (tile + 1) * LANES]


def restore_kernel(order, moved, start, force, displaced, final, left):
    values = [moved[4 * d : 4 * d + 4, :] - start[4 * d : 4 * d + 4, :] for d in range(3)]
    values += [force[4 * d : 4 * d + 4, :] for d in range(3)]
    values += [jnp.zeros((TILES, LANES), jnp.float32)] * 2
    sub = lax.broadcasted_iota(jnp.int32, (LANES, LANES), 0).astype(jnp.float32)
    totals = [jnp.zeros((24, LANES), jnp.float32) for _ in range(TILES)]
    for source in range(TILES):
        block = jnp.concatenate([value[source : source + 1, :] for value in values], axis=0)
        for part, piece in enumerate(three_parts(block)):
            left[8 * part : 8 * part + 8, :] = piece.astype(jnp.float32)
        parts = left[...].astype(jnp.bfloat16)
        for tile in range(TILES):
            hot = jnp.where(order[tile : tile + 1, :] == sub + float(source * LANES), 1.0, 0.0)
            totals[tile] = totals[tile] + jnp.dot(parts, hot.astype(jnp.bfloat16), preferred_element_type=jnp.float32)
    for tile in range(TILES):
        total = totals[tile][0:8] + totals[tile][8:16] + totals[tile][16:24]
        for channel in range(6):
            out = displaced if channel < 3 else final
            out[channel % 3, 0, 0, :, tile * LANES : (tile + 1) * LANES] = total[channel : channel + 1, :]


def plan_kernel(rows, fields, *refs):
    info, own, field = refs[:3]
    sources = refs[3:6]
    if fields == 2:
        known = ()
        listed, tiles, evolved, given, sums, active = refs[6:]
    else:
        known = refs[6:7]
        given = refs[7]
        listed, tiles, evolved, sums, active = refs[8:]
    low, high = [], []
    for dim in range(3):
        living = own[28:32, :] > 0.0
        value = own[4 * dim : 4 * dim + 4, :]
        lo, hi = jnp.where(living, value, FAR), jnp.where(living, value, -FAR)
        for step in (1, 2, 4, 8, 16):
            lo = jnp.minimum(lo, pltpu.roll(lo, LANES - step, 1))
            hi = jnp.maximum(hi, pltpu.roll(hi, LANES - step, 1))
        low.append(lo)
        high.append(hi)
    active[...] = jnp.zeros_like(active)
    tiles[EMPTY:ROOM] = jnp.zeros((ROOM - EMPTY, 8, LANES), jnp.float32)
    after_first, valid = arrivals(info, 2)
    slots = (1, jnp.where(after_first, 2, 0), jnp.where(after_first, 0, 2))
    for source, slot, ok in zip(sources, slots, (None,) + valid):

        for cell in range(9):
            number = slot * 9 + cell
            sides = (cell % 3 - 1, cell // 3 - 1, slot - 1)
            block = source[cell * rows : cell * rows + rows, :]
            if ok is not None:
                block = block * ok
            if known:
                charge = [known[0][4 * number + tile, 4:5, :] for tile in range(TILES)]
                screen = [known[0][4 * number + tile, 3:4, :] for tile in range(TILES)]
                living = jnp.concatenate(screen, axis=0) > 0.0
            else:
                charge = [block[12 + tile : 13 + tile] for tile in range(TILES)]
                screen = [block[16 + tile : 17 + tile] for tile in range(TILES)]
                living = block[16:20] > 0.0
            near_low, near_high = [], []
            for dim in range(3):
                side = sides[dim]
                shift = float(side * BRICK) if isinstance(side, int) else side.astype(jnp.float32) * float(BRICK)
                moved = block[4 * dim : 4 * dim + 4] + shift
                near_low.append(jnp.min(jnp.where(living, moved, FAR), axis=1, keepdims=True))
                near_high.append(jnp.max(jnp.where(living, moved, -FAR), axis=1, keepdims=True))
                scaled = moved * (1.0 / CUTOFF)
                for tile in range(TILES):
                    tiles[4 * number + tile, dim : dim + 1, :] = scaled[tile : tile + 1, :]
            for tile in range(TILES):
                tiles[4 * number + tile, 3:4, :] = screen[tile]
                tiles[4 * number + tile, 4:5, :] = charge[tile]
            for tile in range(TILES):
                apart = jnp.zeros((TILES, LANES), jnp.float32)
                for dim in range(3):
                    lo, hi = low[dim][tile : tile + 1, :], high[dim][tile : tile + 1, :]
                    gap = jnp.maximum(jnp.maximum(near_low[dim] - hi, lo - near_high[dim]), 0.0)
                    apart = apart + gap * gap
                near = jnp.where(apart < CUTOFF * CUTOFF * 1.0001, 1.0, 0.0)
                active[tile, pl.ds(pl.multiple_of(4 * number, TILES), TILES), :] = near
    row = lax.broadcasted_iota(jnp.int32, (LANES, LANES), 0)
    lane = lax.broadcasted_iota(jnp.int32, (LANES, LANES), 1)
    before = jnp.where(lane < row, 1.0, 0.0).astype(jnp.bfloat16)
    for tile in range(TILES):
        flags = active[tile]
        ranks = jnp.dot(before, flags.astype(jnp.bfloat16), preferred_element_type=jnp.float32)
        for part in range(LANES // BLOCK):
            at = slice(part * BLOCK, part * BLOCK + 1)
            chosen = jnp.broadcast_to(flags[:, at], (LANES, LANES)) > 0.0
            place = jnp.broadcast_to(ranks[:, at], (LANES, LANES)).astype(jnp.int32)
            total = jnp.sum(jnp.where(chosen, 1, 0), axis=0, keepdims=True)
            entry = jnp.sum(jnp.where(chosen & (place == lane), row, 0), axis=0, keepdims=True)
            spot = lane[0:1, :]
            entry = jnp.where(spot < total, entry, EMPTY)
            block = tile * (LANES // BLOCK) + part
            listed[block : block + 1, :] = jnp.where(spot == LANES - 1, total, entry)
    lane = lax.broadcasted_iota(jnp.int32, (8, LANES), 1)
    sub = lane & (WIDE - 1)
    own_points = (lane >= WIDE) & (lane < 3 * WIDE) & (sub >= PAD) & (sub < PAD + BRICK)
    squares = jnp.zeros((8, LANES), jnp.float32)
    cross = squares
    target = squares
    adds = shift_masks(info, 2)
    evolved[...] = field[0 : 8 * PLANES, :].reshape(PLANES, 8, LANES)
    take_shares(2, adds, sources[1:], 9 * rows, evolved, 0)
    if fields == 2:
        given[...] = field[8 * PLANES : 16 * PLANES, :].reshape(PLANES, 8, LANES)
        take_shares(2, adds, sources[1:], 9 * rows + 8 * HALF, given, 0)
    for plane in range(PLANES):
        value = evolved[plane]
        if 5 <= plane < 5 + BRICK:
            value = jnp.where(own_points, value, 0.0)
            wanted = jnp.where(own_points, given[plane], 0.0)
            squares = squares + value * value
            cross = cross + value * wanted
            target = target + wanted * wanted
    sums[...] = jnp.zeros_like(sums)
    sums[0:1, :] = jnp.sum(squares, axis=0, keepdims=True)
    sums[1:2, :] = jnp.sum(cross, axis=0, keepdims=True)
    sums[2:3, :] = jnp.sum(target, axis=0, keepdims=True)


def arrivals(info, axis):
    after_first = info[6 + 2 * axis] == 0
    return after_first, (1.0, jnp.where(info[7 + 2 * axis] > 0, 1.0, 0.0))


def upper_half(axis):
    lane = lax.broadcasted_iota(jnp.int32, (8, LANES), 1)
    return (lane >= 64) if axis == 1 else ((lane & (WIDE - 1)) >= BRICK)


def shift_masks(info, axis):
    upper = upper_half(axis)
    after_first, valid = arrivals(info, axis)
    after_one = jnp.where(after_first, 1.0, 0.0)
    masks = []
    for after, ok in zip((after_one, 1.0 - after_one), valid):
        masks.append((jnp.where(upper, after * ok, 0.0), jnp.where(upper, 0.0, (1.0 - after) * ok)))
    return masks


def half_steps(axis):
    return (64, 64) if axis == 1 else (BRICK, LANES - BRICK)


def take_shares(axis, masks, sources, base, into, first):
    up, down = half_steps(axis)
    for plane in range(HALF):
        at = slice(base + 8 * plane, base + 8 * plane + 8)
        low = into[first + plane]
        high = into[first + HALF + plane]
        for (from_after, from_before), source in zip(masks, sources):
            share = source[at, :]
            low = low + pltpu.roll(share, up, 1) * from_after + share * from_before
            high = high + share * from_after + pltpu.roll(share, down, 1) * from_before
        into[first + plane] = low
        into[first + HALF + plane] = high


def give_shares(info, axis, field, first, outs, base):
    up, down = half_steps(axis)
    upper = upper_half(axis)
    after_first, _ = arrivals(info, axis)
    for plane in range(HALF):
        low, high = field[first + plane], field[first + HALF + plane]
        after = jnp.where(upper, high, pltpu.roll(low, down, 1))
        before = jnp.where(upper, pltpu.roll(high, up, 1), low)
        at = slice(base + 8 * plane, base + 8 * plane + 8)
        outs[0][at, :] = jnp.where(after_first, after, before)
        outs[1][at, :] = jnp.where(after_first, before, after)


def merge_kernel(axis, count, rows, fields, info, field, mine, first, second, merged, out_first, out_second):
    after_first, valid = arrivals(info, axis)
    span = count * rows
    slots = (jnp.where(after_first, 2 * span, 0), jnp.where(after_first, 0, 2 * span))
    for out in (out_first, out_second):
        out[span : 2 * span, :] = mine[0:span, :]
        for source, slot, ok in zip((first, second), slots, valid):
            out[pl.ds(pl.multiple_of(slot, 8), span), :] = source[0:span, :] * ok
    merged[...] = field[...].reshape(fields * PLANES, 8, LANES)
    for number in range(fields):
        if axis == 0:
            for source, slot, ok in zip((first, second), slots, valid):
                into = pl.ds(number * PLANES + jnp.where(slot > 0, BRICK, 0), EDGE)
                at = slice(span + 8 * EDGE * number, span + 8 * EDGE * (number + 1))
                merged[into] = merged[into] + source[at, :].reshape(EDGE, 8, LANES) * ok
        else:
            base = span + 8 * HALF * number
            take_shares(axis, shift_masks(info, axis), (first, second), base, merged, number * PLANES)
        base = 3 * span + 8 * HALF * number
        give_shares(info, axis + 1, merged, number * PLANES, (out_first, out_second), base)


def radius_merge_kernel(axis, count, info, mine, first, second, *refs):
    others, (out, sums) = refs[:-2], refs[-2:]
    after_first, _ = arrivals(info, axis)
    span = count * TILES
    out[span : 2 * span, :] = mine[0:span, :]
    slots = (jnp.where(after_first, 2 * span, 0), jnp.where(after_first, 0, 2 * span))
    for source, slot in zip((first, second), slots):
        out[pl.ds(pl.multiple_of(slot, 8), span), :] = source[0:span, :]
    total = mine[span : span + 8, :] + first[span : span + 8, :]
    for other in others:
        total = total + other[...]
    out[3 * span : 3 * span + 8, :] = total
    sums[...] = total


def over_tiles(count, some, carry):
    whole = count // MANY
    carry = lax.fori_loop(0, whole, lambda i, c: some(MANY, i * MANY, c), carry)
    rest = (count - whole * MANY + FEW - 1) // FEW
    return lax.fori_loop(0, rest, lambda i, c: some(FEW, whole * MANY + i * FEW, c), carry)


def born_kernel(listed, tiles, own, out, col, acc):
    for channel in range(3):
        for tile in range(TILES):
            row = own[4 * channel + tile : 4 * channel + tile + 1, :] * (1.0 / CUTOFF)
            col[channel, tile * LANES : (tile + 1) * LANES, :] = spread(row)

    def block(ib, carry):
        at = pl.ds(pl.multiple_of(ib * BLOCK, BLOCK), BLOCK)
        xi, yi, zi = col[0, at, :], col[1, at, :], col[2, at, :]

        def some(width, start, total):
            for k in range(width):
                tile = listed[ib, start + k]
                dx = xi - tiles[tile, 0:1, :]
                dy = yi - tiles[tile, 1:2, :]
                dz = zi - tiles[tile, 2:3, :]
                u = dx * dx + dy * dy + dz * dz
                s = jnp.maximum(1.0 - u, 0.0)
                e = jnp.exp2(u * (-CUTOFF * CUTOFF / 8.0 * math.log2(math.e)))
                total = total + (e * s) * (s * tiles[tile, 3:4, :])
            return total

        acc[at, :] = over_tiles(listed[ib, LANES - 1], some, jnp.zeros((BLOCK, LANES), jnp.float32))
        return carry

    lax.fori_loop(0, BLOCKS, block, 0)
    for tile in range(TILES):
        total = gather_rows(acc[tile * LANES : (tile + 1) * LANES, :]) - own[16 + tile : 17 + tile, :]
        out[tile : tile + 1, :] = own[24 + tile : 25 + tile, :] + total


def gb_kernel(info, listed, tiles, own, own_radius, mine, first, second, out, col, acc, rows):
    for tile in range(TILES):
        at = slice(tile * LANES, (tile + 1) * LANES)
        for channel in range(3):
            row = own[4 * channel + tile : 4 * channel + tile + 1, :] * (1.0 / CUTOFF)
            col[channel, at, :] = spread(row)
        radius = spread(own_radius[tile : tile + 1, :] * (1.0 / CUTOFF))
        col[3, at, :] = radius
        col[4, at, :] = (-0.5 * math.log2(math.e)) / radius
    rows[EMPTY:ROOM] = jnp.ones((ROOM - EMPTY, 2, LANES), jnp.float32)

    after_first, _ = arrivals(info, 2)
    slots = (1, jnp.where(after_first, 2, 0), jnp.where(after_first, 0, 2))
    for source, slot in zip((mine, first, second), slots):
        for cell in range(9):
            radius = source[TILES * cell : TILES * cell + TILES, :] * (1.0 / CUTOFF)
            half = 0.5 / radius
            for tile in range(TILES):
                rows[slot * 36 + 4 * cell + tile, 0:1, :] = radius[tile : tile + 1, :]
                rows[slot * 36 + 4 * cell + tile, 1:2, :] = half[tile : tile + 1, :]

    def block(ib, carry):
        at = pl.ds(pl.multiple_of(ib * BLOCK, BLOCK), BLOCK)
        xi, yi, zi = col[0, at, :], col[1, at, :], col[2, at, :]
        ri, ai = col[3, at, :], col[4, at, :]

        def some(width, start, force):
            fx, fy, fz = force
            for k in range(width):
                tile = listed[ib, start + k]
                dx = xi - tiles[tile, 0:1, :]
                dy = yi - tiles[tile, 1:2, :]
                dz = zi - tiles[tile, 2:3, :]
                u = dx * dx + dy * dy + dz * dz
                s = jnp.maximum(1.0 - u, 0.0)
                e = jnp.exp2(u * (ai * rows[tile, 1:2, :]))
                inv = lax.rsqrt(u + (ri * rows[tile, 0:1, :]) * e)
                t = s * inv
                m = (tiles[tile, 4:5, :] * t) * (16.0 + (t * inv) * (4.0 - e))
                fx = fx + m * dx
                fy = fy + m * dy
                fz = fz + m * dz
            return fx, fy, fz

        zero = jnp.zeros((BLOCK, LANES), jnp.float32)
        force = over_tiles(listed[ib, LANES - 1], some, (zero, zero, zero))
        for channel in range(3):
            acc[channel, at, :] = force[channel]
        return carry

    lax.fori_loop(0, BLOCKS, block, 0)
    for channel in range(3):
        for tile in range(TILES):
            total = gather_rows(acc[channel, tile * LANES : (tile + 1) * LANES, :])
            out[4 * channel + tile : 4 * channel + tile + 1, :] = total


def kernel_weights(reach):
    values = [math.exp(-0.5 * (index - reach) ** 2) for index in range(2 * reach + 1)]
    whole = sum(values)
    return [value / whole for value in values]


TAPS = kernel_weights(BLUR_REACH)


def blurred(values):
    rows = values.shape[0]
    near = pltpu.roll(values, 1, 0) + pltpu.roll(values, rows - 1, 0)
    far = pltpu.roll(values, 2, 0) + pltpu.roll(values, rows - 2, 0)
    return TAPS[2] * values + TAPS[1] * near + TAPS[0] * far


def profiles(row, side, base, rows, low, high, slope):
    number = lax.broadcasted_iota(jnp.int32, (rows, LANES), 0) + base
    shift = side * BRICK
    inside = (number >= low) & (number < high)
    window = inside & (number >= shift - SPLAT_MARGIN) & (number < shift + BRICK + SPLAT_MARGIN)
    moved = row + (float(shift) if isinstance(shift, int) else shift.astype(jnp.float32))
    gap = number.astype(jnp.float32) - moved
    plain = jnp.where(window, jnp.exp(-0.5 * gap * gap), 0.0)
    margin = SPLAT_MARGIN + BLUR_REACH
    reached = inside & (number >= shift - margin) & (number < shift + BRICK + margin)
    first = jnp.where(reached, blurred(plain), 0.0)
    if not slope:
        return first
    return first, jnp.where(reached, blurred(gap * plain), 0.0)


def split(values):
    high = values.astype(jnp.bfloat16)
    return high, (values - high.astype(jnp.float32)).astype(jnp.bfloat16)


def splat_kernel(fields, rows, bounds, own, *refs):
    if fields == 2:
        given = refs[0]
    field, out_first, out_second, px, left_hi, left_lo, right = refs[fields - 1 :]
    for tile in range(TILES):
        lanes = slice(tile * LANES, (tile + 1) * LANES)
        z = profiles(own[8 + tile : 9 + tile, :], 0, -PAD, WIDE, bounds[4], bounds[5], False)
        z_hi, z_lo = split(z)
        right[0:WIDE, lanes] = z_hi
        right[WIDE : 2 * WIDE, lanes] = z_lo
        x = profiles(own[tile : tile + 1, :], 0, -PAD, WIDE, bounds[0], bounds[1], False)
        px[...] = x * own[20 + tile : 21 + tile, :]
        y = profiles(own[4 + tile : 5 + tile, :], 0, -PAD, WIDE, bounds[2], bounds[3], False)
        for plane in range(PLANES):
            at = slice(plane * WIDE, (plane + 1) * WIDE)
            hi, lo = split(px[plane + 3 : plane + 4, :] * y)
            left_hi[at, lanes] = hi
            left_lo[at, lanes] = lo
    weights = right[...]
    dims = (((1,), (1,)), ((), ()))
    placed = lax.dot_general(left_hi[...], weights, dims, preferred_element_type=jnp.float32)
    placed = placed + lax.dot_general(left_lo[...], weights, dims, preferred_element_type=jnp.float32)
    placed = placed[:, 0:WIDE] + placed[:, WIDE : 2 * WIDE]
    placed = placed.reshape(PLANES, 4, 8, WIDE)
    for plane in range(PLANES):
        parts = [placed[plane, k] for k in range(4)]
        field[8 * plane : 8 * plane + 8, :] = jnp.concatenate(parts, axis=1)
    if fields == 2:
        base = 8 * PLANES
        field[base : base + 8 * PLANES, :] = jnp.zeros((8 * PLANES, LANES), jnp.float32)
        for plane in range(BRICK):
            value = pltpu.roll(given[plane, 0:8, :], WIDE + PAD, 1) + pltpu.roll(given[plane, 8:16, :], 2 * WIDE + PAD, 1)
            field[base + 8 * (plane + 5) : base + 8 * (plane + 6), :] = value
    after_first, _ = arrivals(bounds, 0)
    starts = (jnp.where(after_first, 8 * BRICK, 0), jnp.where(after_first, 0, 8 * BRICK))
    for out, start in zip((out_first, out_second), starts):
        out[0:rows, :] = own[0:rows, :]
        for number in range(fields):
            off = pl.ds(pl.multiple_of(8 * PLANES * number + start, 8), 8 * EDGE)
            out[rows + 8 * EDGE * number : rows + 8 * EDGE * (number + 1), :] = field[off, :]


def fit_kernel(scale, parts, bounds, *refs):
    own, evolved, exp_ext, sums = refs[:4]
    gb = refs[4 : 4 + parts]
    moved, force, left, right, inner, px, pxs = refs[4 + parts :]
    squares = jnp.sum(sums[0:1, :], axis=1, keepdims=True)
    cross = jnp.sum(sums[1:2, :], axis=1, keepdims=True)
    target = jnp.sum(sums[2:3, :], axis=1, keepdims=True)
    norm = jnp.sqrt((squares + EPSILON) * (target + EPSILON))
    given_part = 1.0 / norm
    model_part = (cross / norm) / (squares + EPSILON)
    for plane in range(PLANES):
        s = exp_ext[plane] * given_part - evolved[plane] * model_part
        blocks = [s] + [pltpu.roll(s, LANES - WIDE * k, 1) for k in (1, 2, 3)]
        s = jnp.concatenate(blocks, axis=0)
        s = jnp.where(lax.broadcasted_iota(jnp.int32, (WIDE, LANES), 1) < WIDE, s, 0.0)
        hi = s.astype(jnp.bfloat16).astype(jnp.float32)
        lo = (s - hi).astype(jnp.bfloat16).astype(jnp.float32)
        packed = hi + pltpu.roll(lo, WIDE, 1) + pltpu.roll(hi, 2 * WIDE, 1)
        left[plane * WIDE : (plane + 1) * WIDE, :] = packed.astype(jnp.bfloat16)
    moved[3 * TILES :, :] = own[3 * TILES :, :]
    right[...] = jnp.zeros_like(right)
    for tile in range(TILES):
        z, zs = profiles(own[8 + tile : 9 + tile, :], 0, -PAD, WIDE, bounds[4], bounds[5], True)
        for part, values in enumerate((z, zs)):
            lanes = slice(part * LANES, (part + 1) * LANES)
            hi, lo = split(values)
            right[0:WIDE, lanes] = hi
            right[WIDE : 2 * WIDE, lanes] = hi
            right[2 * WIDE : 3 * WIDE, lanes] = lo
        inner[...] = jnp.dot(left[...], right[...], preferred_element_type=jnp.float32)
        x, xs = profiles(own[tile : tile + 1, :], 0, -PAD, WIDE, bounds[0], bounds[1], True)
        y, ys = profiles(own[4 + tile : 5 + tile, :], 0, -PAD, WIDE, bounds[2], bounds[3], True)
        px[...] = x
        pxs[...] = xs
        turned_x = jnp.zeros((WIDE, LANES), jnp.float32)
        plain = turned_x
        turned_z = turned_x
        for plane in range(PLANES):
            rows = slice(plane * WIDE, (plane + 1) * WIDE)
            at_x = px[plane + 3 : plane + 4, :]
            part = inner[rows, 0:LANES]
            turned_x = turned_x + pxs[plane + 3 : plane + 4, :] * part
            plain = plain + at_x * part
            turned_z = turned_z + at_x * inner[rows, LANES : 2 * LANES]
        weight = scale * own[20 + tile : 21 + tile, :]
        charge = -2.0 / (16.0 * CUTOFF * CUTOFF) * own[12 + tile : 13 + tile, :]
        sides = (turned_x * y, plain * ys, turned_z * y)
        for channel in range(3):
            at = slice(4 * channel + tile, 4 * channel + tile + 1)
            pair = gb[0][at, :]
            for other in gb[1:]:
                pair = pair + other[at, :]
            total = charge * pair + weight * jnp.sum(sides[channel], axis=0, keepdims=True)
            force[at, :] = total
            moved[at, :] = own[at, :] + STEP_SIZE * (own[28 + tile : 29 + tile, :] * total)


def partners(axis):
    count = lax.axis_size(axis)
    even = [(i, i ^ 1) for i in range(count)]
    odd = [(i, (i + 1 if i % 2 else i - 1) % count) for i in range(count)]
    return even, odd


def both_sides(blocks, axis):
    even, odd = partners(axis)
    return lax.ppermute(blocks[0], axis, even), lax.ppermute(blocks[1], axis, odd)


def across(block, axes, flips):
    counts = [lax.axis_size(axis) for axis in axes]
    pairs = []
    for source in range(math.prod(counts)):
        target, rest, unit = 0, source, 1
        for count, flip in reversed(list(zip(counts, flips))):
            target += (rest % count ^ flip) * unit
            rest //= count
            unit *= count
        pairs.append((source, target))
    return lax.ppermute(block, tuple(axes), pairs)


def f32(*shape):
    return jax.ShapeDtypeStruct(shape, jnp.float32)


def on_device(positions, charges, atom_types, type_table, live_count, exp_map):
    sizes = [lax.axis_size(axis) for axis in AXES]
    places = [lax.axis_index(axis) for axis in AXES]
    info = []
    for size, place in zip(sizes, places):
        info += [-place * BRICK, (size - place) * BRICK]
    for size, place in zip(sizes, places):
        odd = place % 2
        info += [odd, jnp.where(odd == 0, place > 0, place < size - 1).astype(jnp.int32)]
    info = jnp.stack(info).astype(jnp.int32)
    assert sizes[0] in (2, 4) and all(size in (2, 4, 8) for size in sizes)
    scale = FIT_GAIN * float(BRICK**3 * sizes[0] * sizes[1] * sizes[2])

    atoms, order = call(
        arrange_kernel,
        (f32(32, LANES), f32(TILES, LANES)),
        1 << 22,
        scratch=[pltpu.VMEM((SLOTS, LANES), jnp.float32), pltpu.VMEM((24, LANES), jnp.float32)],
        smem=2,
        n_in=5,
    )(
        type_table,
        live_count.reshape(1),
        positions,
        charges,
        atom_types,
    )
    given = jnp.pad(exp_map, ((0, 0), (0, 0), (0, LANES - BRICK)))
    own = atoms
    for step in range(STEPS):
        fields, rows = (2, 24) if step == 0 else (1, 16)
        planes = 8 * PLANES * fields
        field, *mine = call(
            functools.partial(splat_kernel, fields, rows),
            (f32(planes, LANES),) + (f32(rows + 8 * EDGE * fields, LANES),) * 2,
            1 << 26,
            scratch=[
                pltpu.VMEM((WIDE, LANES), jnp.float32),
                pltpu.VMEM((PLANES * WIDE, SLOTS), jnp.bfloat16),
                pltpu.VMEM((PLANES * WIDE, SLOTS), jnp.bfloat16),
                pltpu.VMEM((2 * WIDE, SLOTS), jnp.bfloat16),
            ],
            smem=1,
            n_in=1 + fields,
        )(*((info, own, given) if step == 0 else (info, own)))
        for number, axis in enumerate(AXES[:2]):
            count = 3**number
            field, *mine = call(
                functools.partial(merge_kernel, number, count, rows, fields),
                (f32(fields * PLANES, 8, LANES),) + (f32(3 * count * rows + 8 * HALF * fields, LANES),) * 2,
                1 << 20,
                smem=1,
                n_in=5,
            )(info, field.reshape(planes, LANES), mine[0], *both_sides(mine, axis))
        before = () if step == 0 else (tiles, exp_ext)
        planned = call(
            functools.partial(plan_kernel, rows, fields),
            (jax.ShapeDtypeStruct((BLOCKS, LANES), jnp.int32), f32(ROOM, 8, LANES))
            + (f32(PLANES, 8, LANES),) * fields
            + (f32(8, LANES),),
            1 << 22,
            scratch=[pltpu.VMEM((TILES, LANES, LANES), jnp.float32)],
            smem=1,
            n_in=6 + len(before),
        )(info, own, field.reshape(planes, LANES), mine[0], *both_sides(mine, AXES[2]), *before)
        if step == 0:
            listed, tiles, evolved, exp_ext, sums = planned
        else:
            listed, tiles, evolved, sums = planned
        early = [across(sums, AXES[:1], [2])] if sizes[0] >= 4 else []
        radius = call(
            born_kernel,
            f32(TILES, LANES),
            1 << 33,
            scratch=[pltpu.VMEM((3, SLOTS, LANES), jnp.float32), pltpu.VMEM((SLOTS, LANES), jnp.float32)],
            smem=1,
            n_in=3,
        )(listed, tiles, own)
        sums = functools.reduce(jnp.add, early, sums)
        line = jnp.concatenate([radius, sums])
        flips = (
            [(("gy",), (4,)), (("gx", "gy"), (1, 4))] if sizes[1] >= 8 else [],
            [(("gy",), (2,)), (("gy",), (3,))] if sizes[1] >= 4 else [],
            [(("gz",), (2,)), (("gz",), (3,))] if sizes[2] >= 4 else [],
        )
        for number, axis in enumerate(AXES):
            count = 3**number
            span = count * TILES
            others = [across(sums, *flip) for flip in flips[number]]
            near = both_sides((line, line), axis)
            if number == 2:
                sums = functools.reduce(jnp.add, others, sums + near[0][span:])
                break
            line, sums = call(
                functools.partial(radius_merge_kernel, number, count),
                (f32(3 * span + 8, LANES), f32(8, LANES)),
                1 << 20,
                smem=1,
                n_in=4 + len(others),
            )(info, line, *near, *others)
        pair = call(
            gb_kernel,
            f32(3 * TILES, LANES),
            1 << 34,
            scratch=[
                pltpu.VMEM((5, SLOTS, LANES), jnp.float32),
                pltpu.VMEM((3, SLOTS, LANES), jnp.float32),
                pltpu.VMEM((ROOM, 2, LANES), jnp.float32),
            ],
            smem=2,
            n_in=8,
        )(info, listed, tiles, own, radius, line, *near)
        if sizes[2] >= 8:
            sums = sums + across(sums, AXES[2:], [7])
        own, force = call(
            functools.partial(fit_kernel, scale, 1),
            (f32(32, LANES), f32(3 * TILES, LANES)),
            1 << 26,
            scratch=[
                pltpu.VMEM((PLANES * WIDE, LANES), jnp.bfloat16),
                pltpu.VMEM((LANES, 2 * LANES), jnp.bfloat16),
                pltpu.VMEM((PLANES * WIDE, 2 * LANES), jnp.float32),
                pltpu.VMEM((WIDE, LANES), jnp.float32),
                pltpu.VMEM((WIDE, LANES), jnp.float32),
            ],
            smem=1,
            n_in=6,
        )(info, own, evolved, exp_ext, sums, pair)
    displaced, final = call(
        restore_kernel,
        (f32(*positions.shape),) * 2,
        1 << 20,
        scratch=[pltpu.VMEM((24, LANES), jnp.float32)],
        n_in=4,
    )(order, own, atoms, force)
    model = evolved[5 : 5 + BRICK].reshape(BRICK, 8, 4, WIDE).transpose(0, 2, 1, 3).reshape(BRICK, WIDE, WIDE)
    model = model[:, PAD : PAD + BRICK, PAD : PAD + BRICK]
    return displaced, final, model


def solution(mesh):
    placed = (
        P(None, *AXES, None),
        P(*AXES, None),
        P(*AXES, None),
        P(),
        P(*AXES),
        P(*AXES),
    )
    return jax.shard_map(
        on_device,
        mesh=mesh,
        in_specs=placed,
        out_specs=(placed[0], placed[0], P(*AXES)),
        check_vma=False,
    )
```

```python
import functools
import math

import jax
import jax.numpy as jnp
from jax import lax
from jax.experimental import pallas as pl
from jax.experimental.pallas import tpu as pltpu
from jax.sharding import PartitionSpec as P

SPLAT_MARGIN = 3
BLUR_REACH = 2
STEPS = 2
CUTOFF = 10.0
EPSILON = 1e-06
STEP_SIZE = 1.0
FIT_GAIN = 0.2

AXES = ("gx", "gy", "gz")
SLOTS = 512
LANES = 128
TILES = SLOTS // LANES
BRICK = 16
PLANES = 26
HALF = PLANES // 2
EDGE = 10
PAD = 8
WIDE = 32
INTERPRET = False


def call(kernel, out_shape, cost, scratch=(), smem=0, n_in=0, vmem=48):
    specs = [pl.BlockSpec(memory_space=pltpu.SMEM)] * smem
    specs += [pl.BlockSpec(memory_space=pltpu.VMEM)] * (n_in - smem)
    many = isinstance(out_shape, (tuple, list))
    out_spec = pl.BlockSpec(memory_space=pltpu.VMEM)
    return pl.pallas_call(
        kernel,
        out_shape=out_shape,
        in_specs=specs,
        out_specs=[out_spec] * len(out_shape) if many else out_spec,
        scratch_shapes=list(scratch),
        cost_estimate=pl.CostEstimate(flops=cost, bytes_accessed=1 << 18, transcendentals=0),
        compiler_params=pltpu.CompilerParams(vmem_limit_bytes=vmem << 20),
        interpret=INTERPRET,
    )


def spread(row):
    return jnp.transpose(jnp.broadcast_to(row, (LANES, LANES)))


def gather_rows(acc):
    return jnp.sum(jnp.transpose(acc), axis=0, keepdims=True)


BLOCK = 32
BLOCKS = SLOTS // BLOCK
MANY = 10
FEW = 4
CELLS = 27
EMPTY = CELLS * TILES
ROOM = EMPTY + 4
FAR = 1e9


def three_parts(values):
    high = values.astype(jnp.bfloat16)
    rest = values - high.astype(jnp.float32)
    middle = rest.astype(jnp.bfloat16)
    return high, middle, (rest - middle.astype(jnp.float32)).astype(jnp.bfloat16)


def tiled(block, *index):
    row = block[(*index, 0, 0)] if index else block[0, 0]
    return jnp.concatenate([row[:, tile * LANES : (tile + 1) * LANES] for tile in range(TILES)], axis=0)


def arrange_kernel(table, live_count, given, charges, types, out, order, col, left):
    count = live_count[0]
    pos = jnp.concatenate([tiled(given, dim) for dim in range(3)], axis=0)
    slot = lax.broadcasted_iota(jnp.int32, (TILES, LANES), 0) * LANES
    slot = slot + lax.broadcasted_iota(jnp.int32, (TILES, LANES), 1)
    living = slot < count
    alive = jnp.where(living, 1.0, 0.0)
    kinds = tiled(types)
    props = []
    for row in range(3):
        value = jnp.zeros((TILES, LANES), jnp.float32)
        for kind in range(table.shape[1]):
            value = jnp.where(kinds == kind, table[row, kind], value)
        props.append(value)
    group = jnp.zeros((TILES, LANES), jnp.float32)
    sub = lax.broadcasted_iota(jnp.int32, (SLOTS, LANES), 0)
    lane = lax.broadcasted_iota(jnp.int32, (SLOTS, LANES), 1)
    for dim, size in ((0, 256), (1, 128), (2, 64), (0, 32)):
        key = group * 64.0 + jnp.where(living, pos[4 * dim : 4 * dim + 4, :], 40.0)
        for tile in range(TILES):
            col[tile * LANES : (tile + 1) * LANES, :] = spread(key[tile : tile + 1, :])
        ranks = []
        for tile in range(TILES):
            row = key[tile : tile + 1, :]
            other = col[...]
            ahead = (other < row) | ((other == row) & (sub < lane + tile * LANES))
            ranks.append(jnp.sum(jnp.where(ahead, 1.0, 0.0), axis=0, keepdims=True))
        rank = jnp.concatenate(ranks, axis=0)
        group = jnp.floor(rank * (1.0 / size))
    order[...] = rank
    values = [pos[0:4, :], pos[4:8, :], pos[8:12, :], tiled(charges) * alive]
    values += [props[1] * alive, props[2] * alive, props[0], alive]
    total = jnp.zeros((3 * len(values), SLOTS), jnp.float32)
    for tile in range(TILES):
        block = jnp.concatenate([value[tile : tile + 1, :] for value in values], axis=0)
        for part, piece in enumerate(three_parts(block)):
            left[8 * part : 8 * part + 8, :] = piece.astype(jnp.float32)
        hot = jnp.where(rank[tile : tile + 1, :] == sub.astype(jnp.float32), 1.0, 0.0).astype(jnp.bfloat16)
        dims = (((1,), (1,)), ((), ()))
        total = total + lax.dot_general(left[...].astype(jnp.bfloat16), hot, dims, preferred_element_type=jnp.float32)
    total = total[0:8] + total[8:16] + total[16:24]
    for channel in range(8):
        for tile in range(TILES):
            at = slice(4 * channel + tile, 4 * channel + tile + 1)
            out[at, :] = total[channel : channel + 1, tile * LANES : (tile + 1) * LANES]


def restore_kernel(order, moved, start, force, displaced, final, left):
    values = [moved[4 * d : 4 * d + 4, :] - start[4 * d : 4 * d + 4, :] for d in range(3)]
    values += [force[4 * d : 4 * d + 4, :] for d in range(3)]
    values += [jnp.zeros((TILES, LANES), jnp.float32)] * 2
    sub = lax.broadcasted_iota(jnp.int32, (LANES, LANES), 0).astype(jnp.float32)
    totals = [jnp.zeros((24, LANES), jnp.float32) for _ in range(TILES)]
    for source in range(TILES):
        block = jnp.concatenate([value[source : source + 1, :] for value in values], axis=0)
        for part, piece in enumerate(three_parts(block)):
            left[8 * part : 8 * part + 8, :] = piece.astype(jnp.float32)
        parts = left[...].astype(jnp.bfloat16)
        for tile in range(TILES):
            hot = jnp.where(order[tile : tile + 1, :] == sub + float(source * LANES), 1.0, 0.0)
            totals[tile] = totals[tile] + jnp.dot(parts, hot.astype(jnp.bfloat16), preferred_element_type=jnp.float32)
    for tile in range(TILES):
        total = totals[tile][0:8] + totals[tile][8:16] + totals[tile][16:24]
        for channel in range(6):
            out = displaced if channel < 3 else final
            out[channel % 3, 0, 0, :, tile * LANES : (tile + 1) * LANES] = total[channel : channel + 1, :]


def block_boxes(own):
    low, high = [], []
    for dim in range(3):
        living = own[28:32, :] > 0.0
        value = own[4 * dim : 4 * dim + 4, :]
        lo, hi = jnp.where(living, value, FAR), jnp.where(living, value, -FAR)
        for step in (1, 2, 4, 8, 16):
            lo = jnp.minimum(lo, pltpu.roll(lo, LANES - step, 1))
            hi = jnp.maximum(hi, pltpu.roll(hi, LANES - step, 1))
        low.append(lo)
        high.append(hi)
    return low, high


def enter_cells(boxes, source, rows, slot, ok, known, tiles, active):
    low, high = boxes
    for cell in range(9):
        number = slot * 9 + cell
        sides = (cell % 3 - 1, cell // 3 - 1, slot - 1)
        block = source[cell * rows : cell * rows + rows, :]
        if ok is not None:
            block = block * ok
        if known:
            charge = [known[0][4 * number + tile, 4:5, :] for tile in range(TILES)]
            screen = [known[0][4 * number + tile, 3:4, :] for tile in range(TILES)]
            living = jnp.concatenate(screen, axis=0) > 0.0
        else:
            charge = [block[12 + tile : 13 + tile] for tile in range(TILES)]
            screen = [block[16 + tile : 17 + tile] for tile in range(TILES)]
            living = block[16:20] > 0.0
        near_low, near_high = [], []
        for dim in range(3):
            side = sides[dim]
            shift = float(side * BRICK) if isinstance(side, int) else side.astype(jnp.float32) * float(BRICK)
            moved = block[4 * dim : 4 * dim + 4] + shift
            near_low.append(jnp.min(jnp.where(living, moved, FAR), axis=1, keepdims=True))
            near_high.append(jnp.max(jnp.where(living, moved, -FAR), axis=1, keepdims=True))
            scaled = moved * (1.0 / CUTOFF)
            for tile in range(TILES):
                tiles[4 * number + tile, dim : dim + 1, :] = scaled[tile : tile + 1, :]
        for tile in range(TILES):
            tiles[4 * number + tile, 3:4, :] = screen[tile]
            tiles[4 * number + tile, 4:5, :] = charge[tile]
        if active is None:
            continue
        for tile in range(TILES):
            apart = jnp.zeros((TILES, LANES), jnp.float32)
            for dim in range(3):
                lo, hi = low[dim][tile : tile + 1, :], high[dim][tile : tile + 1, :]
                gap = jnp.maximum(jnp.maximum(near_low[dim] - hi, lo - near_high[dim]), 0.0)
                apart = apart + gap * gap
            near = jnp.where(apart < CUTOFF * CUTOFF * 1.0001, 1.0, 0.0)
            active[tile, pl.ds(pl.multiple_of(4 * number, TILES), TILES), :] = near


def write_lists(active, listed):
    row = lax.broadcasted_iota(jnp.int32, (LANES, LANES), 0)
    lane = lax.broadcasted_iota(jnp.int32, (LANES, LANES), 1)
    before = jnp.where(lane < row, 1.0, 0.0).astype(jnp.bfloat16)
    for tile in range(TILES):
        flags = active[tile]
        ranks = jnp.dot(before, flags.astype(jnp.bfloat16), preferred_element_type=jnp.float32)
        for part in range(LANES // BLOCK):
            at = slice(part * BLOCK, part * BLOCK + 1)
            chosen = jnp.broadcast_to(flags[:, at], (LANES, LANES)) > 0.0
            place = jnp.broadcast_to(ranks[:, at], (LANES, LANES)).astype(jnp.int32)
            total = jnp.sum(jnp.where(chosen, 1, 0), axis=0, keepdims=True)
            entry = jnp.sum(jnp.where(chosen & (place == lane), row, 0), axis=0, keepdims=True)
            spot = lane[0:1, :]
            entry = jnp.where(spot < total, entry, EMPTY)
            block = tile * (LANES // BLOCK) + part
            listed[block : block + 1, :] = jnp.where(spot == LANES - 1, total, entry)


def plane_plan_kernel(rows, own, mine, *refs):
    known, (listed, tiles, active) = refs[:-3], refs[-3:]
    active[...] = jnp.zeros_like(active)
    tiles[EMPTY:ROOM] = jnp.zeros((ROOM - EMPTY, 8, LANES), jnp.float32)
    enter_cells(block_boxes(own), mine, rows, 1, None, known, tiles, active)
    write_lists(active, listed)


def plan_kernel(rows, fields, *refs):
    info, own, field = refs[:3]
    sources = refs[3:6]
    if fields == 2:
        known = ()
        listed, tiles, evolved, given, sums, active = refs[6:]
    else:
        known = refs[6:7]
        given = refs[7]
        listed, tiles, evolved, sums, active = refs[8:]
    active[...] = jnp.zeros_like(active)
    tiles[EMPTY:ROOM] = jnp.zeros((ROOM - EMPTY, 8, LANES), jnp.float32)
    boxes = block_boxes(own)
    after_first, valid = arrivals(info, 2)
    slots = (1, jnp.where(after_first, 2, 0), jnp.where(after_first, 0, 2))
    for source, slot, ok in zip(sources, slots, (None,) + valid):
        enter_cells(boxes, source, rows, slot, ok, known, tiles, None if ok is None else active)
    write_lists(active, listed)
    lane = lax.broadcasted_iota(jnp.int32, (8, LANES), 1)
    sub = lane & (WIDE - 1)
    own_points = (lane >= WIDE) & (lane < 3 * WIDE) & (sub >= PAD) & (sub < PAD + BRICK)
    squares = jnp.zeros((8, LANES), jnp.float32)
    cross = squares
    target = squares
    adds = shift_masks(info, 2)
    evolved[...] = field[0 : 8 * PLANES, :].reshape(PLANES, 8, LANES)
    take_shares(2, adds, sources[1:], 9 * rows, evolved, 0)
    if fields == 2:
        given[...] = field[8 * PLANES : 16 * PLANES, :].reshape(PLANES, 8, LANES)
        take_shares(2, adds, sources[1:], 9 * rows + 8 * HALF, given, 0)
    for plane in range(PLANES):
        value = evolved[plane]
        if 5 <= plane < 5 + BRICK:
            value = jnp.where(own_points, value, 0.0)
            wanted = jnp.where(own_points, given[plane], 0.0)
            squares = squares + value * value
            cross = cross + value * wanted
            target = target + wanted * wanted
    sums[...] = jnp.zeros_like(sums)
    sums[0:1, :] = jnp.sum(squares, axis=0, keepdims=True)
    sums[1:2, :] = jnp.sum(cross, axis=0, keepdims=True)
    sums[2:3, :] = jnp.sum(target, axis=0, keepdims=True)


def arrivals(info, axis):
    after_first = info[6 + 2 * axis] == 0
    return after_first, (1.0, jnp.where(info[7 + 2 * axis] > 0, 1.0, 0.0))


def upper_half(axis):
    lane = lax.broadcasted_iota(jnp.int32, (8, LANES), 1)
    return (lane >= 64) if axis == 1 else ((lane & (WIDE - 1)) >= BRICK)


def shift_masks(info, axis):
    upper = upper_half(axis)
    after_first, valid = arrivals(info, axis)
    after_one = jnp.where(after_first, 1.0, 0.0)
    masks = []
    for after, ok in zip((after_one, 1.0 - after_one), valid):
        masks.append((jnp.where(upper, after * ok, 0.0), jnp.where(upper, 0.0, (1.0 - after) * ok)))
    return masks


def half_steps(axis):
    return (64, 64) if axis == 1 else (BRICK, LANES - BRICK)


def take_shares(axis, masks, sources, base, into, first):
    up, down = half_steps(axis)
    for plane in range(HALF):
        at = slice(base + 8 * plane, base + 8 * plane + 8)
        low = into[first + plane]
        high = into[first + HALF + plane]
        for (from_after, from_before), source in zip(masks, sources):
            share = source[at, :]
            low = low + pltpu.roll(share, up, 1) * from_after + share * from_before
            high = high + share * from_after + pltpu.roll(share, down, 1) * from_before
        into[first + plane] = low
        into[first + HALF + plane] = high


def give_shares(info, axis, field, first, outs, base):
    up, down = half_steps(axis)
    upper = upper_half(axis)
    after_first, _ = arrivals(info, axis)
    for plane in range(HALF):
        low, high = field[first + plane], field[first + HALF + plane]
        after = jnp.where(upper, high, pltpu.roll(low, down, 1))
        before = jnp.where(upper, pltpu.roll(high, up, 1), low)
        at = slice(base + 8 * plane, base + 8 * plane + 8)
        outs[0][at, :] = jnp.where(after_first, after, before)
        outs[1][at, :] = jnp.where(after_first, before, after)


def merge_kernel(axis, count, rows, fields, info, field, mine, first, second, merged, out_first, out_second):
    after_first, valid = arrivals(info, axis)
    span = count * rows
    slots = (jnp.where(after_first, 2 * span, 0), jnp.where(after_first, 0, 2 * span))
    for out in (out_first, out_second):
        out[span : 2 * span, :] = mine[0:span, :]
        for source, slot, ok in zip((first, second), slots, valid):
            out[pl.ds(pl.multiple_of(slot, 8), span), :] = source[0:span, :] * ok
    merged[...] = field[...].reshape(fields * PLANES, 8, LANES)
    for number in range(fields):
        if axis == 0:
            for source, slot, ok in zip((first, second), slots, valid):
                into = pl.ds(number * PLANES + jnp.where(slot > 0, BRICK, 0), EDGE)
                at = slice(span + 8 * EDGE * number, span + 8 * EDGE * (number + 1))
                merged[into] = merged[into] + source[at, :].reshape(EDGE, 8, LANES) * ok
        else:
            base = span + 8 * HALF * number
            take_shares(axis, shift_masks(info, axis), (first, second), base, merged, number * PLANES)
        base = 3 * span + 8 * HALF * number
        give_shares(info, axis + 1, merged, number * PLANES, (out_first, out_second), base)


def radius_merge_kernel(axis, count, info, mine, first, second, *refs):
    others, (out, sums) = refs[:-2], refs[-2:]
    after_first, _ = arrivals(info, axis)
    span = count * TILES
    out[span : 2 * span, :] = mine[0:span, :]
    slots = (jnp.where(after_first, 2 * span, 0), jnp.where(after_first, 0, 2 * span))
    for source, slot in zip((first, second), slots):
        out[pl.ds(pl.multiple_of(slot, 8), span), :] = source[0:span, :]
    total = mine[span : span + 8, :] + first[span : span + 8, :]
    for other in others:
        total = total + other[...]
    out[3 * span : 3 * span + 8, :] = total
    sums[...] = total


def over_tiles(count, some, carry):
    whole = count // MANY
    carry = lax.fori_loop(0, whole, lambda i, c: some(MANY, i * MANY, c), carry)
    rest = (count - whole * MANY + FEW - 1) // FEW
    return lax.fori_loop(0, rest, lambda i, c: some(FEW, whole * MANY + i * FEW, c), carry)


def born_kernel(listed, tiles, own, *refs):
    partial, (out, col, acc) = refs[:-3], refs[-3:]
    for channel in range(3):
        for tile in range(TILES):
            row = own[4 * channel + tile : 4 * channel + tile + 1, :] * (1.0 / CUTOFF)
            col[channel, tile * LANES : (tile + 1) * LANES, :] = spread(row)

    def block(ib, carry):
        at = pl.ds(pl.multiple_of(ib * BLOCK, BLOCK), BLOCK)
        xi, yi, zi = col[0, at, :], col[1, at, :], col[2, at, :]

        def some(width, start, total):
            for k in range(width):
                tile = listed[ib, start + k]
                dx = xi - tiles[tile, 0:1, :]
                dy = yi - tiles[tile, 1:2, :]
                dz = zi - tiles[tile, 2:3, :]
                u = dx * dx + dy * dy + dz * dz
                s = jnp.maximum(1.0 - u, 0.0)
                e = jnp.exp2(u * (-CUTOFF * CUTOFF / 8.0 * math.log2(math.e)))
                total = total + (e * s) * (s * tiles[tile, 3:4, :])
            return total

        acc[at, :] = over_tiles(listed[ib, LANES - 1], some, jnp.zeros((BLOCK, LANES), jnp.float32))
        return carry

    lax.fori_loop(0, BLOCKS, block, 0)
    for tile in range(TILES):
        total = gather_rows(acc[tile * LANES : (tile + 1) * LANES, :])
        if not partial:
            total = total - own[16 + tile : 17 + tile, :]
        else:
            total = own[24 + tile : 25 + tile, :] + (partial[0][tile : tile + 1, :] + total)
        out[tile : tile + 1, :] = total


def gb_kernel(info, plane_listed, rest_listed, tiles, own, own_radius, mine, first, second, out, col, acc, rows):
    for tile in range(TILES):
        at = slice(tile * LANES, (tile + 1) * LANES)
        for channel in range(3):
            row = own[4 * channel + tile : 4 * channel + tile + 1, :] * (1.0 / CUTOFF)
            col[channel, at, :] = spread(row)
        radius = spread(own_radius[tile : tile + 1, :] * (1.0 / CUTOFF))
        col[3, at, :] = radius
        col[4, at, :] = (-0.5 * math.log2(math.e)) / radius
    rows[EMPTY:ROOM] = jnp.ones((ROOM - EMPTY, 2, LANES), jnp.float32)

    after_first, _ = arrivals(info, 2)
    slots = (1, jnp.where(after_first, 2, 0), jnp.where(after_first, 0, 2))
    for source, slot in zip((mine, first, second), slots):
        for cell in range(9):
            radius = source[TILES * cell : TILES * cell + TILES, :] * (1.0 / CUTOFF)
            half = 0.5 / radius
            for tile in range(TILES):
                rows[slot * 36 + 4 * cell + tile, 0:1, :] = radius[tile : tile + 1, :]
                rows[slot * 36 + 4 * cell + tile, 1:2, :] = half[tile : tile + 1, :]

    def block(ib, carry):
        at = pl.ds(pl.multiple_of(ib * BLOCK, BLOCK), BLOCK)
        xi, yi, zi = col[0, at, :], col[1, at, :], col[2, at, :]
        ri, ai = col[3, at, :], col[4, at, :]

        def some(listed, width, start, force):
            fx, fy, fz = force
            for k in range(width):
                tile = listed[ib, start + k]
                dx = xi - tiles[tile, 0:1, :]
                dy = yi - tiles[tile, 1:2, :]
                dz = zi - tiles[tile, 2:3, :]
                u = dx * dx + dy * dy + dz * dz
                s = jnp.maximum(1.0 - u, 0.0)
                e = jnp.exp2(u * (ai * rows[tile, 1:2, :]))
                inv = lax.rsqrt(u + (ri * rows[tile, 0:1, :]) * e)
                t = s * inv
                m = (tiles[tile, 4:5, :] * t) * (16.0 + (t * inv) * (4.0 - e))
                fx = fx + m * dx
                fy = fy + m * dy
                fz = fz + m * dz
            return fx, fy, fz

        zero = jnp.zeros((BLOCK, LANES), jnp.float32)
        force = (zero, zero, zero)
        for listed in (plane_listed, rest_listed):
            force = over_tiles(listed[ib, LANES - 1], functools.partial(some, listed), force)
        for channel in range(3):
            acc[channel, at, :] = force[channel]
        return carry

    lax.fori_loop(0, BLOCKS, block, 0)
    for channel in range(3):
        for tile in range(TILES):
            total = gather_rows(acc[channel, tile * LANES : (tile + 1) * LANES, :])
            out[4 * channel + tile : 4 * channel + tile + 1, :] = total


def kernel_weights(reach):
    values = [math.exp(-0.5 * (index - reach) ** 2) for index in range(2 * reach + 1)]
    whole = sum(values)
    return [value / whole for value in values]


TAPS = kernel_weights(BLUR_REACH)


def blurred(values):
    rows = values.shape[0]
    near = pltpu.roll(values, 1, 0) + pltpu.roll(values, rows - 1, 0)
    far = pltpu.roll(values, 2, 0) + pltpu.roll(values, rows - 2, 0)
    return TAPS[2] * values + TAPS[1] * near + TAPS[0] * far


def profiles(row, side, base, rows, low, high, slope):
    number = lax.broadcasted_iota(jnp.int32, (rows, LANES), 0) + base
    shift = side * BRICK
    inside = (number >= low) & (number < high)
    window = inside & (number >= shift - SPLAT_MARGIN) & (number < shift + BRICK + SPLAT_MARGIN)
    moved = row + (float(shift) if isinstance(shift, int) else shift.astype(jnp.float32))
    gap = number.astype(jnp.float32) - moved
    plain = jnp.where(window, jnp.exp(-0.5 * gap * gap), 0.0)
    margin = SPLAT_MARGIN + BLUR_REACH
    reached = inside & (number >= shift - margin) & (number < shift + BRICK + margin)
    first = jnp.where(reached, blurred(plain), 0.0)
    if not slope:
        return first
    return first, jnp.where(reached, blurred(gap * plain), 0.0)


def split(values):
    high = values.astype(jnp.bfloat16)
    return high, (values - high.astype(jnp.float32)).astype(jnp.bfloat16)


def splat_kernel(fields, rows, bounds, own, *refs):
    if fields == 2:
        given = refs[0]
    field, out_first, out_second, px, left_hi, left_lo, right = refs[fields - 1 :]
    for tile in range(TILES):
        lanes = slice(tile * LANES, (tile + 1) * LANES)
        z = profiles(own[8 + tile : 9 + tile, :], 0, -PAD, WIDE, bounds[4], bounds[5], False)
        z_hi, z_lo = split(z)
        right[0:WIDE, lanes] = z_hi
        right[WIDE : 2 * WIDE, lanes] = z_lo
        x = profiles(own[tile : tile + 1, :], 0, -PAD, WIDE, bounds[0], bounds[1], False)
        px[...] = x * own[20 + tile : 21 + tile, :]
        y = profiles(own[4 + tile : 5 + tile, :], 0, -PAD, WIDE, bounds[2], bounds[3], False)
        for plane in range(PLANES):
            at = slice(plane * WIDE, (plane + 1) * WIDE)
            hi, lo = split(px[plane + 3 : plane + 4, :] * y)
            left_hi[at, lanes] = hi
            left_lo[at, lanes] = lo
    weights = right[...]
    dims = (((1,), (1,)), ((), ()))
    placed = lax.dot_general(left_hi[...], weights, dims, preferred_element_type=jnp.float32)
    placed = placed + lax.dot_general(left_lo[...], weights, dims, preferred_element_type=jnp.float32)
    placed = placed[:, 0:WIDE] + placed[:, WIDE : 2 * WIDE]
    placed = placed.reshape(PLANES, 4, 8, WIDE)
    for plane in range(PLANES):
        parts = [placed[plane, k] for k in range(4)]
        field[8 * plane : 8 * plane + 8, :] = jnp.concatenate(parts, axis=1)
    if fields == 2:
        base = 8 * PLANES
        field[base : base + 8 * PLANES, :] = jnp.zeros((8 * PLANES, LANES), jnp.float32)
        for plane in range(BRICK):
            value = pltpu.roll(given[plane, 0:8, :], WIDE + PAD, 1) + pltpu.roll(given[plane, 8:16, :], 2 * WIDE + PAD, 1)
            field[base + 8 * (plane + 5) : base + 8 * (plane + 6), :] = value
    after_first, _ = arrivals(bounds, 0)
    starts = (jnp.where(after_first, 8 * BRICK, 0), jnp.where(after_first, 0, 8 * BRICK))
    for out, start in zip((out_first, out_second), starts):
        out[0:rows, :] = own[0:rows, :]
        for number in range(fields):
            off = pl.ds(pl.multiple_of(8 * PLANES * number + start, 8), 8 * EDGE)
            out[rows + 8 * EDGE * number : rows + 8 * EDGE * (number + 1), :] = field[off, :]


def fit_kernel(scale, parts, bounds, *refs):
    own, evolved, exp_ext, sums = refs[:4]
    gb = refs[4 : 4 + parts]
    moved, force, left, right, inner, px, pxs = refs[4 + parts :]
    squares = jnp.sum(sums[0:1, :], axis=1, keepdims=True)
    cross = jnp.sum(sums[1:2, :], axis=1, keepdims=True)
    target = jnp.sum(sums[2:3, :], axis=1, keepdims=True)
    norm = jnp.sqrt((squares + EPSILON) * (target + EPSILON))
    given_part = 1.0 / norm
    model_part = (cross / norm) / (squares + EPSILON)
    for plane in range(PLANES):
        s = exp_ext[plane] * given_part - evolved[plane] * model_part
        blocks = [s] + [pltpu.roll(s, LANES - WIDE * k, 1) for k in (1, 2, 3)]
        s = jnp.concatenate(blocks, axis=0)
        s = jnp.where(lax.broadcasted_iota(jnp.int32, (WIDE, LANES), 1) < WIDE, s, 0.0)
        hi = s.astype(jnp.bfloat16).astype(jnp.float32)
        lo = (s - hi).astype(jnp.bfloat16).astype(jnp.float32)
        packed = hi + pltpu.roll(lo, WIDE, 1) + pltpu.roll(hi, 2 * WIDE, 1)
        left[plane * WIDE : (plane + 1) * WIDE, :] = packed.astype(jnp.bfloat16)
    moved[3 * TILES :, :] = own[3 * TILES :, :]
    right[...] = jnp.zeros_like(right)
    for tile in range(TILES):
        z, zs = profiles(own[8 + tile : 9 + tile, :], 0, -PAD, WIDE, bounds[4], bounds[5], True)
        for part, values in enumerate((z, zs)):
            lanes = slice(part * LANES, (part + 1) * LANES)
            hi, lo = split(values)
            right[0:WIDE, lanes] = hi
            right[WIDE : 2 * WIDE, lanes] = hi
            right[2 * WIDE : 3 * WIDE, lanes] = lo
        inner[...] = jnp.dot(left[...], right[...], preferred_element_type=jnp.float32)
        x, xs = profiles(own[tile : tile + 1, :], 0, -PAD, WIDE, bounds[0], bounds[1], True)
        y, ys = profiles(own[4 + tile : 5 + tile, :], 0, -PAD, WIDE, bounds[2], bounds[3], True)
        px[...] = x
        pxs[...] = xs
        turned_x = jnp.zeros((WIDE, LANES), jnp.float32)
        plain = turned_x
        turned_z = turned_x
        for plane in range(PLANES):
            rows = slice(plane * WIDE, (plane + 1) * WIDE)
            at_x = px[plane + 3 : plane + 4, :]
            part = inner[rows, 0:LANES]
            turned_x = turned_x + pxs[plane + 3 : plane + 4, :] * part
            plain = plain + at_x * part
            turned_z = turned_z + at_x * inner[rows, LANES : 2 * LANES]
        weight = scale * own[20 + tile : 21 + tile, :]
        charge = -2.0 / (16.0 * CUTOFF * CUTOFF) * own[12 + tile : 13 + tile, :]
        sides = (turned_x * y, plain * ys, turned_z * y)
        for channel in range(3):
            at = slice(4 * channel + tile, 4 * channel + tile + 1)
            pair = gb[0][at, :]
            for other in gb[1:]:
                pair = pair + other[at, :]
            total = charge * pair + weight * jnp.sum(sides[channel], axis=0, keepdims=True)
            force[at, :] = total
            moved[at, :] = own[at, :] + STEP_SIZE * (own[28 + tile : 29 + tile, :] * total)


def partners(axis):
    count = lax.axis_size(axis)
    even = [(i, i ^ 1) for i in range(count)]
    odd = [(i, (i + 1 if i % 2 else i - 1) % count) for i in range(count)]
    return even, odd


def both_sides(blocks, axis):
    even, odd = partners(axis)
    return lax.ppermute(blocks[0], axis, even), lax.ppermute(blocks[1], axis, odd)


def across(block, axes, flips):
    counts = [lax.axis_size(axis) for axis in axes]
    pairs = []
    for source in range(math.prod(counts)):
        target, rest, unit = 0, source, 1
        for count, flip in reversed(list(zip(counts, flips))):
            target += (rest % count ^ flip) * unit
            rest //= count
            unit *= count
        pairs.append((source, target))
    return lax.ppermute(block, tuple(axes), pairs)


def f32(*shape):
    return jax.ShapeDtypeStruct(shape, jnp.float32)


def on_device(positions, charges, atom_types, type_table, live_count, exp_map):
    sizes = [lax.axis_size(axis) for axis in AXES]
    places = [lax.axis_index(axis) for axis in AXES]
    info = []
    for size, place in zip(sizes, places):
        info += [-place * BRICK, (size - place) * BRICK]
    for size, place in zip(sizes, places):
        odd = place % 2
        info += [odd, jnp.where(odd == 0, place > 0, place < size - 1).astype(jnp.int32)]
    info = jnp.stack(info).astype(jnp.int32)
    assert sizes[0] in (2, 4) and all(size in (2, 4, 8) for size in sizes)
    scale = FIT_GAIN * float(BRICK**3 * sizes[0] * sizes[1] * sizes[2])

    atoms, order = call(
        arrange_kernel,
        (f32(32, LANES), f32(TILES, LANES)),
        1 << 22,
        scratch=[pltpu.VMEM((SLOTS, LANES), jnp.float32), pltpu.VMEM((24, LANES), jnp.float32)],
        smem=2,
        n_in=5,
    )(
        type_table,
        live_count.reshape(1),
        positions,
        charges,
        atom_types,
    )
    given = jnp.pad(exp_map, ((0, 0), (0, 0), (0, LANES - BRICK)))
    own = atoms
    for step in range(STEPS):
        fields, rows = (2, 24) if step == 0 else (1, 16)
        planes = 8 * PLANES * fields
        field, *mine = call(
            functools.partial(splat_kernel, fields, rows),
            (f32(planes, LANES),) + (f32(rows + 8 * EDGE * fields, LANES),) * 2,
            1 << 26,
            scratch=[
                pltpu.VMEM((WIDE, LANES), jnp.float32),
                pltpu.VMEM((PLANES * WIDE, SLOTS), jnp.bfloat16),
                pltpu.VMEM((PLANES * WIDE, SLOTS), jnp.bfloat16),
                pltpu.VMEM((2 * WIDE, SLOTS), jnp.bfloat16),
            ],
            smem=1,
            n_in=1 + fields,
        )(*((info, own, given) if step == 0 else (info, own)))
        for number, axis in enumerate(AXES[:2]):
            count = 3**number
            field, *mine = call(
                functools.partial(merge_kernel, number, count, rows, fields),
                (f32(fields * PLANES, 8, LANES),) + (f32(3 * count * rows + 8 * HALF * fields, LANES),) * 2,
                1 << 20,
                smem=1,
                n_in=5,
            )(info, field.reshape(planes, LANES), mine[0], *both_sides(mine, axis))
        before = () if step == 0 else (tiles, exp_ext)
        lists = jax.ShapeDtypeStruct((BLOCKS, LANES), jnp.int32)
        plane_listed, plane_tiles = call(
            functools.partial(plane_plan_kernel, rows),
            (lists, f32(ROOM, 8, LANES)),
            1 << 28,
            scratch=[pltpu.VMEM((TILES, LANES, LANES), jnp.float32)],
            n_in=2 + len(before[:1]),
        )(own, mine[0], *before[:1])
        born_scratch = [pltpu.VMEM((3, SLOTS, LANES), jnp.float32), pltpu.VMEM((SLOTS, LANES), jnp.float32)]
        partial = call(born_kernel, f32(TILES, LANES), 1 << 28, scratch=born_scratch, smem=1, n_in=3)(
            plane_listed, plane_tiles, own
        )
        planned = call(
            functools.partial(plan_kernel, rows, fields),
            (lists, f32(ROOM, 8, LANES))
            + (f32(PLANES, 8, LANES),) * fields
            + (f32(8, LANES),),
            1 << 22,
            scratch=[pltpu.VMEM((TILES, LANES, LANES), jnp.float32)],
            smem=1,
            n_in=6 + len(before),
        )(info, own, field.reshape(planes, LANES), mine[0], *both_sides(mine, AXES[2]), *before)
        if step == 0:
            listed, tiles, evolved, exp_ext, sums = planned
        else:
            listed, tiles, evolved, sums = planned
        early = [across(sums, AXES[:1], [2])] if sizes[0] >= 4 else []
        radius = call(born_kernel, f32(TILES, LANES), 1 << 32, scratch=born_scratch, smem=1, n_in=4)(
            listed, tiles, own, partial
        )
        sums = functools.reduce(jnp.add, early, sums)
        line = jnp.concatenate([radius, sums])
        flips = (
            [(("gy",), (4,)), (("gx", "gy"), (1, 4))] if sizes[1] >= 8 else [],
            [(("gy",), (2,)), (("gy",), (3,))] if sizes[1] >= 4 else [],
            [(("gz",), (2,)), (("gz",), (3,))] if sizes[2] >= 4 else [],
        )
        for number, axis in enumerate(AXES):
            count = 3**number
            span = count * TILES
            others = [across(sums, *flip) for flip in flips[number]]
            near = both_sides((line, line), axis)
            if number == 2:
                sums = functools.reduce(jnp.add, others, sums + near[0][span:])
                break
            line, sums = call(
                functools.partial(radius_merge_kernel, number, count),
                (f32(3 * span + 8, LANES), f32(8, LANES)),
                1 << 20,
                smem=1,
                n_in=4 + len(others),
            )(info, line, *near, *others)
        pair = call(
            gb_kernel,
            f32(3 * TILES, LANES),
            1 << 34,
            scratch=[
                pltpu.VMEM((5, SLOTS, LANES), jnp.float32),
                pltpu.VMEM((3, SLOTS, LANES), jnp.float32),
                pltpu.VMEM((ROOM, 2, LANES), jnp.float32),
            ],
            smem=3,
            n_in=9,
        )(info, plane_listed, listed, tiles, own, radius, line, *near)
        if sizes[2] >= 8:
            sums = sums + across(sums, AXES[2:], [7])
        own, force = call(
            functools.partial(fit_kernel, scale, 1),
            (f32(32, LANES), f32(3 * TILES, LANES)),
            1 << 26,
            scratch=[
                pltpu.VMEM((PLANES * WIDE, LANES), jnp.bfloat16),
                pltpu.VMEM((LANES, 2 * LANES), jnp.bfloat16),
                pltpu.VMEM((PLANES * WIDE, 2 * LANES), jnp.float32),
                pltpu.VMEM((WIDE, LANES), jnp.float32),
                pltpu.VMEM((WIDE, LANES), jnp.float32),
            ],
            smem=1,
            n_in=6,
        )(info, own, evolved, exp_ext, sums, pair)
    displaced, final = call(
        restore_kernel,
        (f32(*positions.shape),) * 2,
        1 << 20,
        scratch=[pltpu.VMEM((24, LANES), jnp.float32)],
        n_in=4,
    )(order, own, atoms, force)
    model = evolved[5 : 5 + BRICK].reshape(BRICK, 8, 4, WIDE).transpose(0, 2, 1, 3).reshape(BRICK, WIDE, WIDE)
    model = model[:, PAD : PAD + BRICK, PAD : PAD + BRICK]
    return displaced, final, model


def solution(mesh):
    placed = (
        P(None, *AXES, None),
        P(*AXES, None),
        P(*AXES, None),
        P(),
        P(*AXES),
        P(*AXES),
    )
    return jax.shard_map(
        on_device,
        mesh=mesh,
        in_specs=placed,
        out_specs=(placed[0], placed[0], P(*AXES)),
        check_vma=False,
    )
```

```python
import functools
import math

import jax
import jax.numpy as jnp
from jax import lax
from jax.experimental import pallas as pl
from jax.experimental.pallas import tpu as pltpu
from jax.sharding import PartitionSpec as P

SPLAT_MARGIN = 3
BLUR_REACH = 2
STEPS = 2
CUTOFF = 10.0
EPSILON = 1e-06
STEP_SIZE = 1.0
FIT_GAIN = 0.2

AXES = ("gx", "gy", "gz")
SLOTS = 512
LANES = 128
TILES = SLOTS // LANES
BRICK = 16
PLANES = 26
HALF = PLANES // 2
EDGE = 10
GIVEN_EDGE = 5
PAD = 8
WIDE = 32
INTERPRET = False


def call(kernel, out_shape, cost, scratch=(), smem=0, n_in=0, vmem=48):
    specs = [pl.BlockSpec(memory_space=pltpu.SMEM)] * smem
    specs += [pl.BlockSpec(memory_space=pltpu.VMEM)] * (n_in - smem)
    many = isinstance(out_shape, (tuple, list))
    out_spec = pl.BlockSpec(memory_space=pltpu.VMEM)
    return pl.pallas_call(
        kernel,
        out_shape=out_shape,
        in_specs=specs,
        out_specs=[out_spec] * len(out_shape) if many else out_spec,
        scratch_shapes=list(scratch),
        cost_estimate=pl.CostEstimate(flops=cost, bytes_accessed=1 << 18, transcendentals=0),
        compiler_params=pltpu.CompilerParams(vmem_limit_bytes=vmem << 20),
        interpret=INTERPRET,
    )


def spread(row):
    return jnp.transpose(jnp.broadcast_to(row, (LANES, LANES)))


def gather_rows(acc):
    return jnp.sum(jnp.transpose(acc), axis=0, keepdims=True)


BLOCK = 32
BLOCKS = SLOTS // BLOCK
MANY = 16
FEW = 4
CELLS = 27
EMPTY = CELLS * TILES
ROOM = EMPTY + 4
FAR = 1e9


def three_parts(values):
    high = values.astype(jnp.bfloat16)
    rest = values - high.astype(jnp.float32)
    middle = rest.astype(jnp.bfloat16)
    return high, middle, (rest - middle.astype(jnp.float32)).astype(jnp.bfloat16)


def tiled(block, *index):
    row = block[(*index, 0, 0)] if index else block[0, 0]
    return jnp.concatenate([row[:, tile * LANES : (tile + 1) * LANES] for tile in range(TILES)], axis=0)


def arrange_kernel(table, live_count, given, charges, types, out, order, col, left):
    count = live_count[0]
    pos = jnp.concatenate([tiled(given, dim) for dim in range(3)], axis=0)
    slot = lax.broadcasted_iota(jnp.int32, (TILES, LANES), 0) * LANES
    slot = slot + lax.broadcasted_iota(jnp.int32, (TILES, LANES), 1)
    living = slot < count
    alive = jnp.where(living, 1.0, 0.0)
    kinds = tiled(types)
    props = []
    for row in range(3):
        value = jnp.zeros((TILES, LANES), jnp.float32)
        for kind in range(table.shape[1]):
            value = jnp.where(kinds == kind, table[row, kind], value)
        props.append(value)
    group = jnp.zeros((TILES, LANES), jnp.float32)
    sub = lax.broadcasted_iota(jnp.int32, (SLOTS, LANES), 0)
    lane = lax.broadcasted_iota(jnp.int32, (SLOTS, LANES), 1)
    for dim, size in ((0, 256), (1, 128), (2, 64), (0, 32)):
        key = group * 64.0 + jnp.where(living, pos[4 * dim : 4 * dim + 4, :], 40.0)
        for tile in range(TILES):
            col[tile * LANES : (tile + 1) * LANES, :] = spread(key[tile : tile + 1, :])
        ranks = []
        for tile in range(TILES):
            row = key[tile : tile + 1, :]
            other = col[...]
            ahead = (other < row) | ((other == row) & (sub < lane + tile * LANES))
            ranks.append(jnp.sum(jnp.where(ahead, 1.0, 0.0), axis=0, keepdims=True))
        rank = jnp.concatenate(ranks, axis=0)
        group = jnp.floor(rank * (1.0 / size))
    order[...] = rank
    values = [pos[0:4, :], pos[4:8, :], pos[8:12, :], tiled(charges) * alive]
    values += [props[1] * alive, props[2] * alive, props[0], alive]
    total = jnp.zeros((3 * len(values), SLOTS), jnp.float32)
    for tile in range(TILES):
        block = jnp.concatenate([value[tile : tile + 1, :] for value in values], axis=0)
        for part, piece in enumerate(three_parts(block)):
            left[8 * part : 8 * part + 8, :] = piece.astype(jnp.float32)
        hot = jnp.where(rank[tile : tile + 1, :] == sub.astype(jnp.float32), 1.0, 0.0).astype(jnp.bfloat16)
        dims = (((1,), (1,)), ((), ()))
        total = total + lax.dot_general(left[...].astype(jnp.bfloat16), hot, dims, preferred_element_type=jnp.float32)
    total = total[0:8] + total[8:16] + total[16:24]
    for channel in range(8):
        for tile in range(TILES):
            at = slice(4 * channel + tile, 4 * channel + tile + 1)
            out[at, :] = total[channel : channel + 1, tile * LANES : (tile + 1) * LANES]


def restore_kernel(order, moved, start, force, displaced, final, left):
    values = [moved[4 * d : 4 * d + 4, :] - start[4 * d : 4 * d + 4, :] for d in range(3)]
    values += [force[4 * d : 4 * d + 4, :] for d in range(3)]
    values += [jnp.zeros((TILES, LANES), jnp.float32)] * 2
    sub = lax.broadcasted_iota(jnp.int32, (LANES, LANES), 0).astype(jnp.float32)
    totals = [jnp.zeros((24, LANES), jnp.float32) for _ in range(TILES)]
    for source in range(TILES):
        block = jnp.concatenate([value[source : source + 1, :] for value in values], axis=0)
        for part, piece in enumerate(three_parts(block)):
            left[8 * part : 8 * part + 8, :] = piece.astype(jnp.float32)
        parts = left[...].astype(jnp.bfloat16)
        for tile in range(TILES):
            hot = jnp.where(order[tile : tile + 1, :] == sub + float(source * LANES), 1.0, 0.0)
            totals[tile] = totals[tile] + jnp.dot(parts, hot.astype(jnp.bfloat16), preferred_element_type=jnp.float32)
    for tile in range(TILES):
        total = totals[tile][0:8] + totals[tile][8:16] + totals[tile][16:24]
        for channel in range(6):
            out = displaced if channel < 3 else final
            out[channel % 3, 0, 0, :, tile * LANES : (tile + 1) * LANES] = total[channel : channel + 1, :]


def plan_kernel(rows, fields, *refs):
    info, own, field = refs[:3]
    sources = refs[3:6]
    if fields == 2:
        known = ()
        listed, tiles, evolved, given, sums, active = refs[6:]
    else:
        known = refs[6:7]
        given = refs[7]
        listed, tiles, evolved, sums, model, active = refs[8:]
    low, high = [], []
    for dim in range(3):
        living = own[28:32, :] > 0.0
        value = own[4 * dim : 4 * dim + 4, :]
        lo, hi = jnp.where(living, value, FAR), jnp.where(living, value, -FAR)
        for step in (1, 2, 4, 8, 16):
            lo = jnp.minimum(lo, pltpu.roll(lo, LANES - step, 1))
            hi = jnp.maximum(hi, pltpu.roll(hi, LANES - step, 1))
        low.append(lo)
        high.append(hi)
    active[...] = jnp.zeros_like(active)
    tiles[EMPTY:ROOM] = jnp.zeros((ROOM - EMPTY, 8, LANES), jnp.float32)
    after_first, valid = arrivals(info, 2)
    slots = (1, jnp.where(after_first, 2, 0), jnp.where(after_first, 0, 2))
    for source, slot, ok in zip(sources, slots, (None,) + valid):

        for cell in range(9):
            number = slot * 9 + cell
            sides = (cell % 3 - 1, cell // 3 - 1, slot - 1)
            block = source[cell * rows : cell * rows + rows, :]
            if ok is not None:
                block = block * ok
            if known:
                charge = [known[0][4 * number + tile, 4:5, :] for tile in range(TILES)]
                screen = [known[0][4 * number + tile, 3:4, :] for tile in range(TILES)]
                living = jnp.concatenate(screen, axis=0) > 0.0
            else:
                charge = [block[12 + tile : 13 + tile] for tile in range(TILES)]
                screen = [block[16 + tile : 17 + tile] for tile in range(TILES)]
                living = block[16:20] > 0.0
            near_low, near_high = [], []
            for dim in range(3):
                side = sides[dim]
                shift = float(side * BRICK) if isinstance(side, int) else side.astype(jnp.float32) * float(BRICK)
                moved = block[4 * dim : 4 * dim + 4] + shift
                near_low.append(jnp.min(jnp.where(living, moved, FAR), axis=1, keepdims=True))
                near_high.append(jnp.max(jnp.where(living, moved, -FAR), axis=1, keepdims=True))
                scaled = moved * (1.0 / CUTOFF)
                for tile in range(TILES):
                    tiles[4 * number + tile, dim : dim + 1, :] = scaled[tile : tile + 1, :]
            for tile in range(TILES):
                tiles[4 * number + tile, 3:4, :] = screen[tile]
                tiles[4 * number + tile, 4:5, :] = charge[tile]
            for tile in range(TILES):
                apart = jnp.zeros((TILES, LANES), jnp.float32)
                for dim in range(3):
                    lo, hi = low[dim][tile : tile + 1, :], high[dim][tile : tile + 1, :]
                    gap = jnp.maximum(jnp.maximum(near_low[dim] - hi, lo - near_high[dim]), 0.0)
                    apart = apart + gap * gap
                near = jnp.where(apart < CUTOFF * CUTOFF * 1.0001, 1.0, 0.0)
                active[tile, pl.ds(pl.multiple_of(4 * number, TILES), TILES), :] = near
    row = lax.broadcasted_iota(jnp.int32, (LANES, LANES), 0)
    lane = lax.broadcasted_iota(jnp.int32, (LANES, LANES), 1)
    before = jnp.where(lane < row, 1.0, 0.0).astype(jnp.bfloat16)
    for tile in range(TILES):
        flags = active[tile]
        ranks = jnp.dot(before, flags.astype(jnp.bfloat16), preferred_element_type=jnp.float32)
        for part in range(LANES // BLOCK):
            at = slice(part * BLOCK, part * BLOCK + 1)
            chosen = jnp.broadcast_to(flags[:, at], (LANES, LANES)) > 0.0
            place = jnp.broadcast_to(ranks[:, at], (LANES, LANES)).astype(jnp.int32)
            total = jnp.sum(jnp.where(chosen, 1, 0), axis=0, keepdims=True)
            entry = jnp.sum(jnp.where(chosen & (place == lane), row, 0), axis=0, keepdims=True)
            spot = lane[0:1, :]
            entry = jnp.where(spot < total, entry, EMPTY)
            block = tile * (LANES // BLOCK) + part
            listed[block : block + 1, :] = jnp.where(spot == LANES - 1, total, entry)
    lane = lax.broadcasted_iota(jnp.int32, (8, LANES), 1)
    sub = lane & (WIDE - 1)
    own_points = (lane >= WIDE) & (lane < 3 * WIDE) & (sub >= PAD) & (sub < PAD + BRICK)
    squares = jnp.zeros((8, LANES), jnp.float32)
    cross = squares
    target = squares
    adds = shift_masks(info, 2)
    evolved[...] = field[0 : 8 * PLANES, :].reshape(PLANES, 8, LANES)
    take_shares(2, adds, sources[1:], 9 * rows, evolved, 0)
    if fields == 2:
        given[...] = field[8 * PLANES : 16 * PLANES, :].reshape(PLANES, 8, LANES)
        take_shares(2, adds, sources[1:], 9 * rows + 8 * HALF, given, 0)
    for plane in range(PLANES):
        value = evolved[plane]
        if fields == 1 and 5 <= plane < 5 + BRICK:
            for block in (1, 2):
                moved = pltpu.roll(value, LANES - WIDE * block - PAD, 1)
                model[plane - 5, 8 * block - 8 : 8 * block, :] = moved[:, 0:BRICK]
        if 5 <= plane < 5 + BRICK:
            value = jnp.where(own_points, value, 0.0)
            wanted = jnp.where(own_points, given[plane], 0.0)
            squares = squares + value * value
            cross = cross + value * wanted
            target = target + wanted * wanted
    sums[...] = jnp.zeros_like(sums)
    sums[0:1, :] = jnp.sum(squares, axis=0, keepdims=True)
    sums[1:2, :] = jnp.sum(cross, axis=0, keepdims=True)
    sums[2:3, :] = jnp.sum(target, axis=0, keepdims=True)


def arrivals(info, axis):
    after_first = info[6 + 2 * axis] == 0
    return after_first, (1.0, jnp.where(info[7 + 2 * axis] > 0, 1.0, 0.0))


def upper_half(axis):
    lane = lax.broadcasted_iota(jnp.int32, (8, LANES), 1)
    return (lane >= 64) if axis == 1 else ((lane & (WIDE - 1)) >= BRICK)


def shift_masks(info, axis):
    upper = upper_half(axis)
    after_first, valid = arrivals(info, axis)
    after_one = jnp.where(after_first, 1.0, 0.0)
    masks = []
    for after, ok in zip((after_one, 1.0 - after_one), valid):
        masks.append((jnp.where(upper, after * ok, 0.0), jnp.where(upper, 0.0, (1.0 - after) * ok)))
    return masks


def half_steps(axis):
    return (64, 64) if axis == 1 else (BRICK, LANES - BRICK)


def take_shares(axis, masks, sources, base, into, first):
    up, down = half_steps(axis)
    for plane in range(HALF):
        at = slice(base + 8 * plane, base + 8 * plane + 8)
        low = into[first + plane]
        high = into[first + HALF + plane]
        for (from_after, from_before), source in zip(masks, sources):
            share = source[at, :]
            low = low + pltpu.roll(share, up, 1) * from_after + share * from_before
            high = high + share * from_after + pltpu.roll(share, down, 1) * from_before
        into[first + plane] = low
        into[first + HALF + plane] = high


def give_shares(info, axis, field, first, outs, base):
    up, down = half_steps(axis)
    upper = upper_half(axis)
    after_first, _ = arrivals(info, axis)
    for plane in range(HALF):
        low, high = field[first + plane], field[first + HALF + plane]
        after = jnp.where(upper, high, pltpu.roll(low, down, 1))
        before = jnp.where(upper, pltpu.roll(high, up, 1), low)
        at = slice(base + 8 * plane, base + 8 * plane + 8)
        outs[0][at, :] = jnp.where(after_first, after, before)
        outs[1][at, :] = jnp.where(after_first, before, after)


def merge_kernel(axis, count, rows, fields, info, field, mine, first, second, merged, out_first, out_second):
    after_first, valid = arrivals(info, axis)
    span = count * rows
    slots = (jnp.where(after_first, 2 * span, 0), jnp.where(after_first, 0, 2 * span))
    for out in (out_first, out_second):
        out[span : 2 * span, :] = mine[0:span, :]
        for source, slot, ok in zip((first, second), slots, valid):
            out[pl.ds(pl.multiple_of(slot, 8), span), :] = source[0:span, :] * ok
    merged[...] = field[...].reshape(fields * PLANES, 8, LANES)
    for number in range(fields):
        if axis == 0:
            for source, slot, ok in zip((first, second), slots, valid):
                width = GIVEN_EDGE if number else EDGE
                into = pl.ds(number * PLANES + jnp.where(slot > 0, PLANES - width, 0), width)
                at = slice(span + 8 * EDGE * number, span + 8 * EDGE * number + 8 * width)
                merged[into] = merged[into] + source[at, :].reshape(width, 8, LANES) * ok
        else:
            base = span + 8 * HALF * number
            take_shares(axis, shift_masks(info, axis), (first, second), base, merged, number * PLANES)
        base = 3 * span + 8 * HALF * number
        give_shares(info, axis + 1, merged, number * PLANES, (out_first, out_second), base)


def radius_merge_kernel(axis, count, info, mine, first, second, *refs):
    others, (out, sums) = refs[:-2], refs[-2:]
    after_first, _ = arrivals(info, axis)
    span = count * TILES
    out[span : 2 * span, :] = mine[0:span, :]
    slots = (jnp.where(after_first, 2 * span, 0), jnp.where(after_first, 0, 2 * span))
    for source, slot in zip((first, second), slots):
        out[pl.ds(pl.multiple_of(slot, 8), span), :] = source[0:span, :]
    total = mine[span : span + 8, :] + first[span : span + 8, :]
    for other in others:
        total = total + other[...]
    out[3 * span : 3 * span + 8, :] = total
    sums[...] = total


def over_tiles(count, some, carry):
    whole = count // MANY
    carry = lax.fori_loop(0, whole, lambda i, c: some(MANY, i * MANY, c), carry)
    rest = (count - whole * MANY + FEW - 1) // FEW
    return lax.fori_loop(0, rest, lambda i, c: some(FEW, whole * MANY + i * FEW, c), carry)


def born_kernel(listed, tiles, own, out, col, acc):
    for channel in range(3):
        for tile in range(TILES):
            row = own[4 * channel + tile : 4 * channel + tile + 1, :] * (1.0 / CUTOFF)
            col[channel, tile * LANES : (tile + 1) * LANES, :] = spread(row)

    def block(ib, carry):
        at = pl.ds(pl.multiple_of(ib * BLOCK, BLOCK), BLOCK)
        xi, yi, zi = col[0, at, :], col[1, at, :], col[2, at, :]

        def some(width, start, total):
            for k in range(width):
                tile = listed[ib, start + k]
                dx = xi - tiles[tile, 0:1, :]
                dy = yi - tiles[tile, 1:2, :]
                dz = zi - tiles[tile, 2:3, :]
                u = dx * dx + dy * dy + dz * dz
                s = jnp.maximum(1.0 - u, 0.0)
                e = jnp.exp2(u * (-CUTOFF * CUTOFF / 8.0 * math.log2(math.e)))
                total = total + (e * s) * (s * tiles[tile, 3:4, :])
            return total

        acc[at, :] = over_tiles(listed[ib, LANES - 1], some, jnp.zeros((BLOCK, LANES), jnp.float32))
        return carry

    lax.fori_loop(0, BLOCKS, block, 0)
    for tile in range(TILES):
        total = gather_rows(acc[tile * LANES : (tile + 1) * LANES, :]) - own[16 + tile : 17 + tile, :]
        out[tile : tile + 1, :] = own[24 + tile : 25 + tile, :] + total


def gb_kernel(info, listed, tiles, own, own_radius, mine, first, second, out, col, acc, rows):
    for tile in range(TILES):
        at = slice(tile * LANES, (tile + 1) * LANES)
        for channel in range(3):
            row = own[4 * channel + tile : 4 * channel + tile + 1, :] * (1.0 / CUTOFF)
            col[channel, at, :] = spread(row)
        radius = spread(own_radius[tile : tile + 1, :] * (1.0 / CUTOFF))
        col[3, at, :] = radius
        col[4, at, :] = (-0.5 * math.log2(math.e)) / radius
    rows[EMPTY:ROOM] = jnp.ones((ROOM - EMPTY, 2, LANES), jnp.float32)

    after_first, _ = arrivals(info, 2)
    slots = (1, jnp.where(after_first, 2, 0), jnp.where(after_first, 0, 2))
    for source, slot in zip((mine, first, second), slots):
        for cell in range(9):
            radius = source[TILES * cell : TILES * cell + TILES, :] * (1.0 / CUTOFF)
            half = 0.5 / radius
            for tile in range(TILES):
                rows[slot * 36 + 4 * cell + tile, 0:1, :] = radius[tile : tile + 1, :]
                rows[slot * 36 + 4 * cell + tile, 1:2, :] = half[tile : tile + 1, :]

    def block(ib, carry):
        at = pl.ds(pl.multiple_of(ib * BLOCK, BLOCK), BLOCK)
        xi, yi, zi = col[0, at, :], col[1, at, :], col[2, at, :]
        ri, ai = col[3, at, :], col[4, at, :]

        def some(width, start, force):
            fx, fy, fz = force
            for k in range(width):
                tile = listed[ib, start + k]
                dx = xi - tiles[tile, 0:1, :]
                dy = yi - tiles[tile, 1:2, :]
                dz = zi - tiles[tile, 2:3, :]
                u = dx * dx + dy * dy + dz * dz
                s = jnp.maximum(1.0 - u, 0.0)
                e = jnp.exp2(u * (ai * rows[tile, 1:2, :]))
                inv = lax.rsqrt(u + (ri * rows[tile, 0:1, :]) * e)
                t = s * inv
                m = (tiles[tile, 4:5, :] * t) * (16.0 + (t * inv) * (4.0 - e))
                fx = fx + m * dx
                fy = fy + m * dy
                fz = fz + m * dz
            return fx, fy, fz

        zero = jnp.zeros((BLOCK, LANES), jnp.float32)
        force = over_tiles(listed[ib, LANES - 1], some, (zero, zero, zero))
        for channel in range(3):
            acc[channel, at, :] = force[channel]
        return carry

    lax.fori_loop(0, BLOCKS, block, 0)
    for channel in range(3):
        for tile in range(TILES):
            total = gather_rows(acc[channel, tile * LANES : (tile + 1) * LANES, :])
            out[4 * channel + tile : 4 * channel + tile + 1, :] = total


def kernel_weights(reach):
    values = [math.exp(-0.5 * (index - reach) ** 2) for index in range(2 * reach + 1)]
    whole = sum(values)
    return [value / whole for value in values]


TAPS = kernel_weights(BLUR_REACH)


def blurred(values):
    rows = values.shape[0]
    near = pltpu.roll(values, 1, 0) + pltpu.roll(values, rows - 1, 0)
    far = pltpu.roll(values, 2, 0) + pltpu.roll(values, rows - 2, 0)
    return TAPS[2] * values + TAPS[1] * near + TAPS[0] * far


def profiles(row, side, base, rows, low, high, slope):
    number = lax.broadcasted_iota(jnp.int32, (rows, LANES), 0) + base
    shift = side * BRICK
    inside = (number >= low) & (number < high)
    window = inside & (number >= shift - SPLAT_MARGIN) & (number < shift + BRICK + SPLAT_MARGIN)
    moved = row + (float(shift) if isinstance(shift, int) else shift.astype(jnp.float32))
    gap = number.astype(jnp.float32) - moved
    plain = jnp.where(window, jnp.exp(-0.5 * gap * gap), 0.0)
    margin = SPLAT_MARGIN + BLUR_REACH
    reached = inside & (number >= shift - margin) & (number < shift + BRICK + margin)
    first = jnp.where(reached, blurred(plain), 0.0)
    if not slope:
        return first
    return first, jnp.where(reached, blurred(gap * plain), 0.0)


def split(values):
    high = values.astype(jnp.bfloat16)
    return high, (values - high.astype(jnp.float32)).astype(jnp.bfloat16)


def splat_kernel(fields, rows, bounds, own, *refs):
    if fields == 2:
        given = refs[0]
    field, out_first, out_second, px, left_hi, left_lo, right = refs[fields - 1 :]
    for tile in range(TILES):
        lanes = slice(tile * LANES, (tile + 1) * LANES)
        z = profiles(own[8 + tile : 9 + tile, :], 0, -PAD, WIDE, bounds[4], bounds[5], False)
        z_hi, z_lo = split(z)
        right[0:WIDE, lanes] = z_hi
        right[WIDE : 2 * WIDE, lanes] = z_lo
        x = profiles(own[tile : tile + 1, :], 0, -PAD, WIDE, bounds[0], bounds[1], False)
        px[...] = x * own[20 + tile : 21 + tile, :]
        y = profiles(own[4 + tile : 5 + tile, :], 0, -PAD, WIDE, bounds[2], bounds[3], False)
        for plane in range(PLANES):
            at = slice(plane * WIDE, (plane + 1) * WIDE)
            hi, lo = split(px[plane + 3 : plane + 4, :] * y)
            left_hi[at, lanes] = hi
            left_lo[at, lanes] = lo
    weights = right[...]
    dims = (((1,), (1,)), ((), ()))
    placed = lax.dot_general(left_hi[...], weights, dims, preferred_element_type=jnp.float32)
    placed = placed + lax.dot_general(left_lo[...], weights, dims, preferred_element_type=jnp.float32)
    placed = placed[:, 0:WIDE] + placed[:, WIDE : 2 * WIDE]
    placed = placed.reshape(PLANES, 4, 8, WIDE)
    for plane in range(PLANES):
        parts = [placed[plane, k] for k in range(4)]
        field[8 * plane : 8 * plane + 8, :] = jnp.concatenate(parts, axis=1)
    if fields == 2:
        base = 8 * PLANES
        field[base : base + 8 * PLANES, :] = jnp.zeros((8 * PLANES, LANES), jnp.float32)
        for plane in range(BRICK):
            value = pltpu.roll(given[plane, 0:8, :], WIDE + PAD, 1) + pltpu.roll(given[plane, 8:16, :], 2 * WIDE + PAD, 1)
            field[base + 8 * (plane + 5) : base + 8 * (plane + 6), :] = value
    after_first, _ = arrivals(bounds, 0)
    for out, after in ((out_first, after_first), (out_second, jnp.logical_not(after_first))):
        out[0:rows, :] = own[0:rows, :]
        off = pl.ds(pl.multiple_of(jnp.where(after, 8 * BRICK, 0), 8), 8 * EDGE)
        out[rows : rows + 8 * EDGE, :] = field[off, :]
        if fields == 2:
            start = 8 * PLANES + jnp.where(after, 8 * BRICK, 8 * GIVEN_EDGE)
            off = pl.ds(pl.multiple_of(start, 8), 8 * GIVEN_EDGE)
            out[rows + 8 * EDGE :, :] = field[off, :]


def fit_kernel(scale, parts, bounds, *refs):
    own, evolved, exp_ext, sums = refs[:4]
    gb = refs[4 : 4 + parts]
    moved, force, left, right, inner, px, pxs = refs[4 + parts :]
    squares = jnp.sum(sums[0:1, :], axis=1, keepdims=True)
    cross = jnp.sum(sums[1:2, :], axis=1, keepdims=True)
    target = jnp.sum(sums[2:3, :], axis=1, keepdims=True)
    norm = jnp.sqrt((squares + EPSILON) * (target + EPSILON))
    given_part = 1.0 / norm
    model_part = (cross / norm) / (squares + EPSILON)
    for plane in range(PLANES):
        s = exp_ext[plane] * given_part - evolved[plane] * model_part
        blocks = [s] + [pltpu.roll(s, LANES - WIDE * k, 1) for k in (1, 2, 3)]
        s = jnp.concatenate(blocks, axis=0)
        s = jnp.where(lax.broadcasted_iota(jnp.int32, (WIDE, LANES), 1) < WIDE, s, 0.0)
        hi = s.astype(jnp.bfloat16).astype(jnp.float32)
        lo = (s - hi).astype(jnp.bfloat16).astype(jnp.float32)
        packed = hi + pltpu.roll(lo, WIDE, 1) + pltpu.roll(hi, 2 * WIDE, 1)
        left[plane * WIDE : (plane + 1) * WIDE, :] = packed.astype(jnp.bfloat16)
    moved[3 * TILES :, :] = own[3 * TILES :, :]
    right[...] = jnp.zeros_like(right)
    for tile in range(TILES):
        z, zs = profiles(own[8 + tile : 9 + tile, :], 0, -PAD, WIDE, bounds[4], bounds[5], True)
        for part, values in enumerate((z, zs)):
            lanes = slice(part * LANES, (part + 1) * LANES)
            hi, lo = split(values)
            right[0:WIDE, lanes] = hi
            right[WIDE : 2 * WIDE, lanes] = hi
            right[2 * WIDE : 3 * WIDE, lanes] = lo
        inner[...] = jnp.dot(left[...], right[...], preferred_element_type=jnp.float32)
        x, xs = profiles(own[tile : tile + 1, :], 0, -PAD, WIDE, bounds[0], bounds[1], True)
        y, ys = profiles(own[4 + tile : 5 + tile, :], 0, -PAD, WIDE, bounds[2], bounds[3], True)
        px[...] = x
        pxs[...] = xs
        turned_x = jnp.zeros((WIDE, LANES), jnp.float32)
        plain = turned_x
        turned_z = turned_x
        for plane in range(PLANES):
            rows = slice(plane * WIDE, (plane + 1) * WIDE)
            at_x = px[plane + 3 : plane + 4, :]
            part = inner[rows, 0:LANES]
            turned_x = turned_x + pxs[plane + 3 : plane + 4, :] * part
            plain = plain + at_x * part
            turned_z = turned_z + at_x * inner[rows, LANES : 2 * LANES]
        weight = scale * own[20 + tile : 21 + tile, :]
        charge = -2.0 / (16.0 * CUTOFF * CUTOFF) * own[12 + tile : 13 + tile, :]
        sides = (turned_x * y, plain * ys, turned_z * y)
        for channel in range(3):
            at = slice(4 * channel + tile, 4 * channel + tile + 1)
            pair = gb[0][at, :]
            for other in gb[1:]:
                pair = pair + other[at, :]
            total = charge * pair + weight * jnp.sum(sides[channel], axis=0, keepdims=True)
            force[at, :] = total
            moved[at, :] = own[at, :] + STEP_SIZE * (own[28 + tile : 29 + tile, :] * total)


def partners(axis):
    count = lax.axis_size(axis)
    even = [(i, i ^ 1) for i in range(count)]
    odd = [(i, (i + 1 if i % 2 else i - 1) % count) for i in range(count)]
    return even, odd


def both_sides(blocks, axis):
    even, odd = partners(axis)
    return lax.ppermute(blocks[0], axis, even), lax.ppermute(blocks[1], axis, odd)


def across(block, axes, flips):
    counts = [lax.axis_size(axis) for axis in axes]
    pairs = []
    for source in range(math.prod(counts)):
        target, rest, unit = 0, source, 1
        for count, flip in reversed(list(zip(counts, flips))):
            target += (rest % count ^ flip) * unit
            rest //= count
            unit *= count
        pairs.append((source, target))
    return lax.ppermute(block, tuple(axes), pairs)


def f32(*shape):
    return jax.ShapeDtypeStruct(shape, jnp.float32)


def on_device(positions, charges, atom_types, type_table, live_count, exp_map):
    sizes = [lax.axis_size(axis) for axis in AXES]
    places = [lax.axis_index(axis) for axis in AXES]
    info = []
    for size, place in zip(sizes, places):
        info += [-place * BRICK, (size - place) * BRICK]
    for size, place in zip(sizes, places):
        odd = place % 2
        info += [odd, jnp.where(odd == 0, place > 0, place < size - 1).astype(jnp.int32)]
    info = jnp.stack(info).astype(jnp.int32)
    assert sizes[0] in (2, 4) and all(size in (2, 4, 8) for size in sizes)
    scale = FIT_GAIN * float(BRICK**3 * sizes[0] * sizes[1] * sizes[2])

    atoms, order = call(
        arrange_kernel,
        (f32(32, LANES), f32(TILES, LANES)),
        1 << 22,
        scratch=[pltpu.VMEM((SLOTS, LANES), jnp.float32), pltpu.VMEM((24, LANES), jnp.float32)],
        smem=2,
        n_in=5,
    )(
        type_table,
        live_count.reshape(1),
        positions,
        charges,
        atom_types,
    )
    given = jnp.pad(exp_map, ((0, 0), (0, 0), (0, LANES - BRICK)))
    own = atoms
    for step in range(STEPS):
        fields, rows = (2, 24) if step == 0 else (1, 16)
        planes = 8 * PLANES * fields
        field, *mine = call(
            functools.partial(splat_kernel, fields, rows),
            (f32(planes, LANES),) + (f32(rows + 8 * EDGE + 8 * GIVEN_EDGE * (fields - 1), LANES),) * 2,
            1 << 26,
            scratch=[
                pltpu.VMEM((WIDE, LANES), jnp.float32),
                pltpu.VMEM((PLANES * WIDE, SLOTS), jnp.bfloat16),
                pltpu.VMEM((PLANES * WIDE, SLOTS), jnp.bfloat16),
                pltpu.VMEM((2 * WIDE, SLOTS), jnp.bfloat16),
            ],
            smem=1,
            n_in=1 + fields,
        )(*((info, own, given) if step == 0 else (info, own)))
        for number, axis in enumerate(AXES[:2]):
            count = 3**number
            field, *mine = call(
                functools.partial(merge_kernel, number, count, rows, fields),
                (f32(fields * PLANES, 8, LANES),) + (f32(3 * count * rows + 8 * HALF * fields, LANES),) * 2,
                1 << 20,
                smem=1,
                n_in=5,
            )(info, field.reshape(planes, LANES), mine[0], *both_sides(mine, axis))
        before = () if step == 0 else (tiles, exp_ext)
        planned = call(
            functools.partial(plan_kernel, rows, fields),
            (jax.ShapeDtypeStruct((BLOCKS, LANES), jnp.int32), f32(ROOM, 8, LANES))
            + (f32(PLANES, 8, LANES),) * fields
            + (f32(8, LANES),)
            + (() if step == 0 else (f32(BRICK, BRICK, BRICK),)),
            1 << 22,
            scratch=[pltpu.VMEM((TILES, LANES, LANES), jnp.float32)],
            smem=1,
            n_in=6 + len(before),
        )(info, own, field.reshape(planes, LANES), mine[0], *both_sides(mine, AXES[2]), *before)
        if step == 0:
            listed, tiles, evolved, exp_ext, sums = planned
        else:
            listed, tiles, evolved, sums, model = planned
        early = [across(sums, AXES[:1], [2])] if sizes[0] >= 4 else []
        radius = call(
            born_kernel,
            f32(TILES, LANES),
            1 << 33,
            scratch=[pltpu.VMEM((3, SLOTS, LANES), jnp.float32), pltpu.VMEM((SLOTS, LANES), jnp.float32)],
            smem=1,
            n_in=3,
        )(listed, tiles, own)
        sums = functools.reduce(jnp.add, early, sums)
        line = jnp.concatenate([radius, sums])
        flips = (
            [(("gy",), (4,)), (("gx", "gy"), (1, 4))] if sizes[1] >= 8 else [],
            [(("gy",), (2,)), (("gy",), (3,))] if sizes[1] >= 4 else [],
            [(("gz",), (2,)), (("gz",), (3,))] if sizes[2] >= 4 else [],
        )
        for number, axis in enumerate(AXES):
            count = 3**number
            span = count * TILES
            others = [across(sums, *flip) for flip in flips[number]]
            near = both_sides((line, line), axis)
            if number == 2:
                sums = functools.reduce(jnp.add, others, sums + near[0][span:])
                break
            line, sums = call(
                functools.partial(radius_merge_kernel, number, count),
                (f32(3 * span + 8, LANES), f32(8, LANES)),
                1 << 20,
                smem=1,
                n_in=4 + len(others),
            )(info, line, *near, *others)
        pair = call(
            gb_kernel,
            f32(3 * TILES, LANES),
            1 << 34,
            scratch=[
                pltpu.VMEM((5, SLOTS, LANES), jnp.float32),
                pltpu.VMEM((3, SLOTS, LANES), jnp.float32),
                pltpu.VMEM((ROOM, 2, LANES), jnp.float32),
            ],
            smem=2,
            n_in=8,
        )(info, listed, tiles, own, radius, line, *near)
        if sizes[2] >= 8:
            sums = sums + across(sums, AXES[2:], [7])
        own, force = call(
            functools.partial(fit_kernel, scale, 1),
            (f32(32, LANES), f32(3 * TILES, LANES)),
            1 << 26,
            scratch=[
                pltpu.VMEM((PLANES * WIDE, LANES), jnp.bfloat16),
                pltpu.VMEM((LANES, 2 * LANES), jnp.bfloat16),
                pltpu.VMEM((PLANES * WIDE, 2 * LANES), jnp.float32),
                pltpu.VMEM((WIDE, LANES), jnp.float32),
                pltpu.VMEM((WIDE, LANES), jnp.float32),
            ],
            smem=1,
            n_in=6,
        )(info, own, evolved, exp_ext, sums, pair)
    displaced, final = call(
        restore_kernel,
        (f32(*positions.shape),) * 2,
        1 << 20,
        scratch=[pltpu.VMEM((24, LANES), jnp.float32)],
        n_in=4,
    )(order, own, atoms, force)
    return displaced, final, model


def solution(mesh):
    placed = (
        P(None, *AXES, None),
        P(*AXES, None),
        P(*AXES, None),
        P(),
        P(*AXES),
        P(*AXES),
    )
    return jax.shard_map(
        on_device,
        mesh=mesh,
        in_specs=placed,
        out_specs=(placed[0], placed[0], P(*AXES)),
        check_vma=False,
    )
```

```python
import functools
import math

import jax
import jax.numpy as jnp
from jax import lax
from jax.experimental import pallas as pl
from jax.experimental.pallas import tpu as pltpu
from jax.sharding import PartitionSpec as P

SPLAT_MARGIN = 3
BLUR_REACH = 2
STEPS = 2
CUTOFF = 10.0
EPSILON = 1e-06
STEP_SIZE = 1.0
FIT_GAIN = 0.2

AXES = ("gx", "gy", "gz")
SLOTS = 512
LANES = 128
TILES = SLOTS // LANES
BRICK = 16
PLANES = 26
HALF = PLANES // 2
EDGE = 10
GIVEN_EDGE = 5
PAD = 8
WIDE = 32
INTERPRET = False


def call(kernel, out_shape, cost, scratch=(), smem=0, n_in=0, vmem=48):
    specs = [pl.BlockSpec(memory_space=pltpu.SMEM)] * smem
    specs += [pl.BlockSpec(memory_space=pltpu.VMEM)] * (n_in - smem)
    many = isinstance(out_shape, (tuple, list))
    out_spec = pl.BlockSpec(memory_space=pltpu.VMEM)
    return pl.pallas_call(
        kernel,
        out_shape=out_shape,
        in_specs=specs,
        out_specs=[out_spec] * len(out_shape) if many else out_spec,
        scratch_shapes=list(scratch),
        cost_estimate=pl.CostEstimate(flops=cost, bytes_accessed=1 << 18, transcendentals=0),
        compiler_params=pltpu.CompilerParams(vmem_limit_bytes=vmem << 20),
        interpret=INTERPRET,
    )


def spread(row):
    return jnp.transpose(jnp.broadcast_to(row, (LANES, LANES)))


def gather_rows(acc):
    return jnp.sum(jnp.transpose(acc), axis=0, keepdims=True)


BLOCK = 32
BLOCKS = SLOTS // BLOCK
MANY = 16
FEW = 4
CELLS = 27
EMPTY = CELLS * TILES
ROOM = EMPTY + 4
FAR = 1e9


def three_parts(values):
    high = values.astype(jnp.bfloat16)
    rest = values - high.astype(jnp.float32)
    middle = rest.astype(jnp.bfloat16)
    return high, middle, (rest - middle.astype(jnp.float32)).astype(jnp.bfloat16)


def tiled(block, *index):
    row = block[(*index, 0, 0)] if index else block[0, 0]
    return jnp.concatenate([row[:, tile * LANES : (tile + 1) * LANES] for tile in range(TILES)], axis=0)


def arrange_kernel(table, live_count, given, charges, types, out, order, col, left):
    count = live_count[0]
    pos = jnp.concatenate([tiled(given, dim) for dim in range(3)], axis=0)
    slot = lax.broadcasted_iota(jnp.int32, (TILES, LANES), 0) * LANES
    slot = slot + lax.broadcasted_iota(jnp.int32, (TILES, LANES), 1)
    living = slot < count
    alive = jnp.where(living, 1.0, 0.0)
    kinds = tiled(types)
    props = []
    for row in range(3):
        value = jnp.zeros((TILES, LANES), jnp.float32)
        for kind in range(table.shape[1]):
            value = jnp.where(kinds == kind, table[row, kind], value)
        props.append(value)
    group = jnp.zeros((TILES, LANES), jnp.float32)
    sub = lax.broadcasted_iota(jnp.int32, (SLOTS, LANES), 0)
    lane = lax.broadcasted_iota(jnp.int32, (SLOTS, LANES), 1)
    for dim, size in ((0, 256), (1, 128), (2, 64), (0, 32)):
        key = group * 64.0 + jnp.where(living, pos[4 * dim : 4 * dim + 4, :], 40.0)
        for tile in range(TILES):
            col[tile * LANES : (tile + 1) * LANES, :] = spread(key[tile : tile + 1, :])
        ranks = []
        for tile in range(TILES):
            row = key[tile : tile + 1, :]
            other = col[...]
            ahead = (other < row) | ((other == row) & (sub < lane + tile * LANES))
            ranks.append(jnp.sum(jnp.where(ahead, 1.0, 0.0), axis=0, keepdims=True))
        rank = jnp.concatenate(ranks, axis=0)
        group = jnp.floor(rank * (1.0 / size))
    order[...] = rank
    values = [pos[0:4, :], pos[4:8, :], pos[8:12, :], tiled(charges) * alive]
    values += [props[1] * alive, props[2] * alive, props[0], alive]
    total = jnp.zeros((3 * len(values), SLOTS), jnp.float32)
    for tile in range(TILES):
        block = jnp.concatenate([value[tile : tile + 1, :] for value in values], axis=0)
        for part, piece in enumerate(three_parts(block)):
            left[8 * part : 8 * part + 8, :] = piece.astype(jnp.float32)
        hot = jnp.where(rank[tile : tile + 1, :] == sub.astype(jnp.float32), 1.0, 0.0).astype(jnp.bfloat16)
        dims = (((1,), (1,)), ((), ()))
        total = total + lax.dot_general(left[...].astype(jnp.bfloat16), hot, dims, preferred_element_type=jnp.float32)
    total = total[0:8] + total[8:16] + total[16:24]
    for channel in range(8):
        for tile in range(TILES):
            at = slice(4 * channel + tile, 4 * channel + tile + 1)
            out[at, :] = total[channel : channel + 1, tile * LANES : (tile + 1) * LANES]


def restore_kernel(order, moved, start, force, displaced, final, left):
    values = [moved[4 * d : 4 * d + 4, :] - start[4 * d : 4 * d + 4, :] for d in range(3)]
    values += [force[4 * d : 4 * d + 4, :] for d in range(3)]
    values += [jnp.zeros((TILES, LANES), jnp.float32)] * 2
    sub = lax.broadcasted_iota(jnp.int32, (LANES, LANES), 0).astype(jnp.float32)
    totals = [jnp.zeros((24, LANES), jnp.float32) for _ in range(TILES)]
    for source in range(TILES):
        block = jnp.concatenate([value[source : source + 1, :] for value in values], axis=0)
        for part, piece in enumerate(three_parts(block)):
            left[8 * part : 8 * part + 8, :] = piece.astype(jnp.float32)
        parts = left[...].astype(jnp.bfloat16)
        for tile in range(TILES):
            hot = jnp.where(order[tile : tile + 1, :] == sub + float(source * LANES), 1.0, 0.0)
            totals[tile] = totals[tile] + jnp.dot(parts, hot.astype(jnp.bfloat16), preferred_element_type=jnp.float32)
    for tile in range(TILES):
        total = totals[tile][0:8] + totals[tile][8:16] + totals[tile][16:24]
        for channel in range(6):
            out = displaced if channel < 3 else final
            out[channel % 3, 0, 0, :, tile * LANES : (tile + 1) * LANES] = total[channel : channel + 1, :]


def plan_kernel(rows, fields, *refs):
    info, own, field = refs[:3]
    sources = refs[3:6]
    if fields == 2:
        known = ()
        listed, tiles, evolved, given, sums, active = refs[6:]
    else:
        known = refs[6:7]
        given = refs[7]
        listed, tiles, evolved, sums, model, active = refs[8:]
    low, high = [], []
    for dim in range(3):
        living = own[28:32, :] > 0.0
        value = own[4 * dim : 4 * dim + 4, :]
        lo, hi = jnp.where(living, value, FAR), jnp.where(living, value, -FAR)
        for step in (1, 2, 4, 8, 16):
            lo = jnp.minimum(lo, pltpu.roll(lo, LANES - step, 1))
            hi = jnp.maximum(hi, pltpu.roll(hi, LANES - step, 1))
        low.append(lo)
        high.append(hi)
    active[...] = jnp.zeros_like(active)
    tiles[EMPTY:ROOM] = jnp.zeros((ROOM - EMPTY, 8, LANES), jnp.float32)
    after_first, valid = arrivals(info, 2)
    slots = (1, jnp.where(after_first, 2, 0), jnp.where(after_first, 0, 2))
    for source, slot, ok in zip(sources, slots, (None,) + valid):

        for cell in range(9):
            number = slot * 9 + cell
            sides = (cell % 3 - 1, cell // 3 - 1, slot - 1)
            block = source[cell * rows : cell * rows + rows, :]
            if ok is not None:
                block = block * ok
            if known:
                charge = [known[0][4 * number + tile, 4:5, :] for tile in range(TILES)]
                screen = [known[0][4 * number + tile, 3:4, :] for tile in range(TILES)]
                living = jnp.concatenate(screen, axis=0) > 0.0
            else:
                charge = [block[12 + tile : 13 + tile] for tile in range(TILES)]
                screen = [block[16 + tile : 17 + tile] for tile in range(TILES)]
                living = block[16:20] > 0.0
            near_low, near_high = [], []
            for dim in range(3):
                side = sides[dim]
                shift = float(side * BRICK) if isinstance(side, int) else side.astype(jnp.float32) * float(BRICK)
                moved = block[4 * dim : 4 * dim + 4] + shift
                near_low.append(jnp.min(jnp.where(living, moved, FAR), axis=1, keepdims=True))
                near_high.append(jnp.max(jnp.where(living, moved, -FAR), axis=1, keepdims=True))
                scaled = moved * (1.0 / CUTOFF)
                for tile in range(TILES):
                    tiles[4 * number + tile, dim : dim + 1, :] = scaled[tile : tile + 1, :]
            for tile in range(TILES):
                tiles[4 * number + tile, 3:4, :] = screen[tile]
                tiles[4 * number + tile, 4:5, :] = charge[tile]
            for tile in range(TILES):
                apart = jnp.zeros((TILES, LANES), jnp.float32)
                for dim in range(3):
                    lo, hi = low[dim][tile : tile + 1, :], high[dim][tile : tile + 1, :]
                    gap = jnp.maximum(jnp.maximum(near_low[dim] - hi, lo - near_high[dim]), 0.0)
                    apart = apart + gap * gap
                near = jnp.where(apart < CUTOFF * CUTOFF * 1.0001, 1.0, 0.0)
                active[tile, pl.ds(pl.multiple_of(4 * number, TILES), TILES), :] = near
    row = lax.broadcasted_iota(jnp.int32, (LANES, LANES), 0)
    lane = lax.broadcasted_iota(jnp.int32, (LANES, LANES), 1)
    before = jnp.where(lane < row, 1.0, 0.0).astype(jnp.bfloat16)
    for tile in range(TILES):
        flags = active[tile]
        ranks = jnp.dot(before, flags.astype(jnp.bfloat16), preferred_element_type=jnp.float32)
        for part in range(LANES // BLOCK):
            at = slice(part * BLOCK, part * BLOCK + 1)
            chosen = jnp.broadcast_to(flags[:, at], (LANES, LANES)) > 0.0
            place = jnp.broadcast_to(ranks[:, at], (LANES, LANES)).astype(jnp.int32)
            total = jnp.sum(jnp.where(chosen, 1, 0), axis=0, keepdims=True)
            entry = jnp.sum(jnp.where(chosen & (place == lane), row, 0), axis=0, keepdims=True)
            spot = lane[0:1, :]
            entry = jnp.where(spot < total, entry, EMPTY)
            block = tile * (LANES // BLOCK) + part
            listed[block : block + 1, :] = jnp.where(spot == LANES - 1, total, entry)
    lane = lax.broadcasted_iota(jnp.int32, (8, LANES), 1)
    sub = lane & (WIDE - 1)
    own_points = (lane >= WIDE) & (lane < 3 * WIDE) & (sub >= PAD) & (sub < PAD + BRICK)
    squares = jnp.zeros((8, LANES), jnp.float32)
    cross = squares
    target = squares
    adds = shift_masks(info, 2)
    evolved[...] = field[0 : 8 * PLANES, :].reshape(PLANES, 8, LANES)
    take_shares(2, adds, sources[1:], 9 * rows, evolved, 0)
    if fields == 2:
        given[...] = field[8 * PLANES : 16 * PLANES, :].reshape(PLANES, 8, LANES)
        take_shares(2, adds, sources[1:], 9 * rows + 8 * HALF, given, 0)
    for plane in range(PLANES):
        value = evolved[plane]
        if fields == 1 and 5 <= plane < 5 + BRICK:
            for block in (1, 2):
                moved = pltpu.roll(value, LANES - WIDE * block - PAD, 1)
                model[plane - 5, 8 * block - 8 : 8 * block, :] = moved[:, 0:BRICK]
        if 5 <= plane < 5 + BRICK:
            value = jnp.where(own_points, value, 0.0)
            wanted = jnp.where(own_points, given[plane], 0.0)
            squares = squares + value * value
            cross = cross + value * wanted
            target = target + wanted * wanted
    sums[...] = jnp.zeros_like(sums)
    sums[0:1, :] = jnp.sum(squares, axis=0, keepdims=True)
    sums[1:2, :] = jnp.sum(cross, axis=0, keepdims=True)
    sums[2:3, :] = jnp.sum(target, axis=0, keepdims=True)


def arrivals(info, axis):
    after_first = info[6 + 2 * axis] == 0
    return after_first, (1.0, jnp.where(info[7 + 2 * axis] > 0, 1.0, 0.0))


def upper_half(axis):
    lane = lax.broadcasted_iota(jnp.int32, (8, LANES), 1)
    return (lane >= 64) if axis == 1 else ((lane & (WIDE - 1)) >= BRICK)


def shift_masks(info, axis):
    upper = upper_half(axis)
    after_first, valid = arrivals(info, axis)
    after_one = jnp.where(after_first, 1.0, 0.0)
    masks = []
    for after, ok in zip((after_one, 1.0 - after_one), valid):
        masks.append((jnp.where(upper, after * ok, 0.0), jnp.where(upper, 0.0, (1.0 - after) * ok)))
    return masks


def half_steps(axis):
    return (64, 64) if axis == 1 else (BRICK, LANES - BRICK)


def take_shares(axis, masks, sources, base, into, first):
    up, down = half_steps(axis)
    for plane in range(HALF):
        at = slice(base + 8 * plane, base + 8 * plane + 8)
        low = into[first + plane]
        high = into[first + HALF + plane]
        for (from_after, from_before), source in zip(masks, sources):
            share = source[at, :]
            low = low + pltpu.roll(share, up, 1) * from_after + share * from_before
            high = high + share * from_after + pltpu.roll(share, down, 1) * from_before
        into[first + plane] = low
        into[first + HALF + plane] = high


def give_shares(info, axis, field, first, outs, base):
    up, down = half_steps(axis)
    upper = upper_half(axis)
    after_first, _ = arrivals(info, axis)
    for plane in range(HALF):
        low, high = field[first + plane], field[first + HALF + plane]
        after = jnp.where(upper, high, pltpu.roll(low, down, 1))
        before = jnp.where(upper, pltpu.roll(high, up, 1), low)
        at = slice(base + 8 * plane, base + 8 * plane + 8)
        outs[0][at, :] = jnp.where(after_first, after, before)
        outs[1][at, :] = jnp.where(after_first, before, after)


def merge_kernel(axis, count, rows, fields, info, field, mine, first, second, merged, out_first, out_second):
    after_first, valid = arrivals(info, axis)
    span = count * rows
    slots = (jnp.where(after_first, 2 * span, 0), jnp.where(after_first, 0, 2 * span))
    for out in (out_first, out_second):
        out[span : 2 * span, :] = mine[0:span, :]
        for source, slot, ok in zip((first, second), slots, valid):
            out[pl.ds(pl.multiple_of(slot, 8), span), :] = source[0:span, :] * ok
    merged[...] = field[...].reshape(fields * PLANES, 8, LANES)
    for number in range(fields):
        if axis == 0:
            for source, slot, ok in zip((first, second), slots, valid):
                width = GIVEN_EDGE if number else EDGE
                into = pl.ds(number * PLANES + jnp.where(slot > 0, PLANES - width, 0), width)
                at = slice(span + 8 * EDGE * number, span + 8 * EDGE * number + 8 * width)
                merged[into] = merged[into] + source[at, :].reshape(width, 8, LANES) * ok
        else:
            base = span + 8 * HALF * number
            take_shares(axis, shift_masks(info, axis), (first, second), base, merged, number * PLANES)
        base = 3 * span + 8 * HALF * number
        give_shares(info, axis + 1, merged, number * PLANES, (out_first, out_second), base)


def radius_merge_kernel(axis, count, info, mine, first, second, *refs):
    others, (out, sums) = refs[:-2], refs[-2:]
    after_first, _ = arrivals(info, axis)
    span = count * TILES
    out[span : 2 * span, :] = mine[0:span, :]
    slots = (jnp.where(after_first, 2 * span, 0), jnp.where(after_first, 0, 2 * span))
    for source, slot in zip((first, second), slots):
        out[pl.ds(pl.multiple_of(slot, 8), span), :] = source[0:span, :]
    total = mine[span : span + 8, :] + first[span : span + 8, :]
    for other in others:
        total = total + other[...]
    out[3 * span : 3 * span + 8, :] = total
    sums[...] = total


def over_tiles(count, some, carry):
    whole = count // MANY
    carry = lax.fori_loop(0, whole, lambda i, c: some(MANY, i * MANY, c), carry)
    rest = (count - whole * MANY + FEW - 1) // FEW
    return lax.fori_loop(0, rest, lambda i, c: some(FEW, whole * MANY + i * FEW, c), carry)


def born_kernel(listed, tiles, own, out, col, acc):
    for channel in range(3):
        for tile in range(TILES):
            row = own[4 * channel + tile : 4 * channel + tile + 1, :] * (1.0 / CUTOFF)
            col[channel, tile * LANES : (tile + 1) * LANES, :] = spread(row)

    def block(ib, carry):
        at = pl.ds(pl.multiple_of(ib * BLOCK, BLOCK), BLOCK)
        xi, yi, zi = col[0, at, :], col[1, at, :], col[2, at, :]

        def some(width, start, total):
            for k in range(width):
                tile = listed[ib, start + k]
                dx = xi - tiles[tile, 0:1, :]
                dy = yi - tiles[tile, 1:2, :]
                dz = zi - tiles[tile, 2:3, :]
                u = dx * dx + dy * dy + dz * dz
                s = jnp.maximum(1.0 - u, 0.0)
                e = jnp.exp2(u * (-CUTOFF * CUTOFF / 8.0 * math.log2(math.e)))
                total = total + (e * s) * (s * tiles[tile, 3:4, :])
            return total

        acc[at, :] = over_tiles(listed[ib, LANES - 1], some, jnp.zeros((BLOCK, LANES), jnp.float32))
        return carry

    lax.fori_loop(0, BLOCKS, block, 0)
    for tile in range(TILES):
        total = gather_rows(acc[tile * LANES : (tile + 1) * LANES, :]) - own[16 + tile : 17 + tile, :]
        out[tile : tile + 1, :] = own[24 + tile : 25 + tile, :] + total


def gb_kernel(info, listed, tiles, own, own_radius, mine, first, second, out, col, acc, rows):
    for tile in range(TILES):
        at = slice(tile * LANES, (tile + 1) * LANES)
        for channel in range(3):
            row = own[4 * channel + tile : 4 * channel + tile + 1, :] * (1.0 / CUTOFF)
            col[channel, at, :] = spread(row)
        radius = spread(own_radius[tile : tile + 1, :] * (1.0 / CUTOFF))
        col[3, at, :] = radius
        col[4, at, :] = (-0.5 * math.log2(math.e)) / radius
    rows[EMPTY:ROOM] = jnp.ones((ROOM - EMPTY, 2, LANES), jnp.float32)

    after_first, _ = arrivals(info, 2)
    slots = (1, jnp.where(after_first, 2, 0), jnp.where(after_first, 0, 2))
    for source, slot in zip((mine, first, second), slots):
        for cell in range(9):
            radius = source[TILES * cell : TILES * cell + TILES, :] * (1.0 / CUTOFF)
            half = 0.5 / radius
            for tile in range(TILES):
                rows[slot * 36 + 4 * cell + tile, 0:1, :] = radius[tile : tile + 1, :]
                rows[slot * 36 + 4 * cell + tile, 1:2, :] = half[tile : tile + 1, :]

    def block(ib, carry):
        at = pl.ds(pl.multiple_of(ib * BLOCK, BLOCK), BLOCK)
        xi, yi, zi = col[0, at, :], col[1, at, :], col[2, at, :]
        ri, ai = col[3, at, :], col[4, at, :]

        def some(width, start, force):
            fx, fy, fz = force
            for k in range(width):
                tile = listed[ib, start + k]
                dx = xi - tiles[tile, 0:1, :]
                dy = yi - tiles[tile, 1:2, :]
                dz = zi - tiles[tile, 2:3, :]
                u = dx * dx + dy * dy + dz * dz
                s = jnp.maximum(1.0 - u, 0.0)
                e = jnp.exp2(u * (ai * rows[tile, 1:2, :]))
                inv = lax.rsqrt(u + (ri * rows[tile, 0:1, :]) * e)
                t = s * inv
                m = (tiles[tile, 4:5, :] * t) * (16.0 + (t * inv) * (4.0 - e))
                fx = fx + m * dx
                fy = fy + m * dy
                fz = fz + m * dz
            return fx, fy, fz

        zero = jnp.zeros((BLOCK, LANES), jnp.float32)
        force = over_tiles(listed[ib, LANES - 1], some, (zero, zero, zero))
        for channel in range(3):
            acc[channel, at, :] = force[channel]
        return carry

    lax.fori_loop(0, BLOCKS, block, 0)
    for channel in range(3):
        for tile in range(TILES):
            total = gather_rows(acc[channel, tile * LANES : (tile + 1) * LANES, :])
            out[4 * channel + tile : 4 * channel + tile + 1, :] = total


def kernel_weights(reach):
    values = [math.exp(-0.5 * (index - reach) ** 2) for index in range(2 * reach + 1)]
    whole = sum(values)
    return [value / whole for value in values]


TAPS = kernel_weights(BLUR_REACH)


def blurred(values):
    rows = values.shape[0]
    near = pltpu.roll(values, 1, 0) + pltpu.roll(values, rows - 1, 0)
    far = pltpu.roll(values, 2, 0) + pltpu.roll(values, rows - 2, 0)
    return TAPS[2] * values + TAPS[1] * near + TAPS[0] * far


def profiles(row, side, base, rows, low, high, slope):
    number = lax.broadcasted_iota(jnp.int32, (rows, LANES), 0) + base
    shift = side * BRICK
    inside = (number >= low) & (number < high)
    window = inside & (number >= shift - SPLAT_MARGIN) & (number < shift + BRICK + SPLAT_MARGIN)
    moved = row + (float(shift) if isinstance(shift, int) else shift.astype(jnp.float32))
    gap = number.astype(jnp.float32) - moved
    plain = jnp.where(window, jnp.exp(-0.5 * gap * gap), 0.0)
    margin = SPLAT_MARGIN + BLUR_REACH
    reached = inside & (number >= shift - margin) & (number < shift + BRICK + margin)
    first = jnp.where(reached, blurred(plain), 0.0)
    if not slope:
        return first
    return first, jnp.where(reached, blurred(gap * plain), 0.0)


def split(values):
    high = values.astype(jnp.bfloat16)
    return high, (values - high.astype(jnp.float32)).astype(jnp.bfloat16)


def splat_kernel(fields, rows, bounds, own, *refs):
    if fields == 2:
        given = refs[0]
    field, out_first, out_second, px, left_hi, left_lo, right = refs[fields - 1 :]
    for tile in range(TILES):
        lanes = slice(tile * LANES, (tile + 1) * LANES)
        z = profiles(own[8 + tile : 9 + tile, :], 0, -PAD, WIDE, bounds[4], bounds[5], False)
        z_hi, z_lo = split(z)
        right[0:WIDE, lanes] = z_hi
        right[WIDE : 2 * WIDE, lanes] = z_lo
        x = profiles(own[tile : tile + 1, :], 0, -PAD, WIDE, bounds[0], bounds[1], False)
        px[...] = x * own[20 + tile : 21 + tile, :]
        y = profiles(own[4 + tile : 5 + tile, :], 0, -PAD, WIDE, bounds[2], bounds[3], False)
        for plane in range(PLANES):
            at = slice(plane * WIDE, (plane + 1) * WIDE)
            hi, lo = split(px[plane + 3 : plane + 4, :] * y)
            left_hi[at, lanes] = hi
            left_lo[at, lanes] = lo
    weights = right[...]
    dims = (((1,), (1,)), ((), ()))
    placed = lax.dot_general(left_hi[...], weights, dims, preferred_element_type=jnp.float32)
    placed = placed + lax.dot_general(left_lo[...], weights, dims, preferred_element_type=jnp.float32)
    placed = placed[:, 0:WIDE] + placed[:, WIDE : 2 * WIDE]
    placed = placed.reshape(PLANES, 4, 8, WIDE)
    for plane in range(PLANES):
        parts = [placed[plane, k] for k in range(4)]
        field[8 * plane : 8 * plane + 8, :] = jnp.concatenate(parts, axis=1)
    if fields == 2:
        base = 8 * PLANES
        field[base : base + 8 * PLANES, :] = jnp.zeros((8 * PLANES, LANES), jnp.float32)
        for plane in range(BRICK):
            value = pltpu.roll(given[plane, 0:8, :], WIDE + PAD, 1) + pltpu.roll(given[plane, 8:16, :], 2 * WIDE + PAD, 1)
            field[base + 8 * (plane + 5) : base + 8 * (plane + 6), :] = value
    after_first, _ = arrivals(bounds, 0)
    for out, after in ((out_first, after_first), (out_second, jnp.logical_not(after_first))):
        out[0:rows, :] = own[0:rows, :]
        off = pl.ds(pl.multiple_of(jnp.where(after, 8 * BRICK, 0), 8), 8 * EDGE)
        out[rows : rows + 8 * EDGE, :] = field[off, :]
        if fields == 2:
            start = 8 * PLANES + jnp.where(after, 8 * BRICK, 8 * GIVEN_EDGE)
            off = pl.ds(pl.multiple_of(start, 8), 8 * GIVEN_EDGE)
            out[rows + 8 * EDGE :, :] = field[off, :]


def fit_kernel(scale, parts, bounds, *refs):
    own, evolved, exp_ext, sums = refs[:4]
    gb = refs[4 : 4 + parts]
    moved, force, left, right, inner, px, pxs = refs[4 + parts :]
    squares = jnp.sum(sums[0:1, :], axis=1, keepdims=True)
    cross = jnp.sum(sums[1:2, :], axis=1, keepdims=True)
    target = jnp.sum(sums[2:3, :], axis=1, keepdims=True)
    norm = jnp.sqrt((squares + EPSILON) * (target + EPSILON))
    given_part = 1.0 / norm
    model_part = (cross / norm) / (squares + EPSILON)
    for plane in range(PLANES):
        s = exp_ext[plane] * given_part - evolved[plane] * model_part
        blocks = [s] + [pltpu.roll(s, LANES - WIDE * k, 1) for k in (1, 2, 3)]
        s = jnp.concatenate(blocks, axis=0)
        s = jnp.where(lax.broadcasted_iota(jnp.int32, (WIDE, LANES), 1) < WIDE, s, 0.0)
        hi = s.astype(jnp.bfloat16).astype(jnp.float32)
        lo = (s - hi).astype(jnp.bfloat16).astype(jnp.float32)
        packed = hi + pltpu.roll(lo, WIDE, 1) + pltpu.roll(hi, 2 * WIDE, 1)
        left[plane * WIDE : (plane + 1) * WIDE, :] = packed.astype(jnp.bfloat16)
    moved[3 * TILES :, :] = own[3 * TILES :, :]
    right[...] = jnp.zeros_like(right)
    for tile in range(TILES):
        z, zs = profiles(own[8 + tile : 9 + tile, :], 0, -PAD, WIDE, bounds[4], bounds[5], True)
        for part, values in enumerate((z, zs)):
            lanes = slice(part * LANES, (part + 1) * LANES)
            hi, lo = split(values)
            right[0:WIDE, lanes] = hi
            right[WIDE : 2 * WIDE, lanes] = hi
            right[2 * WIDE : 3 * WIDE, lanes] = lo
        inner[...] = jnp.dot(left[...], right[...], preferred_element_type=jnp.float32)
        x, xs = profiles(own[tile : tile + 1, :], 0, -PAD, WIDE, bounds[0], bounds[1], True)
        y, ys = profiles(own[4 + tile : 5 + tile, :], 0, -PAD, WIDE, bounds[2], bounds[3], True)
        px[...] = x
        pxs[...] = xs
        turned_x = jnp.zeros((WIDE, LANES), jnp.float32)
        plain = turned_x
        turned_z = turned_x
        for plane in range(PLANES):
            rows = slice(plane * WIDE, (plane + 1) * WIDE)
            at_x = px[plane + 3 : plane + 4, :]
            part = inner[rows, 0:LANES]
            turned_x = turned_x + pxs[plane + 3 : plane + 4, :] * part
            plain = plain + at_x * part
            turned_z = turned_z + at_x * inner[rows, LANES : 2 * LANES]
        weight = scale * own[20 + tile : 21 + tile, :]
        charge = -2.0 / (16.0 * CUTOFF * CUTOFF) * own[12 + tile : 13 + tile, :]
        sides = (turned_x * y, plain * ys, turned_z * y)
        for channel in range(3):
            at = slice(4 * channel + tile, 4 * channel + tile + 1)
            pair = gb[0][at, :]
            for other in gb[1:]:
                pair = pair + other[at, :]
            total = charge * pair + weight * jnp.sum(sides[channel], axis=0, keepdims=True)
            force[at, :] = total
            moved[at, :] = own[at, :] + STEP_SIZE * (own[28 + tile : 29 + tile, :] * total)


def partners(axis):
    count = lax.axis_size(axis)
    even = [(i, i ^ 1) for i in range(count)]
    odd = [(i, (i + 1 if i % 2 else i - 1) % count) for i in range(count)]
    return even, odd


def both_sides(blocks, axis):
    even, odd = partners(axis)
    return lax.ppermute(blocks[0], axis, even), lax.ppermute(blocks[1], axis, odd)


def across(block, axes, flips):
    counts = [lax.axis_size(axis) for axis in axes]
    pairs = []
    for source in range(math.prod(counts)):
        target, rest, unit = 0, source, 1
        for count, flip in reversed(list(zip(counts, flips))):
            target += (rest % count ^ flip) * unit
            rest //= count
            unit *= count
        pairs.append((source, target))
    return lax.ppermute(block, tuple(axes), pairs)


def f32(*shape):
    return jax.ShapeDtypeStruct(shape, jnp.float32)


def on_device(positions, charges, atom_types, type_table, live_count, exp_map):
    sizes = [lax.axis_size(axis) for axis in AXES]
    places = [lax.axis_index(axis) for axis in AXES]
    info = []
    for size, place in zip(sizes, places):
        info += [-place * BRICK, (size - place) * BRICK]
    for size, place in zip(sizes, places):
        odd = place % 2
        info += [odd, jnp.where(odd == 0, place > 0, place < size - 1).astype(jnp.int32)]
    info = jnp.stack(info).astype(jnp.int32)
    assert sizes[0] in (2, 4) and all(size in (2, 4, 8) for size in sizes)
    scale = FIT_GAIN * float(BRICK**3 * sizes[0] * sizes[1] * sizes[2])

    atoms, order = call(
        arrange_kernel,
        (f32(32, LANES), f32(TILES, LANES)),
        1 << 22,
        scratch=[pltpu.VMEM((SLOTS, LANES), jnp.float32), pltpu.VMEM((24, LANES), jnp.float32)],
        smem=2,
        n_in=5,
    )(
        type_table,
        live_count.reshape(1),
        positions,
        charges,
        atom_types,
    )
    given = jnp.pad(exp_map, ((0, 0), (0, 0), (0, LANES - BRICK)))
    own = atoms
    for step in range(STEPS):
        fields, rows = (2, 20) if step == 0 else (1, 12)
        planes = 8 * PLANES * fields
        field, *mine = call(
            functools.partial(splat_kernel, fields, rows),
            (f32(planes, LANES),) + (f32(rows + 8 * EDGE + 8 * GIVEN_EDGE * (fields - 1), LANES),) * 2,
            1 << 26,
            scratch=[
                pltpu.VMEM((WIDE, LANES), jnp.float32),
                pltpu.VMEM((PLANES * WIDE, SLOTS), jnp.bfloat16),
                pltpu.VMEM((PLANES * WIDE, SLOTS), jnp.bfloat16),
                pltpu.VMEM((2 * WIDE, SLOTS), jnp.bfloat16),
            ],
            smem=1,
            n_in=1 + fields,
        )(*((info, own, given) if step == 0 else (info, own)))
        for number, axis in enumerate(AXES[:2]):
            count = 3**number
            field, *mine = call(
                functools.partial(merge_kernel, number, count, rows, fields),
                (f32(fields * PLANES, 8, LANES),) + (f32(3 * count * rows + 8 * HALF * fields, LANES),) * 2,
                1 << 20,
                smem=1,
                n_in=5,
            )(info, field.reshape(planes, LANES), mine[0], *both_sides(mine, axis))
        before = () if step == 0 else (tiles, exp_ext)
        planned = call(
            functools.partial(plan_kernel, rows, fields),
            (jax.ShapeDtypeStruct((BLOCKS, LANES), jnp.int32), f32(ROOM, 8, LANES))
            + (f32(PLANES, 8, LANES),) * fields
            + (f32(8, LANES),)
            + (() if step == 0 else (f32(BRICK, BRICK, BRICK),)),
            1 << 22,
            scratch=[pltpu.VMEM((TILES, LANES, LANES), jnp.float32)],
            smem=1,
            n_in=6 + len(before),
        )(info, own, field.reshape(planes, LANES), mine[0], *both_sides(mine, AXES[2]), *before)
        if step == 0:
            listed, tiles, evolved, exp_ext, sums = planned
        else:
            listed, tiles, evolved, sums, model = planned
        early = [across(sums, AXES[:1], [2])] if sizes[0] >= 4 else []
        radius = call(
            born_kernel,
            f32(TILES, LANES),
            1 << 33,
            scratch=[pltpu.VMEM((3, SLOTS, LANES), jnp.float32), pltpu.VMEM((SLOTS, LANES), jnp.float32)],
            smem=1,
            n_in=3,
        )(listed, tiles, own)
        sums = functools.reduce(jnp.add, early, sums)
        line = jnp.concatenate([radius, sums])
        flips = (
            [(("gy",), (4,)), (("gx", "gy"), (1, 4))] if sizes[1] >= 8 else [],
            [(("gy",), (2,)), (("gy",), (3,))] if sizes[1] >= 4 else [],
            [(("gz",), (2,)), (("gz",), (3,))] if sizes[2] >= 4 else [],
        )
        for number, axis in enumerate(AXES):
            count = 3**number
            span = count * TILES
            others = [across(sums, *flip) for flip in flips[number]]
            near = both_sides((line, line), axis)
            if number == 2:
                sums = functools.reduce(jnp.add, others, sums + near[0][span:])
                break
            line, sums = call(
                functools.partial(radius_merge_kernel, number, count),
                (f32(3 * span + 8, LANES), f32(8, LANES)),
                1 << 20,
                smem=1,
                n_in=4 + len(others),
            )(info, line, *near, *others)
        pair = call(
            gb_kernel,
            f32(3 * TILES, LANES),
            1 << 34,
            scratch=[
                pltpu.VMEM((5, SLOTS, LANES), jnp.float32),
                pltpu.VMEM((3, SLOTS, LANES), jnp.float32),
                pltpu.VMEM((ROOM, 2, LANES), jnp.float32),
            ],
            smem=2,
            n_in=8,
        )(info, listed, tiles, own, radius, line, *near)
        if sizes[2] >= 8:
            sums = sums + across(sums, AXES[2:], [7])
        own, force = call(
            functools.partial(fit_kernel, scale, 1),
            (f32(32, LANES), f32(3 * TILES, LANES)),
            1 << 26,
            scratch=[
                pltpu.VMEM((PLANES * WIDE, LANES), jnp.bfloat16),
                pltpu.VMEM((LANES, 2 * LANES), jnp.bfloat16),
                pltpu.VMEM((PLANES * WIDE, 2 * LANES), jnp.float32),
                pltpu.VMEM((WIDE, LANES), jnp.float32),
                pltpu.VMEM((WIDE, LANES), jnp.float32),
            ],
            smem=1,
            n_in=6,
        )(info, own, evolved, exp_ext, sums, pair)
    displaced, final = call(
        restore_kernel,
        (f32(*positions.shape),) * 2,
        1 << 20,
        scratch=[pltpu.VMEM((24, LANES), jnp.float32)],
        n_in=4,
    )(order, own, atoms, force)
    return displaced, final, model


def solution(mesh):
    placed = (
        P(None, *AXES, None),
        P(*AXES, None),
        P(*AXES, None),
        P(),
        P(*AXES),
        P(*AXES),
    )
    return jax.shard_map(
        on_device,
        mesh=mesh,
        in_specs=placed,
        out_specs=(placed[0], placed[0], P(*AXES)),
        check_vma=False,
    )
```
